32 devices in a mesh: dp: 8 (over z, y), tensor: 4 (over x, core).
Axes of the slice: x: 2, y: 2, z: 4, core: 2. Of those that a mesh axis runs over, the one named last changes fastest.
Arguments:
- inputs: bfloat16 [16, 1024, 768], P('dp', 'tensor'), may hold values from -6 to 6
- random_blocks: int32 [12, 16, 3], P('tensor'), may hold values from 0 to 15
- query_weight: bfloat16 [768, 768], P('dp', 'tensor'), may hold values from -0.21875 to 0.21875
- query_bias: bfloat16 [768], P(('tensor', 'dp')), may hold values from -3 to 3
- key_weight: bfloat16 [768, 768], P('dp', 'tensor'), may hold values from -0.21875 to 0.21875
- value_weight: bfloat16 [768, 768], P('dp', 'tensor'), may hold values from -0.21875 to 0.21875
- value_bias: bfloat16 [768], P(('tensor', 'dp')), may hold values from -0.59765625 to 0.59765625
- out_weight: bfloat16 [768, 768], P('tensor', 'dp'), may hold values from -0.875 to 0.875
- out_bias: bfloat16 [768], P('dp'), may hold values from -3 to 3
- first_gain: bfloat16 [768], P('dp'), may hold values from 0.5 to 1.5
- first_shift: bfloat16 [768], P('dp'), may hold values from -3 to 3
- up_weight: bfloat16 [768, 3072], P('dp', 'tensor'), may hold values from -0.21875 to 0.21875
- up_bias: bfloat16 [3072], P(('tensor', 'dp')), may hold values from -3 to 3
- down_weight: bfloat16 [3072, 768], P('tensor', 'dp'), may hold values from -0.109375 to 0.109375
- down_bias: bfloat16 [768], P('dp'), may hold values from -3 to 3
- second_gain: bfloat16 [768], P('dp'), may hold values from 0.5 to 1.5
- second_shift: bfloat16 [768], P('dp'), may hold values from -3 to 3
- cotangent: bfloat16 [16, 1024, 768], P('dp', 'tensor'), may hold values from -6 to 6
Outputs:
- output: bfloat16 [16, 1024, 768], P('dp', 'tensor')
- input_grad: float32 [16, 1024, 768], P('dp', 'tensor')
- query_weight_grad: float32 [768, 768], P('dp', 'tensor')
- query_bias_grad: float32 [768], P(('tensor', 'dp'))
- key_weight_grad: float32 [768, 768], P('dp', 'tensor')
- value_weight_grad: float32 [768, 768], P('dp', 'tensor')
- value_bias_grad: float32 [768], P(('tensor', 'dp'))
- out_weight_grad: float32 [768, 768], P('tensor', 'dp')
- out_bias_grad: float32 [768], P('dp')
- first_gain_grad: float32 [768], P('dp')
- first_shift_grad: float32 [768], P('dp')
- up_weight_grad: float32 [768, 3072], P('dp', 'tensor')
- up_bias_grad: float32 [3072], P(('tensor', 'dp'))
- down_weight_grad: float32 [3072, 768], P('tensor', 'dp')
- down_bias_grad: float32 [768], P('dp')
- second_gain_grad: float32 [768], P('dp')
- second_shift_grad: float32 [768], P('dp')
The draws below stay inside these ranges and needn't reach their ends.
Inputs may be any that keep to these rules, and one draw needn't show every extreme that they name: `random_blocks`: entry [h, i, r] names a key block of the same sequence that query block i attends to in head h; entries may repeat one another or fall on the window or the global blocks.
All inputs are finite; a program needn't handle non-finite values.
Results may differ from the reference program's by a relative error of at most 0.017.
Values may be sent and summed in bfloat16 or wider, within the bound.
A program may use at most 192 MiB of HBM per device.

```python
import jax
import jax.numpy as jnp
from jax import lax

D = 768
HEADS = 12
HEAD_DIM = 64
FF = 3072
BLOCK = 64
RAND = 3
LEN = 1024
NB = 16
SEQS = 16


def with_ends(entries, key, least, largest):
    longest = entries.shape.index(max(entries.shape))
    spots = []
    for shift in (0, 1):
        where = [jax.random.randint(jax.random.fold_in(key, axis), (), 0, length) for axis, length in enumerate(entries.shape)]
        where[longest] = (where[longest] + shift) % entries.shape[longest]
        spots.append(tuple(where))
    return entries.at[spots[0]].set(least).at[spots[1]].set(largest)


def with_spikes(array, key, source, target, blocks, factor):
    def block_of(position):
        return (jnp.arange(array.shape[position]) // (array.shape[position] // blocks)).reshape((-1,) + (1,) * (array.ndim - 1 - position))

    one_side = jax.random.permutation(key, blocks)[block_of(target)]
    other_side = (block_of(target) + blocks // 2) % blocks
    return jnp.where((block_of(source) == one_side) | (block_of(source) == other_side), factor * array, array)


def shard_levels(rng, extent, shards, smallest, high):
    level = 1.0
    for position, parts in shards:
        draws = jax.random.uniform(jax.random.fold_in(jax.random.fold_in(rng, 6), position), (parts,), jnp.float32, smallest / len(shards), high / len(shards))
        level = level * jnp.repeat(jnp.exp(draws), extent[position] // parts).reshape((-1,) + (1,) * (len(extent) - 1 - position))
    return level


def normal_values(stream_key, dims, width, limit, cuts=(), kind=jnp.bfloat16):
    entries = jax.random.normal(stream_key, dims, jnp.float32) * width
    if len(cuts) > 0:
        entries = shard_levels(stream_key, dims, cuts, -0.22, 0.18) * entries
    return jnp.clip(entries, min=-limit, max=limit).astype(kind)


def noise_with(key, shape, width, most, split, heavy, kind=jnp.bfloat16):
    entries = width * jax.random.normal(key, shape, jnp.float32)
    if split:
        entries = entries * shard_levels(key, shape, split, -0.22, 0.18)
    return jnp.clip(with_spikes(entries, jax.random.fold_in(key, 3), *heavy), -most, most).astype(kind)


def setup_inputs(seed: int = 0) -> dict:
    streams_of = jax.random.split(jax.random.key(seed), 19)
    inputs = normal_values(streams_of[0], (SEQS, LEN, D), 1.0, 6.0, ((0, 8), (1, 4)))
    random_blocks = with_ends(jax.random.randint(streams_of[1], (HEADS, NB, RAND), 0, NB), jax.random.fold_in(streams_of[1], 1), 0, NB - 1).astype(jnp.int32)
    query_weight = normal_values(streams_of[2], (D, D), D ** -0.5, 0.21875, ((0, 8), (1, 4)))
    query_bias = normal_values(streams_of[3], (D,), 0.5, 3.0, ((0, 32),))
    key_weight = normal_values(streams_of[4], (D, D), D ** -0.5, 0.21875, ((0, 8), (1, 4)))
    value_weight = normal_values(streams_of[5], (D, D), D ** -0.5, 0.21875, ((0, 8), (1, 4)))
    value_bias = normal_values(streams_of[6], (D,), 0.1, 0.59765625, ((0, 32),))
    out_weight = normal_values(streams_of[7], (D, D), (D // 16) ** -0.5, 0.875, ((0, 4), (1, 8)))
    out_bias = normal_values(streams_of[8], (D,), 0.5, 3.0, ((0, 8),))
    first_gain = jnp.clip(1.0 + 0.1 * jax.random.normal(streams_of[9], (D,), jnp.float32), 0.5, 1.5).astype(jnp.bfloat16)
    first_shift = normal_values(streams_of[10], (D,), 0.5, 3.0, ((0, 8),))
    up_weight = normal_values(streams_of[11], (D, FF), D ** -0.5, 0.21875, ((0, 8), (1, 4)))
    up_bias = normal_values(streams_of[12], (FF,), 0.5, 3.0, ((0, 32),))
    down_weight = normal_values(streams_of[13], (FF, D), FF ** -0.5, 0.109375, ((0, 4), (1, 8)))
    down_bias = normal_values(streams_of[14], (D,), 0.5, 3.0, ((0, 8),))
    second_gain = jnp.clip(1.0 + 0.1 * jax.random.normal(streams_of[15], (D,), jnp.float32), 0.5, 1.5).astype(jnp.bfloat16)
    second_shift = normal_values(streams_of[16], (D,), 0.5, 3.0, ((0, 8),))
    cotangent = noise_with(streams_of[17], (SEQS, LEN, D), 1.0, 6.0, ((0, 8), (1, 4)), (0, 1, 8, 2.0))
    return dict(inputs=inputs, random_blocks=random_blocks, query_weight=query_weight, query_bias=query_bias, key_weight=key_weight, value_weight=value_weight, value_bias=value_bias, out_weight=out_weight, out_bias=out_bias, first_gain=first_gain, first_shift=first_shift, up_weight=up_weight, up_bias=up_bias, down_weight=down_weight, down_bias=down_bias, second_gain=second_gain, second_shift=second_shift, cotangent=cotangent)


@jax.custom_vjp
def low(v):
    return lax.optimization_barrier(v.astype(jnp.bfloat16)).astype(jnp.float32)

@jax.custom_vjp
def low_back(v):
    return v

def low_keep(v):
    return (low(v), None)

def low_pass(kept, grad):
    return (grad,)

def back_keep(v):
    return (v, None)

def back_low(kept, grad):
    return (low(grad),)
low.defvjp(low_keep, low_pass)
low_back.defvjp(back_keep, back_low)
norm_eps = 1e-12
highest = lax.Precision.HIGHEST

def block_allowed(random_blocks, block_count):
    row_ids = jnp.arange(block_count, dtype=jnp.int32)[:, None]
    col_ids = jnp.arange(block_count, dtype=jnp.int32)[None, :]
    fixed = (jnp.abs(row_ids - col_ids) <= 1) | (col_ids == 0) | (col_ids == block_count - 1) | (row_ids == 0) | (row_ids == block_count - 1)
    picked = jnp.any(random_blocks[:, :, :, None] == jnp.arange(block_count, dtype=jnp.int32)[None, None, None, :], axis=2)
    return fixed[None, :, :] | picked

def layer_norm(values, gain, shift):
    mean = lax.optimization_barrier(jnp.mean(values, axis=-1, keepdims=True))
    spread = lax.optimization_barrier(jnp.mean(values * values, axis=-1, keepdims=True)) - mean * mean
    return (values - mean) * lax.rsqrt(spread + norm_eps) * gain + shift

def layer(params, tokens, allowed):
    query_weight, query_bias, key_weight, value_weight, value_bias, out_weight, out_bias, first_gain, first_shift, up_weight, up_bias, down_weight, down_bias, second_gain, second_shift = params
    length = tokens.shape[0]
    queries = low(low_back(jnp.dot(tokens, query_weight, precision=highest) + query_bias))
    keys_all = low(low_back(jnp.dot(tokens, key_weight, precision=highest)))
    values_all = low(low_back(jnp.dot(tokens, value_weight, precision=highest) + value_bias))
    query_heads = queries.reshape(length, HEADS, HEAD_DIM)
    key_heads = keys_all.reshape(length, HEADS, HEAD_DIM)
    value_heads = values_all.reshape(length, HEADS, HEAD_DIM)
    products = low_back(jnp.einsum('qhd,khd->hqk', query_heads, key_heads, precision=highest))
    blocks = length // BLOCK
    scaled = (products * HEAD_DIM ** (-0.5)).reshape(HEADS, blocks, BLOCK, blocks, BLOCK)
    masked = jnp.where(allowed[:, :, None, :, None], scaled, -1000000000.0).reshape(HEADS, length, length)
    probs = low(jax.nn.softmax(masked, axis=-1))
    mixed = jnp.einsum('hqk,khd->qhd', probs, value_heads, precision=highest).reshape(length, D)
    mixed = low(low_back(mixed))
    branch = low_back(jnp.dot(mixed, out_weight, precision=highest))
    hidden = tokens + branch + out_bias
    first_norm = layer_norm(hidden, first_gain, first_shift)
    inner = low_back(jnp.dot(low(first_norm), up_weight, precision=highest) + up_bias)
    active = low(jax.nn.gelu(inner, approximate=False))
    feed = low_back(jnp.dot(active, down_weight, precision=highest))
    return layer_norm(first_norm + feed + down_bias, second_gain, second_shift)

def reference(inputs, random_blocks, query_weight, query_bias, key_weight, value_weight, value_bias, out_weight, out_bias, first_gain, first_shift, up_weight, up_bias, down_weight, down_bias, second_gain, second_shift, cotangent):
    allowed = block_allowed(random_blocks, LEN // BLOCK)
    params = tuple((weight.astype(jnp.float32) for weight in (query_weight, query_bias, key_weight, value_weight, value_bias, out_weight, out_bias, first_gain, first_shift, up_weight, up_bias, down_weight, down_bias, second_gain, second_shift)))
    tokens_all = inputs.astype(jnp.float32)
    upstream_all = cotangent.astype(jnp.float32)

    def one_sequence(totals, items):
        tokens, upstream = items
        result, pull = jax.vjp(lambda weights, rows: layer(weights, rows, allowed), params, tokens)
        weight_grads, token_grads = pull(upstream)
        return (jax.tree.map(jnp.add, totals, weight_grads), (result.astype(jnp.bfloat16), token_grads))
    start = jax.tree.map(jnp.zeros_like, params)
    totals, (results, token_grads) = lax.scan(one_sequence, start, (tokens_all, upstream_all))
    return (results, token_grads, totals[0], totals[1], totals[2], totals[3], totals[4], totals[5], totals[6], totals[7], totals[8], totals[9], totals[10], totals[11], totals[12], totals[13], totals[14])
```

```python
from functools import partial

import jax
import jax.numpy as jnp
from jax import lax
from jax.experimental import pallas as pl
from jax.experimental.pallas import tpu as pltpu
from jax.sharding import PartitionSpec as P

HEAD_DIM = 64
BLOCK = 64


norm_eps = 1e-12


def gather_weights(shards):
    return (
        lax.all_gather(shards[0], "dp", axis=0, tiled=True),
        lax.all_gather(shards[1], "dp", axis=0, tiled=True),
        lax.all_gather(shards[2], "dp", axis=0, tiled=True),
        lax.all_gather(shards[3], "dp", axis=0, tiled=True),
        lax.all_gather(shards[4], "dp", axis=0, tiled=True),
        lax.all_gather(shards[5], "dp", axis=1, tiled=True),
        lax.all_gather(shards[6], "dp", axis=0, tiled=True),
        lax.all_gather(shards[7], "dp", axis=0, tiled=True),
        lax.all_gather(shards[8], "dp", axis=0, tiled=True),
        lax.all_gather(shards[9], "dp", axis=0, tiled=True),
        lax.all_gather(shards[10], "dp", axis=0, tiled=True),
        lax.all_gather(shards[11], "dp", axis=1, tiled=True),
        lax.all_gather(shards[12], "dp", axis=0, tiled=True),
        lax.all_gather(shards[13], "dp", axis=0, tiled=True),
        lax.all_gather(shards[14], "dp", axis=0, tiled=True),
    )


def reduce_grads(grads):
    return (
        lax.psum_scatter(grads[0], "dp", scatter_dimension=0, tiled=True),
        lax.psum_scatter(grads[1], "dp", scatter_dimension=0, tiled=True),
        lax.psum_scatter(grads[2], "dp", scatter_dimension=0, tiled=True),
        lax.psum_scatter(grads[3], "dp", scatter_dimension=0, tiled=True),
        lax.psum_scatter(grads[4], "dp", scatter_dimension=0, tiled=True),
        lax.psum_scatter(grads[5], "dp", scatter_dimension=1, tiled=True),
        lax.psum_scatter(grads[6], "dp", scatter_dimension=0, tiled=True),
        lax.psum_scatter(grads[7], "dp", scatter_dimension=0, tiled=True),
        lax.psum_scatter(grads[8], "dp", scatter_dimension=0, tiled=True),
        lax.psum_scatter(grads[9], "dp", scatter_dimension=0, tiled=True),
        lax.psum_scatter(grads[10], "dp", scatter_dimension=0, tiled=True),
        lax.psum_scatter(grads[11], "dp", scatter_dimension=1, tiled=True),
        lax.psum_scatter(grads[12], "dp", scatter_dimension=0, tiled=True),
        lax.psum_scatter(grads[13], "dp", scatter_dimension=0, tiled=True),
        lax.psum_scatter(grads[14], "dp", scatter_dimension=0, tiled=True),
    )


def full_rows(block):
    return lax.all_gather(block, "tensor", axis=0, tiled=True)


def column_sums(partial_terms):
    return lax.psum_scatter(
        partial_terms.astype(jnp.bfloat16), "tensor", scatter_dimension=0, tiled=True
    ).astype(jnp.float32)


def block_allowed(random_blocks, block_count):
    row_ids = jnp.arange(block_count, dtype=jnp.int32)[:, None]
    col_ids = jnp.arange(block_count, dtype=jnp.int32)[None, :]
    fixed = (
        (jnp.abs(row_ids - col_ids) <= 1)
        | (col_ids == 0)
        | (col_ids == block_count - 1)
        | (row_ids == 0)
        | (row_ids == block_count - 1)
    )
    picked = jnp.any(
        random_blocks[:, :, :, None]
        == jnp.arange(block_count, dtype=jnp.int32)[None, None, None, :],
        axis=2,
    )
    return fixed[None, :, :] | picked


def layer_norm(values, gain, shift):
    mean = jnp.mean(values, axis=1, keepdims=True)
    spread = jnp.mean(values * values, axis=1, keepdims=True) - mean * mean
    factor = lax.rsqrt(spread + norm_eps)
    normed = (values - mean) * factor
    return (normed * gain + shift, normed, factor)


def norm_back(upstream, normed, factor, gain):
    scaled = upstream * gain
    plain = jnp.mean(scaled, axis=1, keepdims=True)
    along = jnp.mean(scaled * normed, axis=1, keepdims=True)
    back = factor * (scaled - plain - normed * along)
    return (back, jnp.sum(upstream * normed, axis=0), jnp.sum(upstream, axis=0))


def row_parts(array, span):
    return array.reshape((array.shape[0] // span, span) + array.shape[1:])


def mask_parts(allowed, span):
    return allowed.reshape(allowed.shape[0], -1, span // BLOCK, allowed.shape[2]).transpose(
        1, 0, 2, 3
    )


def block_scores(query_block, key_heads, mask_block):
    products = jnp.einsum(
        "qhd,khd->hqk", query_block, key_heads, preferred_element_type=jnp.float32
    )
    head_count, row_count, key_count = products.shape
    scaled = (products * HEAD_DIM ** (-0.5)).reshape(
        head_count, row_count // BLOCK, BLOCK, key_count // BLOCK, BLOCK
    )
    masked = jnp.where(mask_block[:, :, None, :, None], scaled, -1000000000.0)
    return masked.reshape(head_count, row_count, key_count)


def attend(query_heads, key_heads, value_heads, allowed):
    length = query_heads.shape[0]
    span = min(512, length)

    def one_part(items):
        query_block, mask_block = items
        scores = block_scores(query_block, key_heads, mask_block)
        largest = jnp.max(scores, axis=-1, keepdims=True)
        log_total = largest + jnp.log(jnp.sum(jnp.exp(scores - largest), axis=-1, keepdims=True))
        weights_low = jnp.exp(scores - log_total).astype(jnp.bfloat16)
        mixed = jnp.einsum(
            "hqk,khd->qhd", weights_low, value_heads, preferred_element_type=jnp.float32
        )
        return (mixed, log_total[..., 0])

    mixed, log_totals = lax.map(one_part, (row_parts(query_heads, span), mask_parts(allowed, span)))
    return (mixed.reshape(length, -1).astype(jnp.bfloat16), log_totals)


def attend_back(query_heads, key_heads, value_heads, mixed_back, log_totals, allowed):
    length = query_heads.shape[0]
    span = min(512, length)

    def one_part(carry, items):
        key_sum, value_sum = carry
        query_block, back_block, log_total, mask_block = items
        scores = block_scores(query_block, key_heads, mask_block)
        weights = jnp.exp(scores - log_total[..., None])
        weights_low = weights.astype(jnp.bfloat16)
        weights_back = jnp.einsum(
            "qhd,khd->hqk", back_block, value_heads, preferred_element_type=jnp.float32
        )
        centre = jnp.sum(weights_back * weights, axis=-1, keepdims=True)
        scores_back = (weights * (weights_back - centre) * HEAD_DIM ** (-0.5)).astype(jnp.bfloat16)
        query_back = jnp.einsum(
            "hqk,khd->qhd", scores_back, key_heads, preferred_element_type=jnp.float32
        )
        key_sum = key_sum + jnp.einsum(
            "hqk,qhd->khd", scores_back, query_block, preferred_element_type=jnp.float32
        )
        value_sum = value_sum + jnp.einsum(
            "hqk,qhd->khd", weights_low, back_block, preferred_element_type=jnp.float32
        )
        return ((key_sum, value_sum), query_back)

    empty = jnp.zeros(key_heads.shape, jnp.float32)
    (key_back, value_back), query_back = lax.scan(
        one_part,
        (empty, empty),
        (
            row_parts(query_heads, span),
            row_parts(mixed_back, span),
            log_totals,
            mask_parts(allowed, span),
        ),
    )
    return (
        query_back.reshape(length, -1).astype(jnp.bfloat16),
        key_back.reshape(length, -1).astype(jnp.bfloat16),
        value_back.reshape(length, -1).astype(jnp.bfloat16),
    )


def forward_pass(weights, token_block, allowed):
    (
        query_weight,
        query_bias,
        key_weight,
        value_weight,
        value_bias,
        out_weight,
        out_bias,
        first_gain,
        first_shift,
        up_weight,
        up_bias,
        down_weight,
        down_bias,
        second_gain,
        second_shift,
    ) = weights
    token_rows = full_rows(token_block)
    length = token_rows.shape[0]

    def heads_of(product):
        return product.astype(jnp.bfloat16).reshape(length, -1, HEAD_DIM)

    query_heads = heads_of(
        jnp.dot(token_rows, query_weight, preferred_element_type=jnp.float32) + query_bias
    )
    key_heads = heads_of(jnp.dot(token_rows, key_weight, preferred_element_type=jnp.float32))
    value_heads = heads_of(
        jnp.dot(token_rows, value_weight, preferred_element_type=jnp.float32) + value_bias
    )
    mixed, log_totals = attend(query_heads, key_heads, value_heads, allowed)
    branch_terms = jnp.dot(mixed, out_weight, preferred_element_type=jnp.float32)
    hidden = token_block.astype(jnp.float32) + column_sums(branch_terms) + out_bias
    first_norm, first_normed, first_factor = layer_norm(hidden, first_gain, first_shift)
    first_rows = full_rows(first_norm.astype(jnp.bfloat16))
    inner = jnp.dot(first_rows, up_weight, preferred_element_type=jnp.float32) + up_bias
    active = jax.nn.gelu(inner, approximate=False).astype(jnp.bfloat16)
    second_in = (
        first_norm
        + column_sums(jnp.dot(active, down_weight, preferred_element_type=jnp.float32))
        + down_bias
    )
    result, second_normed, second_factor = layer_norm(second_in, second_gain, second_shift)
    kept = (
        token_rows,
        query_heads,
        key_heads,
        value_heads,
        log_totals,
        mixed,
        first_normed,
        first_factor,
        first_rows,
        inner,
        active,
        second_normed,
        second_factor,
    )
    return (result, kept)


def backward_pass(weights, kept, upstream_block, allowed):
    (
        query_weight,
        query_bias,
        key_weight,
        value_weight,
        value_bias,
        out_weight,
        out_bias,
        first_gain,
        first_shift,
        up_weight,
        up_bias,
        down_weight,
        down_bias,
        second_gain,
        second_shift,
    ) = weights
    (
        token_rows,
        query_heads,
        key_heads,
        value_heads,
        log_totals,
        mixed,
        first_normed,
        first_factor,
        first_rows,
        inner,
        active,
        second_normed,
        second_factor,
    ) = kept
    length = token_rows.shape[0]
    upstream = upstream_block.astype(jnp.float32)
    second_back, second_gain_grad, second_shift_grad = norm_back(
        upstream, second_normed, second_factor, second_gain
    )
    down_bias_grad = jnp.sum(second_back, axis=0)
    feed_rows = full_rows(second_back.astype(jnp.bfloat16))
    down_weight_grad = jnp.einsum(
        "tf,td->fd", active, feed_rows, preferred_element_type=jnp.float32
    )
    active_back = jnp.einsum(
        "td,fd->tf", feed_rows, down_weight, preferred_element_type=jnp.float32
    )
    inner_back = jax.vjp(partial(jax.nn.gelu, approximate=False), inner)[1](active_back)[0].astype(
        jnp.bfloat16
    )
    up_bias_grad = jnp.sum(inner_back, axis=0, dtype=jnp.float32)
    up_weight_grad = jnp.einsum(
        "td,tf->df", first_rows, inner_back, preferred_element_type=jnp.float32
    )
    first_back = second_back + column_sums(
        jnp.einsum("tf,df->td", inner_back, up_weight, preferred_element_type=jnp.float32)
    )
    hidden_back, first_gain_grad, first_shift_grad = norm_back(
        first_back, first_normed, first_factor, first_gain
    )
    out_bias_grad = jnp.sum(hidden_back, axis=0)
    branch_rows = full_rows(hidden_back.astype(jnp.bfloat16))
    out_weight_grad = jnp.einsum(
        "tc,td->cd", mixed, branch_rows, preferred_element_type=jnp.float32
    )
    mixed_back = jnp.einsum(
        "td,cd->tc", branch_rows, out_weight, preferred_element_type=jnp.float32
    ).astype(jnp.bfloat16)
    query_back, key_back, value_back = attend_back(
        query_heads,
        key_heads,
        value_heads,
        mixed_back.reshape(length, -1, HEAD_DIM),
        log_totals,
        allowed,
    )
    query_weight_grad = jnp.einsum(
        "td,tc->dc", token_rows, query_back, preferred_element_type=jnp.float32
    )
    key_weight_grad = jnp.einsum(
        "td,tc->dc", token_rows, key_back, preferred_element_type=jnp.float32
    )
    value_weight_grad = jnp.einsum(
        "td,tc->dc", token_rows, value_back, preferred_element_type=jnp.float32
    )
    query_bias_grad = jnp.sum(query_back, axis=0, dtype=jnp.float32)
    value_bias_grad = jnp.sum(value_back, axis=0, dtype=jnp.float32)
    projected = (
        jnp.einsum("tc,dc->td", query_back, query_weight, preferred_element_type=jnp.float32)
        + jnp.einsum("tc,dc->td", key_back, key_weight, preferred_element_type=jnp.float32)
        + jnp.einsum("tc,dc->td", value_back, value_weight, preferred_element_type=jnp.float32)
    )
    input_back = hidden_back + column_sums(projected)
    grads = (
        query_weight_grad,
        query_bias_grad,
        key_weight_grad,
        value_weight_grad,
        value_bias_grad,
        out_weight_grad,
        out_bias_grad,
        first_gain_grad,
        first_shift_grad,
        up_weight_grad,
        up_bias_grad,
        down_weight_grad,
        down_bias_grad,
        second_gain_grad,
        second_shift_grad,
    )
    return (input_back, grads)


def local(
    inputs,
    random_blocks,
    query_weight,
    query_bias,
    key_weight,
    value_weight,
    value_bias,
    out_weight,
    out_bias,
    first_gain,
    first_shift,
    up_weight,
    up_bias,
    down_weight,
    down_bias,
    second_gain,
    second_shift,
    cotangent,
):
    shards = (
        query_weight,
        query_bias,
        key_weight,
        value_weight,
        value_bias,
        out_weight,
        out_bias,
        first_gain,
        first_shift,
        up_weight,
        up_bias,
        down_weight,
        down_bias,
        second_gain,
        second_shift,
    )
    allowed = block_allowed(random_blocks, random_blocks.shape[1])
    resident = gather_weights(shards)
    growth = lax.axis_size("dp")
    grown_dims = (0, 0, 0, 0, 0, 1, 0, 0, 0, 0, 0, 1, 0, 0, 0)
    start = tuple(
        (
            jnp.zeros(
                tuple(
                    (
                        extent * growth if position == grown_dim else extent
                        for position, extent in enumerate(shard.shape)
                    )
                ),
                jnp.float32,
            )
            for shard, grown_dim in zip(shards, grown_dims)
        )
    )

    def one_sequence(totals, items):
        token_block, upstream_block = items
        result, kept = forward_pass(resident, token_block, allowed)
        input_back, grads = backward_pass(resident, kept, upstream_block, allowed)
        totals = tuple((summed + update for summed, update in zip(totals, grads)))
        return (totals, (result.astype(jnp.bfloat16), input_back))

    totals, (results, input_backs) = lax.scan(one_sequence, start, (inputs, cotangent))
    shares = reduce_grads(totals)
    vectors = lax.psum(
        (shares[6], shares[7], shares[8], shares[12], shares[13], shares[14]), "tensor"
    )
    return (
        results,
        input_backs,
        shares[0],
        shares[1],
        shares[2],
        shares[3],
        shares[4],
        shares[5],
        vectors[0],
        vectors[1],
        vectors[2],
        shares[9],
        shares[10],
        shares[11],
        vectors[3],
        vectors[4],
        vectors[5],
    )


MESH = pl.DeviceIdType.MESH
F32 = jnp.float32
BF16 = jnp.bfloat16
LOG2E = 1.4426950408889634
SCORE_SCALE = HEAD_DIM ** (-0.5)
TILE = 256
MESSAGES = 160


def dims(left, right, left_dim, right_dim):
    return lax.dot_general(
        left, right, (((left_dim,), (right_dim,)), ((), ())), preferred_element_type=F32
    )


def low_lanes(shape):
    return lax.broadcasted_iota(jnp.int32, shape, len(shape) - 1) < HEAD_DIM


def half_turn(block):
    return pltpu.roll(block.astype(F32), HEAD_DIM, 1).astype(block.dtype)


def pairs_of(first, second):
    tile = lambda pack, index: pack[:, 128 * index : 128 * index + 128]
    low = low_lanes((first.shape[0], 128))
    e0, e1, f0, f1 = tile(first, 3), tile(second, 3), tile(first, 4), tile(second, 4)
    query = (tile(first, 0), tile(second, 0), jnp.where(low, e0, half_turn(e1)))
    key = (tile(first, 1), tile(second, 1), jnp.where(low, half_turn(e0), e1))
    value = (tile(first, 2), tile(second, 2), jnp.where(low, f0, half_turn(f1)))
    out = (tile(first, 5), tile(second, 5), jnp.where(low, half_turn(f0), f1))
    return query, key, value, out


def packs_of(query, key, value, out):
    low = low_lanes(query[0].shape)
    first = (
        query[0],
        key[0],
        value[0],
        jnp.where(low, query[2], half_turn(key[2])),
        jnp.where(low, value[2], half_turn(out[2])),
        out[0],
    )
    second = (
        query[1],
        key[1],
        value[1],
        jnp.where(low, half_turn(query[2]), key[2]),
        jnp.where(low, half_turn(value[2]), out[2]),
        out[1],
    )
    return jnp.concatenate(first, 1), jnp.concatenate(second, 1)


def norm_of(values):
    mean = jnp.mean(values, axis=1, keepdims=True)
    spread = jnp.mean(values * values, axis=1, keepdims=True) - mean * mean
    factor = lax.rsqrt(spread + norm_eps)
    return (values - mean) * factor, factor


def norm_pull(upstream, normed, factor, gain):
    scaled = upstream * gain
    plain = jnp.mean(scaled, axis=1, keepdims=True)
    along = jnp.mean(scaled * normed, axis=1, keepdims=True)
    return factor * (scaled - plain - normed * along)


def row_sum(block):
    return jnp.sum(block, axis=0, keepdims=True)


def layer_kernel(
    pack_ref,
    vec_ref,
    mask_ref,
    in_ref,
    cot_ref,
    out_ref,
    grad_ref,
    gout_ref,
    vout_ref,
    full,
    vec_z,
    vec_y,
    vec_all,
    masks,
    tokens,
    cots,
    w_in,
    w_out,
    bias_q,
    bias_k,
    heads,
    mixed,
    lse,
    rows_stat,
    first_low,
    feed_low,
    branch_low,
    hat_first,
    fac_first,
    back_rows,
    active,
    slope,
    inner_buf,
    send_buf,
    recv_buf,
    mixed_back,
    key_sum,
    value_sum,
    heads_back,
    out_grad,
    diag_x,
    diag_y,
    near_x,
    near_y,
    near_z,
    total,
    swap_out,
    swap_in,
    vgrad,
    vsend,
    vrecv,
    send_sem,
    recv_sem,
):
    dp, tensor = lax.axis_index("dp"), lax.axis_index("tensor")
    z, y = dp // 2, dp % 2
    a, b = tensor // 2, tensor % 2
    core_dev = (dp, tensor + 1 - 2 * b)
    x_dev = (dp, tensor + 2 - 4 * a)
    y_dev = (dp + 1 - 2 * y, tensor)

    def z_at(shift):
        return (z + shift) % 4

    def z_dev(shift):
        return (z_at(shift) * 2 + y, tensor)

    barrier = pltpu.get_barrier_semaphore()
    for dev in (core_dev, x_dev, y_dev, z_dev(1), z_dev(2), z_dev(3)):
        pl.semaphore_signal(barrier, inc=1, device_id=dev, device_id_type=MESH)
    pl.semaphore_wait(barrier, 6)

    sent = []

    def copy(index, src, dst, dev):
        return pltpu.make_async_remote_copy(
            src_ref=src,
            dst_ref=dst,
            send_sem=send_sem.at[index],
            recv_sem=recv_sem.at[index],
            device_id=dev,
            device_id_type=MESH,
        )

    def send(index, src, dst, dev):
        copy(index, src, dst, dev).start()

    def arrived(index, region, dev=None):
        copy(index, region, region, core_dev).wait_recv()

    def left(index, region):
        copy(index, region, region, core_dev).wait_send()

    def piece(side, pack, chip, start=0, size=96):
        first = pl.multiple_of(chip * 96, 16) + start
        return full.at[side, pack, pl.ds(pl.multiple_of(first, 16), size), :]

    def gz(pack, j):
        return pack * 19 + j - 1

    def gx(pack, j):
        return pack * 19 + 3 + j

    def gy(pack, j):
        return pack * 19 + 7 + j

    def gdx(pack, j):
        return pack * 19 + 11 + j

    def gdy(pack, j):
        return pack * 19 + 15 + j

    def sdx(pack, i):
        return 57 + pack * 19 + i

    def sdy(pack, i):
        return 57 + pack * 19 + 4 + i

    def snx(pack, i):
        return 57 + pack * 19 + 8 + i

    def sny(pack, i):
        return 57 + pack * 19 + 12 + i

    def snz(pack, i):
        return 57 + pack * 19 + 15 + i

    M_IN, M_COT, M_MASK, M_VZ, M_VY, M_VX = 114, 115, 116, 117, 120, 121
    M_TOK, M_OUT, M_GRAD, M_VG = 122, 124, 125, 126
    M_ROWS, M_PART = 132, 138

    def gather_start(pack):
        own = pack_ref.at[pack]
        for j in (1, 3, 2):
            send(gz(pack, j), own, piece(a, pack, dp), z_dev(j))
        send(gx(pack, 0), own, piece(a, pack, dp), x_dev)
        send(gy(pack, 0), own, piece(a, pack, dp), y_dev)
        full[a, pack, pl.ds(pl.multiple_of(dp * 96, 16), 96), :] = pack_ref[pack]

    def gather_spread(pack, j):
        spot = piece(a, pack, z_at(-j) * 2 + y)
        arrived(gz(pack, j), spot)
        send(gx(pack, j), spot, spot, x_dev)
        send(gy(pack, j), spot, spot, y_dev)

    def gather_corner(pack, j):
        from_y = piece(a, pack, z_at(-j) * 2 + 1 - y)
        arrived(gy(pack, j), from_y)
        half = piece(a, pack, z_at(-j) * 2 + 1 - y, 0, 48)
        send(gdx(pack, j), half, half, x_dev)
        from_x = piece(1 - a, pack, z_at(-j) * 2 + y)
        arrived(gx(pack, j), from_x)
        half = piece(1 - a, pack, z_at(-j) * 2 + y, 48, 48)
        send(gdy(pack, j), half, half, y_dev)

    def gather_end(pack):
        for j in range(4):
            arrived(gdx(pack, j), piece(1 - a, pack, z_at(-j) * 2 + 1 - y, 0, 48))
            arrived(gdy(pack, j), piece(1 - a, pack, z_at(-j) * 2 + 1 - y, 48, 48))

    def gather_left(pack):
        whole, half = piece(a, pack, dp), piece(a, pack, dp, 0, 48)
        for j in range(1, 4):
            left(gz(pack, j), whole)
        for j in range(4):
            left(gx(pack, j), whole)
            left(gy(pack, j), whole)
            left(gdx(pack, j), half)
            left(gdy(pack, j), half)

    def scatter_start(pack):
        for i in (2, 1, 3, 0):
            chip = z_at(i) * 2 + 1 - y
            send(sdx(pack, i), piece(1 - a, pack, chip, 0, 48), diag_x.at[pack, i], x_dev)
            send(sdy(pack, i), piece(1 - a, pack, chip, 48, 48), diag_y.at[pack, i], y_dev)

    def add_to(side, pack, chip, start, size, block):
        rows = pl.ds(pl.multiple_of(pl.multiple_of(chip * 96, 16) + start, 16), size)
        full[side, pack, rows, :] = (
            full[side, pack, rows, :].astype(F32) + block.astype(F32)
        ).astype(BF16)

    def scatter_near(pack, i):
        chip = z_at(i) * 2
        arrived(sdx(pack, i), diag_x.at[pack, i])
        add_to(a, pack, chip + 1 - y, 0, 48, diag_x[pack, i])
        send(sny(pack, i), piece(a, pack, chip + 1 - y), near_y.at[pack, i], y_dev)
        arrived(sdy(pack, i), diag_y.at[pack, i])
        add_to(1 - a, pack, chip + y, 48, 48, diag_y[pack, i])
        send(snx(pack, i), piece(1 - a, pack, chip + y), near_x.at[pack, i], x_dev)

    def scatter_line(pack, i):
        arrived(snx(pack, i), near_x.at[pack, i])
        arrived(sny(pack, i), near_y.at[pack, i])
        chip = z_at(i) * 2 + y
        rows = pl.ds(pl.multiple_of(chip * 96, 16), 96)
        own = (
            full[a, pack, rows, :].astype(F32)
            + near_x[pack, i].astype(F32)
            + near_y[pack, i].astype(F32)
        )
        if i == 0:
            total[pack] = own
        else:
            full[a, pack, rows, :] = own.astype(BF16)
            send(snz(pack, i), piece(a, pack, chip), near_z.at[pack, i - 1], z_dev(i))

    def scatter_end(pack):
        own = total[pack]
        for i in range(1, 4):
            arrived(snz(pack, i), near_z.at[pack, i - 1])
            own = own + near_z[pack, i - 1].astype(F32)
        gout_ref[pack] = own

    def scatter_left(pack):
        whole, half = piece(a, pack, dp), piece(a, pack, dp, 0, 48)
        for i in range(4):
            left(sdx(pack, i), half)
            left(sdy(pack, i), half)
            left(snx(pack, i), whole)
            left(sny(pack, i), whole)
            if i > 0:
                left(snz(pack, i), whole)

    send(M_MASK, mask_ref, masks.at[a], x_dev)
    send(M_IN, in_ref.at[1 - a], tokens.at[tensor], x_dev)
    for j in range(1, 4):
        send(M_VZ + j - 1, vec_ref, vec_z.at[j - 1], z_dev(j))
    gather_start(0)
    tokens[tensor] = in_ref[a]
    masks[a] = mask_ref[...]
    cots[a] = cot_ref[a]
    send(M_TOK, tokens.at[tensor], tokens.at[tensor], core_dev)
    vec_own = vec_ref[...].astype(F32)
    for j in range(1, 4):
        arrived(M_VZ + j - 1, vec_z.at[j - 1])
        vec_own = vec_own + vec_z[j - 1].astype(F32)
    vec_y[0] = vec_own.astype(BF16)
    send(M_VY, vec_y.at[0], vec_y.at[1], y_dev)
    gather_spread(0, 1)
    gather_spread(0, 3)
    gather_spread(0, 2)
    arrived(M_VY, vec_y.at[1])
    vec_all[a] = (vec_own + vec_y[1].astype(F32)).astype(BF16)
    send(M_VX, vec_all.at[a], vec_all.at[a], x_dev)
    gather_corner(0, 0)
    other = (tensor + 2) % 4
    arrived(M_IN, tokens.at[other])
    send(M_TOK + 1, tokens.at[other], tokens.at[other], core_dev)
    gather_corner(0, 1)
    gather_corner(0, 3)
    gather_corner(0, 2)
    gather_start(1)
    arrived(M_MASK, masks.at[1 - a])
    spread = (
        lax.broadcasted_iota(jnp.int32, (128, 16 * BLOCK), 1) // BLOCK
        == lax.broadcasted_iota(jnp.int32, (128, 16 * BLOCK), 0)
    )
    spread = jnp.where(spread, 1.0, 0.0).astype(BF16)
    for side in range(2):
        bias = (dims(masks[side], spread, 1, 0) - 1.0) * 1e9
        for head in range(3):
            pair, place = (side, head) if head < 2 else (2, side)
            for part in range(4):
                start = head * 16 + part * 4
                bias_q[pair, place, part] = bias[start : start + 4]
            bias_k[pair, place] = bias[48 + head * 16 : 64 + head * 16]
    arrived(M_VX, vec_all.at[1 - a])
    vecs = [vec_all[side].astype(F32) for side in range(2)]
    arrived(M_TOK, tokens.at[0])
    arrived(M_TOK + 1, tokens.at[0])
    gather_end(0)

    def vector(row):
        return vec_all[0, row : row + 1, :].astype(F32)

    @pl.loop(0, 3)
    def _(part):
        rows = pl.ds(pl.multiple_of(part * TILE, TILE), TILE)
        query, key, value, out = pairs_of(full[0, 0, rows, :], full[1, 0, rows, :])
        w_in[rows, :] = jnp.concatenate(query + key + value, 1)
        w_out[rows, :] = jnp.concatenate(out, 1)

    query, key, value, _ = pairs_of(vecs[0], vecs[1])
    in_bias = jnp.concatenate(query + key + value, 1)[7:8]

    @pl.loop(0, 4)
    def _(quarter):
        rows = pl.ds(pl.multiple_of(quarter * TILE, TILE), TILE)
        for kind in range(3):
            cols = slice(384 * kind, 384 * kind + 384)
            block = dims(tokens[quarter], w_in[:, cols], 1, 0) + in_bias[:, cols]
            block = block.astype(BF16)
            for pair in range(3):
                heads[3 * kind + pair, rows, :] = block[:, 128 * pair : 128 * pair + 128]

    gather_spread(1, 1)
    gather_spread(1, 3)
    gather_spread(1, 2)

    low = low_lanes((TILE, 128))
    none = jnp.zeros((TILE, 128), BF16)

    def of_head(block, head):
        return jnp.where(low, block, none) if head == 0 else jnp.where(low, none, block)

    @pl.loop(0, 12)
    def _(step):
        pair, part = step // 4, step % 4
        rows = pl.ds(pl.multiple_of(part * TILE, TILE), TILE)
        query_block = heads[pair, rows, :]
        outs = []
        for head in range(2):
            scores = dims(of_head(query_block, head), heads[3 + pair], 1, 1)
            bias = bias_q[pair, head, part]
            scores = (
                scores.reshape(4, BLOCK, 16 * BLOCK) * (SCORE_SCALE * LOG2E)
                + bias.reshape(4, 1, 16 * BLOCK)
            ).reshape(TILE, 16 * BLOCK)
            most = jnp.max(scores, axis=1, keepdims=True)
            terms = jnp.exp2(scores - most)
            sums = jnp.sum(terms, axis=1, keepdims=True)
            outs.append((dims(terms.astype(BF16), heads[6 + pair], 1, 0) / sums, most + jnp.log2(sums)))
        mixed[pair, rows, :] = jnp.where(low, outs[0][0], outs[1][0]).astype(BF16)
        lse[pair, rows, :] = jnp.where(low, outs[0][1], outs[1][1])

        @pl.when(step % 3 == 2)
        def _():
            gather_corner(1, step // 3)

    gather_start(2)

    def wide(ref, start, count, quarter):
        rows = pl.ds(pl.multiple_of(quarter * TILE, TILE), TILE)
        return jnp.concatenate([ref[start + index, rows, :] for index in range(count)], 1)

    def give(number, slot, block):
        send_buf[number % 2, slot] = block.astype(BF16)
        index = M_PART + 2 * number + slot
        send(index, send_buf.at[number % 2, slot], recv_buf.at[number, slot], core_dev)

    def take(number, slot):
        arrived(M_PART + 2 * number + slot, recv_buf.at[number, slot])
        return recv_buf[number, slot].astype(F32)

    def given(number):
        for slot in range(2):
            left(M_PART + 2 * number + slot, send_buf.at[number % 2, slot])

    def share(kind, slot, ref):
        spot = ref.at[2 * slot + b]
        send(M_ROWS + 2 * kind + slot, spot, spot, core_dev)

    def shared(kind, slot, ref):
        arrived(M_ROWS + 2 * kind + slot, ref.at[2 * slot + 1 - b])

    def branch_part(quarter):
        return dims(wide(mixed, 0, 3, quarter), w_out[...], 1, 1)

    for slot in range(2):
        give(0, slot, branch_part(2 * slot + 1 - b))
    for slot in range(2):
        quarter = 2 * slot + b
        own = branch_part(quarter)
        hidden = tokens[quarter].astype(F32) + own + take(0, slot) + vector(0)
        normed, factor = norm_of(hidden)
        hat_first[slot] = normed
        fac_first[slot] = factor
        first_low[quarter] = (normed * vector(1) + vector(2)).astype(BF16)
        share(0, slot, first_low)
    gather_spread(2, 1)
    gather_spread(2, 3)
    gather_spread(2, 2)
    gather_end(1)

    def feed_up(quarter):
        for side in range(2):
            inner_buf[...] = (
                dims(first_low[quarter], full[side, 1], 1, 0)
                + vec_all[side, 6:7, :].astype(F32)
            )

            @pl.loop(0, TILE // 32)
            def _(chunk):
                rows = pl.ds(pl.multiple_of(chunk * 32, 32), 32)
                inner = inner_buf[rows, :]
                normal = 0.5 * (1.0 + lax.erf(inner * 0.7071067811865476))
                density = jnp.exp2(inner * inner * (-0.5 * LOG2E)) * 0.3989422804014327
                active[side, quarter, rows, :] = (inner * normal).astype(BF16)
                slope[side, quarter, rows, :] = (normal + inner * density).astype(BF16)

    def feed_down(quarter):
        return dims(active[0, quarter], full[0, 2], 1, 1) + dims(active[1, quarter], full[1, 2], 1, 1)

    feed_up(b)
    gather_corner(2, 0)
    gather_corner(2, 1)
    feed_up(2 + b)
    gather_corner(2, 3)
    gather_corner(2, 2)
    send(M_COT, cot_ref.at[1 - a], cots.at[a], x_dev)
    for slot in range(2):
        shared(0, slot, first_low)
        feed_up(2 * slot + 1 - b)
    gather_end(2)
    for slot in range(2):
        give(1, slot, feed_down(2 * slot + 1 - b))
    arrived(M_COT, cots.at[1 - a])
    vgrad[...] = jnp.zeros_like(vgrad)
    for slot in range(2):
        quarter = 2 * slot + b
        own = feed_down(quarter)
        second_in = hat_first[slot] * vector(1) + vector(2) + own + take(1, slot) + vector(3)
        normed, factor = norm_of(second_in)
        swap_out[slot] = (normed * vector(4) + vector(5)).astype(BF16)
        upstream = cots[slot].astype(F32)
        back = norm_pull(upstream, normed, factor, vector(4))
        back_rows[slot] = back
        feed_low[quarter] = back.astype(BF16)
        share(1, slot, feed_low)
        vgrad[0:1, :] += row_sum(upstream * normed)
        vgrad[1:2, :] += row_sum(upstream)
        vgrad[2:3, :] += row_sum(back)
    out_ref[a] = swap_out[a]
    send(M_OUT, swap_out.at[1 - a], out_ref.at[a], x_dev)
    for pack in range(3):
        gather_left(pack)

    def feed_back(quarter):
        for side in range(2):
            block = dims(feed_low[quarter], full[side, 2], 1, 0) * slope[side, quarter].astype(F32)
            inner_low = block.astype(BF16)
            slope[side, quarter] = inner_low
            vgrad[6 + side : 7 + side, :] += row_sum(inner_low.astype(F32))

    def rest_back(quarter):
        return dims(slope[0, quarter], full[0, 1], 1, 1) + dims(slope[1, quarter], full[1, 1], 1, 1)

    def tall(ref, cols):
        return ref[:, :, cols].reshape(4 * TILE, TILE)

    def weight_grad(pack, left_rows, right_rows):
        for side_step in range(2):
            side = 1 - a if side_step == 0 else a
            right = right_rows[side].reshape(4 * TILE, 768)
            for part in range(3):
                block = dims(tall(left_rows, slice(TILE * part, TILE * part + TILE)), right, 0, 0)
                full[side, pack, TILE * part : TILE * part + TILE, :] = block.astype(BF16)

    feed_back(b)
    feed_back(2 + b)
    for slot in range(2):
        shared(1, slot, feed_low)
        feed_back(2 * slot + 1 - b)
    given(0)
    for slot in range(2):
        give(2, slot, rest_back(2 * slot + 1 - b))
    weight_grad(2, feed_low, active)
    scatter_start(2)
    for slot in range(2):
        quarter = 2 * slot + b
        own = rest_back(quarter)
        upstream = back_rows[slot] + own + take(2, slot)
        normed = hat_first[slot]
        back = norm_pull(upstream, normed, fac_first[slot], vector(1))
        back_rows[slot] = back
        branch_low[quarter] = back.astype(BF16)
        share(2, slot, branch_low)
        vgrad[3:4, :] += row_sum(upstream * normed)
        vgrad[4:5, :] += row_sum(upstream)
        vgrad[5:6, :] += row_sum(back)
    weight_grad(1, first_low, slope)
    scatter_start(1)

    for slot in range(2):
        shared(2, slot, branch_low)

    @pl.loop(0, 4)
    def _(quarter):
        rows = pl.ds(pl.multiple_of(quarter * TILE, TILE), TILE)
        block = dims(branch_low[quarter], w_out[...], 1, 0).astype(BF16)
        for pair in range(3):
            mixed_back[pair, rows, :] = block[:, 128 * pair : 128 * pair + 128]

    @pl.loop(0, 12)
    def _(step):
        pair, part = step // 4, step % 4

        @pl.when(part == 0)
        def _():
            pick = (
                lax.broadcasted_iota(jnp.int32, (8, 128), 1) // HEAD_DIM
                == lax.broadcasted_iota(jnp.int32, (8, 128), 0)
            )
            pick = jnp.where(pick, 1.0, 0.0).astype(BF16)
            product = mixed[pair].astype(F32) * mixed_back[pair].astype(F32)
            high = product.astype(BF16)
            rest = (product - high.astype(F32)).astype(BF16)
            rows_stat[0:8, :] = dims(pick, high, 1, 1) + dims(pick, rest, 1, 1)
            turned = lse[pair].T
            rows_stat[8:9, :] = turned[0:1]
            rows_stat[9:10, :] = turned[HEAD_DIM : HEAD_DIM + 1]
            key_sum[...] = jnp.zeros_like(key_sum)
            value_sum[...] = jnp.zeros_like(value_sum)

        cols = pl.ds(pl.multiple_of(part * TILE, TILE), TILE)
        query_block, back_block = heads[pair, cols, :], mixed_back[pair, cols, :]
        key_block, value_block = heads[3 + pair], heads[6 + pair]
        key_turned = key_block.T
        weights, score_backs, queries, backs, query_back = [], [], [], [], []
        for head in range(2):
            query_head, back_head = of_head(query_block, head), of_head(back_block, head)
            scores = dims(key_block, query_head, 1, 1)
            bias = bias_k[pair, head, :, cols] - rows_stat[8 + head : 9 + head, cols]
            weight = jnp.exp2(
                scores.reshape(16, BLOCK, TILE) * (SCORE_SCALE * LOG2E) + bias.reshape(16, 1, TILE)
            ).reshape(16 * BLOCK, TILE)
            weight_back = dims(value_block, back_head, 1, 1)
            score_back = (weight * (weight_back - rows_stat[head : head + 1, cols])).astype(BF16)
            weights.append(weight.astype(BF16))
            score_backs.append(score_back)
            queries.append(query_head)
            backs.append(back_head)
            query_back.append(dims(key_turned, score_back, 1, 0))
        value_sum[...] += dims(jnp.concatenate(weights, 1), jnp.concatenate(backs, 0), 1, 0)
        key_sum[...] += dims(jnp.concatenate(score_backs, 1), jnp.concatenate(queries, 0), 1, 0)
        top = lax.broadcasted_iota(jnp.int32, (128, TILE), 0) < HEAD_DIM
        query_grad = jnp.where(top, query_back[0], query_back[1]).T * SCORE_SCALE
        heads_back[pair, cols, :] = query_grad.astype(BF16)

        @pl.when(part == 3)
        def _():
            heads_back[3 + pair] = (key_sum[...] * SCORE_SCALE).astype(BF16)
            heads_back[6 + pair] = value_sum[...].astype(BF16)

        @pl.when(part == 3)
        def _():
            for i in (2, 1, 3, 0):

                @pl.when(pair == 0)
                def _():
                    scatter_near(2, i)

                @pl.when(pair == 1)
                def _():
                    scatter_line(2, i)
                    scatter_near(1, i)

                @pl.when(pair == 2)
                def _():
                    scatter_line(1, i)

    for part in range(3):
        cols = slice(TILE * part, TILE * part + TILE)
        token_cols = tall(tokens, cols)
        kinds = []
        for kind in range(3):
            right = jnp.concatenate([heads_back[3 * kind + pair] for pair in range(3)], 1)
            block = dims(token_cols, right, 0, 0)
            kinds.append(tuple(block[:, 128 * pair : 128 * pair + 128] for pair in range(3)))
        right = jnp.concatenate([mixed[pair] for pair in range(3)], 1)
        block = dims(tall(branch_low, cols), right, 0, 0)
        kinds.append(tuple(block[:, 128 * pair : 128 * pair + 128] for pair in range(3)))
        first, second = packs_of(*kinds)
        full[0, 0, cols, :] = first.astype(BF16)
        full[1, 0, cols, :] = second.astype(BF16)
    scatter_start(0)
    for pair in range(3):
        vgrad[8:9, 128 * pair : 128 * pair + 128] = row_sum(heads_back[pair].astype(F32))
        vgrad[8:9, 384 + 128 * pair : 512 + 128 * pair] = row_sum(heads_back[6 + pair].astype(F32))
    send(M_VG, vgrad, vrecv.at[0], core_dev)

    def input_part(quarter):
        return dims(wide(heads_back, 0, 9, quarter), w_in[...], 1, 1)

    given(1)
    for slot in range(2):
        give(3, slot, input_part(2 * slot + 1 - b))
    arrived(M_VG, vrecv.at[0])
    mine = lax.broadcasted_iota(jnp.int32, (16, 768), 0) < 6
    vsend[0] = vgrad[...] + jnp.where(mine, vrecv[0], 0.0)
    send(M_VG + 1, vsend.at[0], vrecv.at[1], x_dev)
    for i in (2, 1, 3, 0):
        scatter_near(0, i)
    for slot in range(2):
        own = input_part(2 * slot + b)
        back_rows[slot] = back_rows[slot] + own + take(3, slot)
    swap_in[0] = back_rows[1 - a].astype(BF16)
    send(M_GRAD, swap_in.at[0], swap_in.at[1], x_dev)
    grad_ref[a] = back_rows[a]
    arrived(M_VG + 1, vrecv.at[1])
    vsend[1] = vsend[0] + vrecv[1]
    send(M_VG + 2, vsend.at[1], vrecv.at[2], y_dev)
    scatter_end(2)
    scatter_end(1)
    arrived(M_VG + 2, vrecv.at[2])
    vsend[2] = vsend[1] + vrecv[2]
    for j in range(1, 4):
        send(M_VG + 2 + j, vsend.at[2], vrecv.at[2 + j], z_dev(j))
    for i in (2, 1, 3, 0):
        scatter_line(0, i)
    every = vsend[2]
    for j in range(1, 4):
        arrived(M_VG + 2 + j, vrecv.at[2 + j])
        every = every + vrecv[2 + j]
    vout_ref[...] = every
    arrived(M_GRAD, swap_in.at[1])
    grad_ref[1 - a] = swap_in[1].astype(F32)
    arrived(M_OUT, out_ref.at[1 - a])
    scatter_end(0)

    for pack in range(3):
        scatter_left(pack)
    given(2)
    given(3)
    left(M_MASK, mask_ref)
    left(M_IN, in_ref.at[0])
    left(M_COT, cot_ref.at[0])
    left(M_OUT, swap_out.at[0])
    left(M_GRAD, swap_in.at[0])
    for j in range(3):
        left(M_VZ + j, vec_ref)
    left(M_VY, vec_y.at[0])
    left(M_VX, vec_all.at[0])
    for slot in range(2):
        left(M_TOK + slot, tokens.at[0])
        for kind in range(3):
            left(M_ROWS + 2 * kind + slot, first_low.at[0])
    for index in range(6):
        left(M_VG + index, vsend.at[0])


def layer_call(packs, vectors, masks, tokens, cotangent):
    vmem = pltpu.VMEM
    anywhere = pl.BlockSpec(memory_space=pltpu.VMEM)
    shape = jax.ShapeDtypeStruct
    scratch = [
        vmem((2, 3, 768, 768), BF16),
        vmem((3, 16, 768), BF16),
        vmem((2, 16, 768), BF16),
        vmem((2, 16, 768), BF16),
        vmem((2, 96, 128), BF16),
        vmem((4, TILE, 768), BF16),
        vmem((2, TILE, 768), BF16),
        vmem((768, 1152), BF16),
        vmem((768, 384), BF16),
        vmem((3, 2, 4, 4, 1024), F32),
        vmem((3, 2, 16, 1024), F32),
        vmem((9, 1024, 128), BF16),
        vmem((3, 1024, 128), BF16),
        vmem((3, 1024, 128), F32),
        vmem((16, 1024), F32),
        vmem((4, TILE, 768), BF16),
        vmem((4, TILE, 768), BF16),
        vmem((4, TILE, 768), BF16),
        vmem((2, TILE, 768), F32),
        vmem((2, TILE, 1), F32),
        vmem((2, TILE, 768), F32),
        vmem((2, 4, TILE, 768), BF16),
        vmem((2, 4, TILE, 768), BF16),
        vmem((TILE, 768), F32),
        vmem((2, 2, TILE, 768), BF16),
        vmem((4, 2, TILE, 768), BF16),
        vmem((3, 1024, 128), BF16),
        vmem((1024, 128), F32),
        vmem((1024, 128), F32),
        vmem((9, 1024, 128), BF16),
        vmem((8, 128), F32),
        vmem((3, 4, 48, 768), BF16),
        vmem((3, 4, 48, 768), BF16),
        vmem((3, 4, 96, 768), BF16),
        vmem((3, 4, 96, 768), BF16),
        vmem((3, 3, 96, 768), BF16),
        vmem((3, 96, 768), F32),
        vmem((2, TILE, 768), BF16),
        vmem((2, TILE, 768), BF16),
        vmem((16, 768), F32),
        vmem((3, 16, 768), F32),
        vmem((6, 16, 768), F32),
        pltpu.SemaphoreType.DMA((MESSAGES,)),
        pltpu.SemaphoreType.DMA((MESSAGES,)),
    ]
    return pl.pallas_call(
        layer_kernel,
        out_shape=(
            shape(tokens.shape, BF16),
            shape(tokens.shape, F32),
            shape(packs.shape, F32),
            shape(vectors.shape, F32),
        ),
        in_specs=[anywhere] * 5,
        out_specs=(anywhere,) * 4,
        scratch_shapes=scratch,
        compiler_params=pltpu.CompilerParams(
            collective_id=0, has_side_effects=True, vmem_limit_bytes=62 << 20
        ),
    )(packs, vectors, masks, tokens, cotangent)


def local_fast(
    inputs,
    random_blocks,
    query_weight,
    query_bias,
    key_weight,
    value_weight,
    value_bias,
    out_weight,
    out_bias,
    first_gain,
    first_shift,
    up_weight,
    up_bias,
    down_weight,
    down_bias,
    second_gain,
    second_shift,
    cotangent,
):
    dp, tensor = lax.axis_index("dp"), lax.axis_index("tensor")
    out_turned = out_weight.T
    first_pack = jnp.concatenate(
        (
            query_weight[:, :128],
            key_weight[:, :128],
            value_weight[:, :128],
            query_weight[:, 128:],
            key_weight[:, 128:],
            value_weight[:, 128:],
            out_turned[:, 128:],
            out_turned[:, :128],
        ),
        1,
    )
    packs = jnp.stack((first_pack, up_weight, down_weight.T))

    def placed(values):
        width = values.shape[0]
        spots = jnp.arange(8 * width, dtype=jnp.int32) // width
        return jnp.where(spots == dp, jnp.tile(values, 8), jnp.zeros((), values.dtype))

    query_row, value_row = placed(query_bias), placed(value_bias)
    gap = jnp.zeros((128,), BF16)
    in_row = jnp.concatenate(
        (query_row[:128], gap, value_row[:128], query_row[128:], gap[:64], value_row[128:], gap, gap[:64])
    )
    rows = [
        placed(v) for v in (out_bias, first_gain, first_shift, down_bias, second_gain, second_shift, up_bias)
    ]
    vectors = jnp.concatenate((jnp.stack(rows + [in_row]), jnp.zeros((8, 768), BF16)))
    allowed = block_allowed(random_blocks, random_blocks.shape[1]).astype(BF16)
    masks = jnp.concatenate((allowed.reshape(48, 16), allowed.transpose(0, 2, 1).reshape(48, 16)))
    masks = jnp.pad(masks, ((0, 0), (0, 112)))
    output, input_grad, grads, sums = layer_call(packs, vectors, masks, inputs, cotangent)
    first = grads[0]
    query_grad = jnp.concatenate((first[:, 0:128], first[:, 384:448]), 1)
    key_grad = jnp.concatenate((first[:, 128:256], first[:, 448:512]), 1)
    value_grad = jnp.concatenate((first[:, 256:384], first[:, 512:576]), 1)
    out_grad = jnp.concatenate((first[:, 640:768], first[:, 576:640]), 1).T
    side = tensor // 2

    def own(row):
        return lax.dynamic_slice(row, (dp * 96,), (96,))

    def head_bias(row):
        both = jnp.concatenate(
            (
                lax.dynamic_slice(row, (side * 128,), (128,)),
                lax.dynamic_slice(row, (256 + side * 64,), (64,)),
            )
        )
        return lax.dynamic_slice(both, (dp * 24,), (24,))

    return (
        output,
        input_grad,
        query_grad,
        head_bias(sums[8, :384]),
        key_grad,
        value_grad,
        head_bias(sums[8, 384:]),
        out_grad,
        own(sums[5]),
        own(sums[3]),
        own(sums[4]),
        grads[1],
        own(lax.dynamic_slice(sums, (6 + side, 0), (1, 768))[0]),
        grads[2].T,
        own(sums[2]),
        own(sums[0]),
        own(sums[1]),
    )


def solution(mesh):
    sizes = mesh.shape
    fast = sizes["dp"] == 8 and sizes["tensor"] == 4
    return jax.shard_map(
        local_fast if fast else local,
        mesh=mesh,
        in_specs=(
            P("dp", "tensor", None),
            P("tensor", None, None),
            P("dp", "tensor"),
            P(("tensor", "dp")),
            P("dp", "tensor"),
            P("dp", "tensor"),
            P(("tensor", "dp")),
            P("tensor", "dp"),
            P("dp"),
            P("dp"),
            P("dp"),
            P("dp", "tensor"),
            P(("tensor", "dp")),
            P("tensor", "dp"),
            P("dp"),
            P("dp"),
            P("dp"),
            P("dp", "tensor", None),
        ),
        out_specs=(
            P("dp", "tensor", None),
            P("dp", "tensor", None),
            P("dp", "tensor"),
            P(("tensor", "dp")),
            P("dp", "tensor"),
            P("dp", "tensor"),
            P(("tensor", "dp")),
            P("tensor", "dp"),
            P("dp"),
            P("dp"),
            P("dp"),
            P("dp", "tensor"),
            P(("tensor", "dp")),
            P("tensor", "dp"),
            P("dp"),
            P("dp"),
            P("dp"),
        ),
        check_vma=False,
    )
```

```python
from functools import partial

import jax
import jax.numpy as jnp
from jax import lax
from jax.experimental import pallas as pl
from jax.experimental.pallas import tpu as pltpu
from jax.sharding import PartitionSpec as P

HEAD_DIM = 64
BLOCK = 64


norm_eps = 1e-12


def gather_weights(shards):
    return (
        lax.all_gather(shards[0], "dp", axis=0, tiled=True),
        lax.all_gather(shards[1], "dp", axis=0, tiled=True),
        lax.all_gather(shards[2], "dp", axis=0, tiled=True),
        lax.all_gather(shards[3], "dp", axis=0, tiled=True),
        lax.all_gather(shards[4], "dp", axis=0, tiled=True),
        lax.all_gather(shards[5], "dp", axis=1, tiled=True),
        lax.all_gather(shards[6], "dp", axis=0, tiled=True),
        lax.all_gather(shards[7], "dp", axis=0, tiled=True),
        lax.all_gather(shards[8], "dp", axis=0, tiled=True),
        lax.all_gather(shards[9], "dp", axis=0, tiled=True),
        lax.all_gather(shards[10], "dp", axis=0, tiled=True),
        lax.all_gather(shards[11], "dp", axis=1, tiled=True),
        lax.all_gather(shards[12], "dp", axis=0, tiled=True),
        lax.all_gather(shards[13], "dp", axis=0, tiled=True),
        lax.all_gather(shards[14], "dp", axis=0, tiled=True),
    )


def reduce_grads(grads):
    return (
        lax.psum_scatter(grads[0], "dp", scatter_dimension=0, tiled=True),
        lax.psum_scatter(grads[1], "dp", scatter_dimension=0, tiled=True),
        lax.psum_scatter(grads[2], "dp", scatter_dimension=0, tiled=True),
        lax.psum_scatter(grads[3], "dp", scatter_dimension=0, tiled=True),
        lax.psum_scatter(grads[4], "dp", scatter_dimension=0, tiled=True),
        lax.psum_scatter(grads[5], "dp", scatter_dimension=1, tiled=True),
        lax.psum_scatter(grads[6], "dp", scatter_dimension=0, tiled=True),
        lax.psum_scatter(grads[7], "dp", scatter_dimension=0, tiled=True),
        lax.psum_scatter(grads[8], "dp", scatter_dimension=0, tiled=True),
        lax.psum_scatter(grads[9], "dp", scatter_dimension=0, tiled=True),
        lax.psum_scatter(grads[10], "dp", scatter_dimension=0, tiled=True),
        lax.psum_scatter(grads[11], "dp", scatter_dimension=1, tiled=True),
        lax.psum_scatter(grads[12], "dp", scatter_dimension=0, tiled=True),
        lax.psum_scatter(grads[13], "dp", scatter_dimension=0, tiled=True),
        lax.psum_scatter(grads[14], "dp", scatter_dimension=0, tiled=True),
    )


def full_rows(block):
    return lax.all_gather(block, "tensor", axis=0, tiled=True)


def column_sums(partial_terms):
    return lax.psum_scatter(
        partial_terms.astype(jnp.bfloat16), "tensor", scatter_dimension=0, tiled=True
    ).astype(jnp.float32)


def block_allowed(random_blocks, block_count):
    row_ids = jnp.arange(block_count, dtype=jnp.int32)[:, None]
    col_ids = jnp.arange(block_count, dtype=jnp.int32)[None, :]
    fixed = (
        (jnp.abs(row_ids - col_ids) <= 1)
        | (col_ids == 0)
        | (col_ids == block_count - 1)
        | (row_ids == 0)
        | (row_ids == block_count - 1)
    )
    picked = jnp.any(
        random_blocks[:, :, :, None]
        == jnp.arange(block_count, dtype=jnp.int32)[None, None, None, :],
        axis=2,
    )
    return fixed[None, :, :] | picked


def layer_norm(values, gain, shift):
    mean = jnp.mean(values, axis=1, keepdims=True)
    spread = jnp.mean(values * values, axis=1, keepdims=True) - mean * mean
    factor = lax.rsqrt(spread + norm_eps)
    normed = (values - mean) * factor
    return (normed * gain + shift, normed, factor)


def norm_back(upstream, normed, factor, gain):
    scaled = upstream * gain
    plain = jnp.mean(scaled, axis=1, keepdims=True)
    along = jnp.mean(scaled * normed, axis=1, keepdims=True)
    back = factor * (scaled - plain - normed * along)
    return (back, jnp.sum(upstream * normed, axis=0), jnp.sum(upstream, axis=0))


def row_parts(array, span):
    return array.reshape((array.shape[0] // span, span) + array.shape[1:])


def mask_parts(allowed, span):
    return allowed.reshape(allowed.shape[0], -1, span // BLOCK, allowed.shape[2]).transpose(
        1, 0, 2, 3
    )


def block_scores(query_block, key_heads, mask_block):
    products = jnp.einsum(
        "qhd,khd->hqk", query_block, key_heads, preferred_element_type=jnp.float32
    )
    head_count, row_count, key_count = products.shape
    scaled = (products * HEAD_DIM ** (-0.5)).reshape(
        head_count, row_count // BLOCK, BLOCK, key_count // BLOCK, BLOCK
    )
    masked = jnp.where(mask_block[:, :, None, :, None], scaled, -1000000000.0)
    return masked.reshape(head_count, row_count, key_count)


def attend(query_heads, key_heads, value_heads, allowed):
    length = query_heads.shape[0]
    span = min(512, length)

    def one_part(items):
        query_block, mask_block = items
        scores = block_scores(query_block, key_heads, mask_block)
        largest = jnp.max(scores, axis=-1, keepdims=True)
        log_total = largest + jnp.log(jnp.sum(jnp.exp(scores - largest), axis=-1, keepdims=True))
        weights_low = jnp.exp(scores - log_total).astype(jnp.bfloat16)
        mixed = jnp.einsum(
            "hqk,khd->qhd", weights_low, value_heads, preferred_element_type=jnp.float32
        )
        return (mixed, log_total[..., 0])

    mixed, log_totals = lax.map(one_part, (row_parts(query_heads, span), mask_parts(allowed, span)))
    return (mixed.reshape(length, -1).astype(jnp.bfloat16), log_totals)


def attend_back(query_heads, key_heads, value_heads, mixed_back, log_totals, allowed):
    length = query_heads.shape[0]
    span = min(512, length)

    def one_part(carry, items):
        key_sum, value_sum = carry
        query_block, back_block, log_total, mask_block = items
        scores = block_scores(query_block, key_heads, mask_block)
        weights = jnp.exp(scores - log_total[..., None])
        weights_low = weights.astype(jnp.bfloat16)
        weights_back = jnp.einsum(
            "qhd,khd->hqk", back_block, value_heads, preferred_element_type=jnp.float32
        )
        centre = jnp.sum(weights_back * weights, axis=-1, keepdims=True)
        scores_back = (weights * (weights_back - centre) * HEAD_DIM ** (-0.5)).astype(jnp.bfloat16)
        query_back = jnp.einsum(
            "hqk,khd->qhd", scores_back, key_heads, preferred_element_type=jnp.float32
        )
        key_sum = key_sum + jnp.einsum(
            "hqk,qhd->khd", scores_back, query_block, preferred_element_type=jnp.float32
        )
        value_sum = value_sum + jnp.einsum(
            "hqk,qhd->khd", weights_low, back_block, preferred_element_type=jnp.float32
        )
        return ((key_sum, value_sum), query_back)

    empty = jnp.zeros(key_heads.shape, jnp.float32)
    (key_back, value_back), query_back = lax.scan(
        one_part,
        (empty, empty),
        (
            row_parts(query_heads, span),
            row_parts(mixed_back, span),
            log_totals,
            mask_parts(allowed, span),
        ),
    )
    return (
        query_back.reshape(length, -1).astype(jnp.bfloat16),
        key_back.reshape(length, -1).astype(jnp.bfloat16),
        value_back.reshape(length, -1).astype(jnp.bfloat16),
    )


def forward_pass(weights, token_block, allowed):
    (
        query_weight,
        query_bias,
        key_weight,
        value_weight,
        value_bias,
        out_weight,
        out_bias,
        first_gain,
        first_shift,
        up_weight,
        up_bias,
        down_weight,
        down_bias,
        second_gain,
        second_shift,
    ) = weights
    token_rows = full_rows(token_block)
    length = token_rows.shape[0]

    def heads_of(product):
        return product.astype(jnp.bfloat16).reshape(length, -1, HEAD_DIM)

    query_heads = heads_of(
        jnp.dot(token_rows, query_weight, preferred_element_type=jnp.float32) + query_bias
    )
    key_heads = heads_of(jnp.dot(token_rows, key_weight, preferred_element_type=jnp.float32))
    value_heads = heads_of(
        jnp.dot(token_rows, value_weight, preferred_element_type=jnp.float32) + value_bias
    )
    mixed, log_totals = attend(query_heads, key_heads, value_heads, allowed)
    branch_terms = jnp.dot(mixed, out_weight, preferred_element_type=jnp.float32)
    hidden = token_block.astype(jnp.float32) + column_sums(branch_terms) + out_bias
    first_norm, first_normed, first_factor = layer_norm(hidden, first_gain, first_shift)
    first_rows = full_rows(first_norm.astype(jnp.bfloat16))
    inner = jnp.dot(first_rows, up_weight, preferred_element_type=jnp.float32) + up_bias
    active = jax.nn.gelu(inner, approximate=False).astype(jnp.bfloat16)
    second_in = (
        first_norm
        + column_sums(jnp.dot(active, down_weight, preferred_element_type=jnp.float32))
        + down_bias
    )
    result, second_normed, second_factor = layer_norm(second_in, second_gain, second_shift)
    kept = (
        token_rows,
        query_heads,
        key_heads,
        value_heads,
        log_totals,
        mixed,
        first_normed,
        first_factor,
        first_rows,
        inner,
        active,
        second_normed,
        second_factor,
    )
    return (result, kept)


def backward_pass(weights, kept, upstream_block, allowed):
    (
        query_weight,
        query_bias,
        key_weight,
        value_weight,
        value_bias,
        out_weight,
        out_bias,
        first_gain,
        first_shift,
        up_weight,
        up_bias,
        down_weight,
        down_bias,
        second_gain,
        second_shift,
    ) = weights
    (
        token_rows,
        query_heads,
        key_heads,
        value_heads,
        log_totals,
        mixed,
        first_normed,
        first_factor,
        first_rows,
        inner,
        active,
        second_normed,
        second_factor,
    ) = kept
    length = token_rows.shape[0]
    upstream = upstream_block.astype(jnp.float32)
    second_back, second_gain_grad, second_shift_grad = norm_back(
        upstream, second_normed, second_factor, second_gain
    )
    down_bias_grad = jnp.sum(second_back, axis=0)
    feed_rows = full_rows(second_back.astype(jnp.bfloat16))
    down_weight_grad = jnp.einsum(
        "tf,td->fd", active, feed_rows, preferred_element_type=jnp.float32
    )
    active_back = jnp.einsum(
        "td,fd->tf", feed_rows, down_weight, preferred_element_type=jnp.float32
    )
    inner_back = jax.vjp(partial(jax.nn.gelu, approximate=False), inner)[1](active_back)[0].astype(
        jnp.bfloat16
    )
    up_bias_grad = jnp.sum(inner_back, axis=0, dtype=jnp.float32)
    up_weight_grad = jnp.einsum(
        "td,tf->df", first_rows, inner_back, preferred_element_type=jnp.float32
    )
    first_back = second_back + column_sums(
        jnp.einsum("tf,df->td", inner_back, up_weight, preferred_element_type=jnp.float32)
    )
    hidden_back, first_gain_grad, first_shift_grad = norm_back(
        first_back, first_normed, first_factor, first_gain
    )
    out_bias_grad = jnp.sum(hidden_back, axis=0)
    branch_rows = full_rows(hidden_back.astype(jnp.bfloat16))
    out_weight_grad = jnp.einsum(
        "tc,td->cd", mixed, branch_rows, preferred_element_type=jnp.float32
    )
    mixed_back = jnp.einsum(
        "td,cd->tc", branch_rows, out_weight, preferred_element_type=jnp.float32
    ).astype(jnp.bfloat16)
    query_back, key_back, value_back = attend_back(
        query_heads,
        key_heads,
        value_heads,
        mixed_back.reshape(length, -1, HEAD_DIM),
        log_totals,
        allowed,
    )
    query_weight_grad = jnp.einsum(
        "td,tc->dc", token_rows, query_back, preferred_element_type=jnp.float32
    )
    key_weight_grad = jnp.einsum(
        "td,tc->dc", token_rows, key_back, preferred_element_type=jnp.float32
    )
    value_weight_grad = jnp.einsum(
        "td,tc->dc", token_rows, value_back, preferred_element_type=jnp.float32
    )
    query_bias_grad = jnp.sum(query_back, axis=0, dtype=jnp.float32)
    value_bias_grad = jnp.sum(value_back, axis=0, dtype=jnp.float32)
    projected = (
        jnp.einsum("tc,dc->td", query_back, query_weight, preferred_element_type=jnp.float32)
        + jnp.einsum("tc,dc->td", key_back, key_weight, preferred_element_type=jnp.float32)
        + jnp.einsum("tc,dc->td", value_back, value_weight, preferred_element_type=jnp.float32)
    )
    input_back = hidden_back + column_sums(projected)
    grads = (
        query_weight_grad,
        query_bias_grad,
        key_weight_grad,
        value_weight_grad,
        value_bias_grad,
        out_weight_grad,
        out_bias_grad,
        first_gain_grad,
        first_shift_grad,
        up_weight_grad,
        up_bias_grad,
        down_weight_grad,
        down_bias_grad,
        second_gain_grad,
        second_shift_grad,
    )
    return (input_back, grads)


def local(
    inputs,
    random_blocks,
    query_weight,
    query_bias,
    key_weight,
    value_weight,
    value_bias,
    out_weight,
    out_bias,
    first_gain,
    first_shift,
    up_weight,
    up_bias,
    down_weight,
    down_bias,
    second_gain,
    second_shift,
    cotangent,
):
    shards = (
        query_weight,
        query_bias,
        key_weight,
        value_weight,
        value_bias,
        out_weight,
        out_bias,
        first_gain,
        first_shift,
        up_weight,
        up_bias,
        down_weight,
        down_bias,
        second_gain,
        second_shift,
    )
    allowed = block_allowed(random_blocks, random_blocks.shape[1])
    resident = gather_weights(shards)
    growth = lax.axis_size("dp")
    grown_dims = (0, 0, 0, 0, 0, 1, 0, 0, 0, 0, 0, 1, 0, 0, 0)
    start = tuple(
        (
            jnp.zeros(
                tuple(
                    (
                        extent * growth if position == grown_dim else extent
                        for position, extent in enumerate(shard.shape)
                    )
                ),
                jnp.float32,
            )
            for shard, grown_dim in zip(shards, grown_dims)
        )
    )

    def one_sequence(totals, items):
        token_block, upstream_block = items
        result, kept = forward_pass(resident, token_block, allowed)
        input_back, grads = backward_pass(resident, kept, upstream_block, allowed)
        totals = tuple((summed + update for summed, update in zip(totals, grads)))
        return (totals, (result.astype(jnp.bfloat16), input_back))

    totals, (results, input_backs) = lax.scan(one_sequence, start, (inputs, cotangent))
    shares = reduce_grads(totals)
    vectors = lax.psum(
        (shares[6], shares[7], shares[8], shares[12], shares[13], shares[14]), "tensor"
    )
    return (
        results,
        input_backs,
        shares[0],
        shares[1],
        shares[2],
        shares[3],
        shares[4],
        shares[5],
        vectors[0],
        vectors[1],
        vectors[2],
        shares[9],
        shares[10],
        shares[11],
        vectors[3],
        vectors[4],
        vectors[5],
    )


MESH = pl.DeviceIdType.MESH
(
    START,
    SPREAD,
    OVER_Y,
    OVER_X,
    DEEP,
    BACK_DEEP,
    BACK_Y,
    BACK_X,
    BACK_LINE,
    COT,
) = range(10)
PLAN = {
    "pre": (
        (START, 1, 0),
        (OVER_Y, 0, 0),
        (SPREAD, 0, 1),
        (OVER_Y, 1, 0),
        (SPREAD, 0, 2),
    ),
    "tok": (
        (SPREAD, 0, 3),
        (SPREAD, 1, 1),
        (OVER_X, 1, 0),
    ),
    "p0": (
        (OVER_X, 0, 1),
        (SPREAD, 1, 2),
        (OVER_X, 0, 0),
        (DEEP, 0, 0),
        (OVER_Y, 0, 3),
        (OVER_X, 0, 2),
        (OVER_Y, 0, 2),
        (OVER_Y, 0, 1),
        (START, 2, 0),
        (OVER_X, 0, 3),
        (OVER_Y, 1, 2),
        (DEEP, 1, 0),
        (START, 3, 0),
        (OVER_X, 1, 1),
        (OVER_X, 1, 2),
    ),
    "q0": (
        (SPREAD, 1, 3),
        (SPREAD, 2, 1),
    ),
    "q1": (
        (OVER_Y, 2, 0),
        (SPREAD, 2, 3),
        (OVER_X, 1, 3),
        (OVER_Y, 1, 3),
        (DEEP, 2, 0),
        (OVER_Y, 1, 1),
    ),
    "f1": (
        (OVER_X, 2, 0),
        (OVER_X, 2, 1),
        (SPREAD, 2, 2),
    ),
    "f3": (
        (OVER_Y, 2, 1),
        (OVER_X, 2, 3),
    ),
    "f4": (
        (COT, 0, 0),
    ),
    "f7": (
        (OVER_X, 3, 0),
    ),
    "p1": (
        (SPREAD, 3, 1),
    ),
    "f9": (
        (OVER_X, 2, 2),
    ),
    "f10": (
        (OVER_Y, 2, 3),
        (OVER_Y, 3, 0),
        (SPREAD, 3, 3),
    ),
    "f11": (
        (OVER_Y, 2, 2),
        (SPREAD, 3, 2),
    ),
    "b0": (
        (OVER_X, 3, 1),
        (OVER_Y, 3, 1),
    ),
    "b1": (
        (OVER_Y, 3, 3),
    ),
    "u0": (
        (OVER_X, 3, 3),
    ),
    "u1": (
        (OVER_X, 3, 2),
        (DEEP, 3, 0),
        (OVER_Y, 3, 2),
    ),
    "r0": (
        (BACK_X, 3, 2),
        (BACK_Y, 3, 3),
        (BACK_Y, 3, 2),
        (BACK_X, 4, 3),
        (BACK_X, 3, 3),
        (BACK_X, 4, 1),
        (BACK_DEEP, 3, 0),
        (BACK_Y, 4, 3),
        (BACK_X, 3, 1),
        (BACK_Y, 4, 1),
    ),
    "r1": (
        (BACK_LINE, 3, 2),
        (BACK_X, 4, 2),
        (BACK_DEEP, 4, 0),
    ),
    "r2": (
        (BACK_X, 3, 0),
        (BACK_X, 4, 0),
        (BACK_Y, 3, 1),
        (BACK_LINE, 3, 3),
        (BACK_Y, 3, 0),
    ),
    "r3": (
        (BACK_Y, 4, 2),
        (BACK_Y, 4, 0),
    ),
    "k0": (
        (BACK_LINE, 4, 3),
    ),
    "k1": (
        (BACK_X, 2, 2),
        (BACK_X, 2, 3),
    ),
    "k2": (
        (BACK_LINE, 3, 1),
    ),
    "k3": (
        (BACK_LINE, 4, 1),
        (BACK_Y, 2, 2),
        (BACK_LINE, 4, 2),
    ),
    "k4": (
        (BACK_X, 2, 1),
        (BACK_DEEP, 2, 0),
    ),
    "k5": (
        (BACK_Y, 2, 1),
        (BACK_Y, 2, 3),
    ),
    "k7": (
        (BACK_LINE, 2, 2),
        (BACK_Y, 2, 0),
    ),
    "k8": (
        (BACK_Y, 0, 2),
        (BACK_X, 2, 0),
    ),
    "k9": (
        (BACK_Y, 0, 3),
        (BACK_X, 0, 2),
    ),
    "k10": (
        (BACK_X, 0, 1),
    ),
    "k11": (
        (BACK_X, 0, 3),
    ),
    "t0": (
        (BACK_LINE, 3, 0),
        (BACK_LINE, 4, 0),
        (BACK_DEEP, 0, 0),
    ),
    "t1": (
        (BACK_LINE, 0, 2),
        (BACK_LINE, 2, 1),
        (BACK_Y, 0, 1),
        (BACK_LINE, 2, 3),
        (BACK_X, 1, 2),
        (BACK_X, 1, 3),
        (BACK_Y, 1, 1),
        (BACK_X, 0, 0),
        (BACK_X, 1, 1),
        (BACK_LINE, 2, 0),
        (BACK_Y, 1, 3),
    ),
    "t2": (
        (BACK_LINE, 0, 1),
        (BACK_Y, 1, 2),
        (BACK_LINE, 1, 1),
        (BACK_LINE, 0, 3),
        (BACK_Y, 0, 0),
        (BACK_LINE, 1, 2),
        (BACK_LINE, 1, 3),
        (BACK_DEEP, 1, 0),
        (BACK_LINE, 0, 0),
    ),
    "t3": (
        (BACK_X, 1, 0),
        (BACK_Y, 1, 0),
        (BACK_LINE, 1, 0),
    ),
}
F32 = jnp.float32
BF16 = jnp.bfloat16
LOG2E = 1.4426950408889634
SCORE_SCALE = HEAD_DIM ** (-0.5)
TILE = 256
MESSAGES = 272
LEAN = 16
TURN = 32
BEND = 48


def dims(left, right, left_dim, right_dim):
    return lax.dot_general(
        left, right, (((left_dim,), (right_dim,)), ((), ())), preferred_element_type=F32
    )


def low_lanes(shape):
    return lax.broadcasted_iota(jnp.int32, shape, len(shape) - 1) < HEAD_DIM


def half_turn(block):
    return pltpu.roll(block.astype(F32), HEAD_DIM, 1).astype(block.dtype)


def pairs_of(first, second):
    tile = lambda pack, index: pack[:, 128 * index : 128 * index + 128]
    low = low_lanes((first.shape[0], 128))
    e0, e1, f0, f1 = tile(first, 0), tile(second, 0), tile(first, 1), tile(second, 1)
    third = (
        jnp.where(low, e0, half_turn(e1)),
        jnp.where(low, half_turn(e0), e1),
        jnp.where(low, f0, half_turn(f1)),
    )
    out = (tile(first, 2), tile(second, 2), jnp.where(low, half_turn(f0), f1))
    return jnp.concatenate(third, 1), jnp.concatenate(out, 1)


def packs_of(third, out):
    tile = lambda block, index: block[:, 128 * index : 128 * index + 128]
    query, key, value = (tile(third, index) for index in range(3))
    low = low_lanes(query.shape)
    first = (
        jnp.where(low, query, half_turn(key)),
        jnp.where(low, value, half_turn(tile(out, 2))),
        tile(out, 0),
    )
    second = (
        jnp.where(low, half_turn(query), key),
        jnp.where(low, half_turn(value), tile(out, 2)),
        tile(out, 1),
    )
    return jnp.concatenate(first, 1), jnp.concatenate(second, 1)


def norm_of(values):
    mean = jnp.mean(values, axis=1, keepdims=True)
    spread = jnp.mean(values * values, axis=1, keepdims=True) - mean * mean
    factor = lax.rsqrt(spread + norm_eps)
    return (values - mean) * factor, factor


def norm_pull(upstream, normed, factor, gain):
    scaled = upstream * gain
    plain = jnp.mean(scaled, axis=1, keepdims=True)
    along = jnp.mean(scaled * normed, axis=1, keepdims=True)
    return factor * (scaled - plain - normed * along)


def row_sum(block):
    return jnp.sum(block, axis=0, keepdims=True)


def layer_kernel(
    query_ref,
    key_ref,
    value_ref,
    down_ref,
    up_ref,
    project_ref,
    row_refs,
    query_bias_ref,
    value_bias_ref,
    picks_ref,
    in_ref,
    cot_ref,
    out_ref,
    grad_ref,
    gout_half,
    gout_wide,
    vout_ref,
    pack_ref,
    vec_ref,
    mask_ref,
    half,
    wide,
    vec_z,
    vec_y,
    vec_all,
    masks,
    tokens,
    tokens_turned,
    cots,
    w_in,
    w_out,
    bias_q,
    bias_k,
    heads,
    keys_turned,
    mixed,
    lse,
    centre,
    first_low,
    first_turned,
    feed_low,
    branch_low,
    hat_first,
    fac_first,
    back_rows,
    active,
    slope,
    inner_buf,
    send_buf,
    recv_buf,
    mixed_back,
    key_sum,
    value_sum,
    heads_back,
    out_grad,
    diag_x,
    diag_y,
    near_x,
    near_y,
    near_z,
    deep_z,
    total,
    swap_out,
    vgrad,
    vsend,
    vrecv,
    send_sem,
    recv_sem,
):
    dp, tensor = lax.axis_index("dp"), lax.axis_index("tensor")
    z, y = dp // 2, dp % 2
    a, b = tensor // 2, tensor % 2
    core_dev = (dp, tensor + 1 - 2 * b)
    x_dev = (dp, tensor + 2 - 4 * a)
    y_dev = (dp + 1 - 2 * y, tensor)

    def z_at(shift):
        return (z + shift) % 4

    def z_dev(shift):
        return (z_at(shift) * 2 + y, tensor)

    barrier = pltpu.get_barrier_semaphore()
    for dev in (core_dev, x_dev, y_dev, z_dev(1), z_dev(2), z_dev(3)):
        pl.semaphore_signal(barrier, inc=1, device_id=dev, device_id_type=MESH)
    pl.semaphore_wait(barrier, 6)

    def copy(index, src, dst, dev):
        return pltpu.make_async_remote_copy(
            src_ref=src,
            dst_ref=dst,
            send_sem=send_sem.at[index],
            recv_sem=recv_sem.at[index],
            device_id=dev,
            device_id_type=MESH,
        )

    def send(index, src, dst, dev):
        copy(index, src, dst, dev).start()

    def arrived(index, region):
        copy(index, region, region, core_dev).wait_recv()

    def left(index, region):
        copy(index, region, region, core_dev).wait_send()

    def store(pack):
        return (half, wide)[pack // 2], pack % 2

    def chip_rows(chip, start=0, size=96):
        first = pl.multiple_of(chip * 96, 16) + start
        return pl.ds(pl.multiple_of(first, 16), size)

    def piece(side, pack, chip, start=0, size=96):
        ref, slot = store(pack)
        return ref.at[side, slot, chip_rows(chip, start, size), :]

    def back_store(pack):
        if pack == 2:
            return wide, 0, slice(0, 768)
        if pack > 2:
            return half, pack - 3, slice(0, 384)
        return wide, 1, slice(384 * pack, 384 * pack + 384)

    def back_piece(side, pack, chip, start=0, size=96):
        ref, slot, cols = back_store(pack)
        return ref.at[side, slot, chip_rows(chip, start, size), cols]

    def part_of(refs, pack):
        return refs[1].at[0] if pack == 2 else refs[0].at[(0, 1, None, 2, 3)[pack]]

    def gather_id(pack, kind, j):
        return pack * 28 + 4 * kind + j

    def scatter_id(pack, kind, i):
        return 112 + pack * 24 + 4 * kind + i

    M_IN, M_COT, M_MASK, M_VZ, M_VY, M_VX = 232, 233, 234, 235, 238, 239
    M_TOK, M_OUT, M_GRAD, M_VG = 240, 242, 243, 244
    M_ROWS, M_PART = 250, 256
    Z_OWN, X_NEAR, Y_NEAR, X_CORNER, Y_CORNER, Z_X, Z_Y = range(7)

    def corner_id(pack, j):
        return gather_id(pack, (Z_OWN, Z_X, Z_Y)[j - 1], 0)

    D_X, D_Y, N_X, N_Y, L_Z, Q_Z = range(6)

    def gather_start(pack):
        own = (pack_ref.at[0], pack_ref.at[1], up_ref, down_ref)[pack]
        for j in (1, 3, 2):
            send(gather_id(pack, Z_OWN, j), own, piece(a, pack, dp), z_dev(j))
        send(gather_id(pack, X_NEAR, 0), own, piece(a, pack, dp), x_dev)
        send(gather_id(pack, Y_NEAR, 0), own, piece(a, pack, dp), y_dev)
        ref, slot = store(pack)
        ref[a, slot, chip_rows(dp), :] = own[...]

    def gather_spread(pack, j):
        chip = z_at(-j) * 2 + y
        arrived(gather_id(pack, Z_OWN, j), piece(a, pack, chip))
        spot = piece(a, pack, chip, LEAN, 96 - LEAN)
        send(gather_id(pack, X_NEAR, j), spot, spot, x_dev)
        send(gather_id(pack, Y_NEAR, j), spot, spot, y_dev)

    def gather_over_y(pack, j):
        first = 0 if j == 0 else LEAN
        chip = z_at(-j) * 2 + 1 - y
        arrived(gather_id(pack, Y_NEAR, j), piece(a, pack, chip, first, 96 - first))
        spot = piece(a, pack, chip, first, TURN - first)
        send(gather_id(pack, X_CORNER, j), spot, spot, x_dev)
        if j == 0:
            for step in (1, 3, 2):
                spot = piece(a, pack, chip, 0, LEAN)
                send(gather_id(pack, Z_Y, step), spot, spot, z_dev(step))

    def gather_over_x(pack, j):
        first = 0 if j == 0 else LEAN
        chip = z_at(-j) * 2 + y
        arrived(gather_id(pack, X_NEAR, j), piece(1 - a, pack, chip, first, 96 - first))
        spot = piece(1 - a, pack, chip, TURN, 96 - TURN)
        send(gather_id(pack, Y_CORNER, j), spot, spot, y_dev)
        if j == 0:
            for step in (1, 3, 2):
                spot = piece(1 - a, pack, chip, 0, LEAN)
                send(gather_id(pack, Z_X, step), spot, spot, z_dev(step))

    def gather_deep(pack, _):
        chip = z * 2 + 1 - y
        arrived(gather_id(pack, X_CORNER, 0), piece(1 - a, pack, chip, 0, TURN))
        spot = piece(1 - a, pack, chip, 0, LEAN)
        for step in (1, 3, 2):
            send(corner_id(pack, step), spot, spot, z_dev(step))

    def gather_end(pack):
        for j in range(4):
            over_y, over_x = z_at(-j) * 2 + 1 - y, z_at(-j) * 2 + y
            arrived(gather_id(pack, Y_CORNER, j), piece(1 - a, pack, over_y, TURN, 96 - TURN))
            if j > 0:
                arrived(gather_id(pack, X_CORNER, j), piece(1 - a, pack, over_y, LEAN, TURN - LEAN))
                arrived(gather_id(pack, Z_Y, j), piece(a, pack, over_y, 0, LEAN))
                arrived(gather_id(pack, Z_X, j), piece(1 - a, pack, over_x, 0, LEAN))
                arrived(corner_id(pack, j), piece(1 - a, pack, over_y, 0, LEAN))

    def gather_left(pack):
        def rows(size):
            return piece(a, pack, dp, 0, size)

        for j in range(4):
            first = 0 if j == 0 else LEAN
            left(gather_id(pack, X_NEAR, j), rows(96 - first))
            left(gather_id(pack, Y_NEAR, j), rows(96 - first))
            left(gather_id(pack, X_CORNER, j), rows(TURN - first))
            left(gather_id(pack, Y_CORNER, j), rows(96 - TURN))
            if j > 0:
                left(gather_id(pack, Z_OWN, j), rows(96))
                left(gather_id(pack, Z_Y, j), rows(LEAN))
                left(gather_id(pack, Z_X, j), rows(LEAN))
                left(corner_id(pack, j), rows(LEAN))

    def add_to(side, pack, chip, start, *blocks):
        ref, slot, cols = back_store(pack)
        rows = chip_rows(chip, start, blocks[0].shape[0])
        summed = ref[side, slot, rows, cols].astype(F32)
        for block in blocks:
            summed = summed + block.astype(F32)
        ref[side, slot, rows, cols] = summed.astype(BF16)

    def scatter_corner(pack, i):
        first = 0 if i == 0 else LEAN
        chip = z_at(i) * 2 + 1 - y
        over_x = part_of(diag_x, pack).at[i, pl.ds(0, BEND - first), :]
        send(scatter_id(pack, D_X, i), back_piece(1 - a, pack, chip, first, BEND - first), over_x, x_dev)
        over_y = part_of(diag_y, pack).at[i]
        send(scatter_id(pack, D_Y, i), back_piece(1 - a, pack, chip, BEND, 96 - BEND), over_y, y_dev)

    def scatter_first(pack):
        for i in (2, 1, 3):
            scatter_corner(pack, i)

    def scatter_start(pack):
        for i in (2, 1, 3):
            for side in range(2):
                for line in range(2):
                    spot = back_piece(side, pack, z_at(i) * 2 + line, 0, LEAN)
                    slot = part_of(deep_z, pack).at[i - 1, 2 * side + line]
                    send(scatter_id(pack, Q_Z, i), spot, slot, z_dev(i))

    def scatter_deep(pack, _):
        parts = part_of(deep_z, pack)
        for i in range(1, 4):
            arrived(scatter_id(pack, Q_Z, i), parts.at[i - 1])
        for side in range(2):
            for line in range(2):
                terms = [parts[i, 2 * side + line] for i in range(3)]
                add_to(side, pack, z * 2 + line, 0, *terms)
        scatter_corner(pack, 0)

    def scatter_near_y(pack, i):
        first = 0 if i == 0 else LEAN
        chip = z_at(i) * 2 + 1 - y
        over_x = part_of(diag_x, pack).at[i, pl.ds(0, BEND - first), :]
        arrived(scatter_id(pack, D_X, i), over_x)
        add_to(a, pack, chip, first, over_x[...])
        spot = back_piece(a, pack, chip, first, 96 - first)
        goal = part_of(near_y, pack).at[i, pl.ds(0, 96 - first), :]
        send(scatter_id(pack, N_Y, i), spot, goal, y_dev)

    def scatter_near_x(pack, i):
        first = 0 if i == 0 else LEAN
        chip = z_at(i) * 2 + y
        over_y = part_of(diag_y, pack).at[i]
        arrived(scatter_id(pack, D_Y, i), over_y)
        add_to(1 - a, pack, chip, BEND, over_y[...])
        spot = back_piece(1 - a, pack, chip, first, 96 - first)
        goal = part_of(near_x, pack).at[i, pl.ds(0, 96 - first), :]
        send(scatter_id(pack, N_X, i), spot, goal, x_dev)

    def scatter_line(pack, i):
        first = 0 if i == 0 else LEAN
        size = 96 - first
        from_x = part_of(near_x, pack).at[i, pl.ds(0, size), :]
        from_y = part_of(near_y, pack).at[i, pl.ds(0, size), :]
        arrived(scatter_id(pack, N_X, i), from_x)
        arrived(scatter_id(pack, N_Y, i), from_y)
        chip = z_at(i) * 2 + y
        ref, slot, cols = back_store(pack)
        rows = chip_rows(chip, first, size)
        own = ref[a, slot, rows, cols].astype(F32) + from_x[...].astype(F32) + from_y[...].astype(F32)
        if i == 0:
            part_of(total, pack)[...] = own
        else:
            ref[a, slot, rows, cols] = own.astype(BF16)
            spot = back_piece(a, pack, chip, first, size)
            send(scatter_id(pack, L_Z, i), spot, part_of(near_z, pack).at[i - 1], z_dev(i))

    def scatter_end(pack):
        parts, sums = part_of(near_z, pack), part_of(total, pack)
        for i in range(1, 4):
            arrived(scatter_id(pack, L_Z, i), parts.at[i - 1])
        goal = part_of((gout_half, gout_wide), pack)
        goal[0:LEAN, :] = sums[0:LEAN, :]
        own = sums[LEAN:96, :]
        for i in range(3):
            own = own + parts[i].astype(F32)
        goal[LEAN:96, :] = own

    def scatter_left(pack):
        def rows(size):
            return back_piece(a, pack, dp, 0, size)

        for i in range(4):
            first = 0 if i == 0 else LEAN
            left(scatter_id(pack, D_X, i), rows(BEND - first))
            left(scatter_id(pack, D_Y, i), rows(96 - BEND))
            left(scatter_id(pack, N_X, i), rows(96 - first))
            left(scatter_id(pack, N_Y, i), rows(96 - first))
            if i > 0:
                left(scatter_id(pack, L_Z, i), rows(96 - LEAN))
                left(scatter_id(pack, Q_Z, i), rows(4 * LEAN))

    def send_cot(pack, _):
        send(M_COT, cot_ref.at[1 - a], cots.at[a], x_dev)

    moves = (
        lambda pack, _: gather_start(pack),
        gather_spread,
        gather_over_y,
        gather_over_x,
        gather_deep,
        scatter_deep,
        scatter_near_y,
        scatter_near_x,
        scatter_line,
        send_cot,
    )

    def run(label):
        for kind, pack, place in PLAN.get(label, ()):
            moves[kind](pack, place)

    def run_at(step, prefix, count):
        for index in range(count):
            if PLAN.get(prefix + str(index)):
                pl.when(step == index)(lambda: run(prefix + str(index)))

    def turned(ref):
        block = ref[...].astype(F32)
        gap = jnp.zeros((block.shape[0], 128 - block.shape[1]), F32)
        return jnp.concatenate((block, gap), 1).T[: block.shape[1], :].astype(BF16)

    def placed(rows, width):
        gap = jnp.zeros((rows.shape[0], width - rows.shape[1]), F32)
        return pltpu.roll(jnp.concatenate((rows, gap), 1), dp * rows.shape[1], 1)

    project = turned(project_ref)
    pack_ref[0] = jnp.concatenate((query_ref[:, :128], key_ref[:, :128], value_ref[:, :128]), 1)
    pack_ref[1] = jnp.concatenate(
        (
            query_ref[:, 128:],
            key_ref[:, 128:],
            value_ref[:, 128:],
            project[:, 128:],
            project[:, :128],
        ),
        1,
    )
    rows = jnp.concatenate([ref[...].reshape(1, 96).astype(F32) for ref in row_refs], 0)
    query_row = placed(query_bias_ref[...].reshape(1, 24).astype(F32), 256)
    value_row = placed(value_bias_ref[...].reshape(1, 24).astype(F32), 256)
    gap = jnp.zeros((1, 128), F32)
    in_row = jnp.concatenate(
        (query_row[:, :128], gap, value_row[:, :128], query_row[:, 128:], value_row[:, 128:], gap), 1
    )
    vec_ref[...] = jnp.concatenate((placed(rows, 768), in_row, jnp.zeros((8, 768), F32)), 0).astype(
        BF16
    )
    column = lax.broadcasted_iota(jnp.int32, (16, 128), 1)
    row = lax.broadcasted_iota(jnp.int32, (16, 128), 0)
    fixed = (
        ((column - row <= 1) & (row - column <= 1))
        | (column == 0)
        | (column == 15)
        | (row == 0)
        | (row == 15)
    )
    for head in range(3):
        allowed = fixed
        for pick in range(picks_ref.shape[1]):
            picks = picks_ref[head, pick : pick + 1, :]
            picks = jnp.concatenate((picks, jnp.full((1, 112), -1, jnp.int32)), 1)
            allowed = allowed | (picks == row)
        mask_ref[16 * head : 16 * head + 16, :] = jnp.where(allowed, 1.0, 0.0).astype(BF16)
    send(M_MASK, mask_ref, masks.at[a], x_dev)
    send(M_IN, in_ref.at[1 - a], tokens.at[tensor], x_dev)
    for j in range(1, 4):
        send(M_VZ + j - 1, vec_ref, vec_z.at[j - 1], z_dev(j))
    gather_start(0)
    tokens[tensor] = in_ref[a]
    masks[a] = mask_ref[...]
    cots[a] = cot_ref[a]
    send(M_TOK, tokens.at[tensor], tokens.at[tensor], core_dev)
    vec_own = vec_ref[...].astype(F32)
    for j in range(1, 4):
        arrived(M_VZ + j - 1, vec_z.at[j - 1])
        vec_own = vec_own + vec_z[j - 1].astype(F32)
    vec_y[0] = vec_own.astype(BF16)
    send(M_VY, vec_y.at[0], vec_y.at[1], y_dev)
    arrived(M_MASK, masks.at[1 - a])
    spread = (
        lax.broadcasted_iota(jnp.int32, (128, 16 * BLOCK), 1) // BLOCK
        == lax.broadcasted_iota(jnp.int32, (128, 16 * BLOCK), 0)
    )
    spread = jnp.where(spread, 1.0, 0.0).astype(BF16)
    for side in range(2):
        bias = (dims(masks[side], spread, 1, 0) - 1.0) * 1e9
        for head in range(3):
            pair, place = (side, head) if head < 2 else (2, side)
            bias_k[pair, place] = bias[16 * head : 16 * head + 16]
            rows = masks[side, 16 * head : 16 * head + 16, :]
            turned_bias = (dims(rows, spread[:16], 0, 0) - 1.0) * 1e9
            for part in range(4):
                bias_q[pair, place, part] = turned_bias[4 * part : 4 * part + 4]
    run("pre")
    arrived(M_VY, vec_y.at[1])
    vec_all[a] = (vec_own + vec_y[1].astype(F32)).astype(BF16)
    send(M_VX, vec_all.at[a], vec_all.at[a], x_dev)
    other = (tensor + 2) % 4
    arrived(M_IN, tokens.at[other])
    send(M_TOK + 1, tokens.at[other], tokens.at[other], core_dev)
    run("tok")

    def vector(row):
        return vec_all[0, row : row + 1, :].astype(F32)

    def turn_rows(goal, ref, quarter):
        cols = pl.ds(pl.multiple_of(quarter * TILE, TILE), TILE)
        goal[:, cols] = ref[quarter].astype(F32).T.astype(BF16)

    arrived(M_TOK, tokens.at[0])
    arrived(M_TOK + 1, tokens.at[0])

    @pl.loop(0, 4)
    def _(quarter):
        turn_rows(tokens_turned, tokens, quarter)

    def project_heads(pair, bias):
        @pl.loop(0, 4)
        def _(quarter):
            rows = pl.ds(pl.multiple_of(quarter * TILE, TILE), TILE)
            block = dims(tokens[quarter], w_in[pair], 1, 0) + bias
            for kind in range(3):
                tile = block[:, 128 * kind : 128 * kind + 128]
                heads[3 * kind + pair, rows, :] = tile.astype(BF16)
                if kind == 1:
                    keys_turned[pair, :, rows] = tile.T.astype(BF16)

    run("p0")
    gather_end(0)
    arrived(M_VX, vec_all.at[1 - a])
    for side in range(2):
        w_in[side] = half[side, 0]
        project_heads(side, vec_all[side, 7:8, 0:384].astype(F32))
        run("q" + str(side))

    def third_heads():
        run("p1")
        gather_end(1)

        @pl.loop(0, 3)
        def _(part):
            rows = pl.ds(pl.multiple_of(part * TILE, TILE), TILE)
            third, out = pairs_of(half[0, 1, rows, :], half[1, 1, rows, :])
            w_in[2, rows, :] = third
            w_out[rows, :] = out

        vecs = [vec_all[side, :, 384:768].astype(F32) for side in range(2)]
        project_heads(2, pairs_of(vecs[0], vecs[1])[0][7:8])

    low = low_lanes((TILE, 128))
    none = jnp.zeros((TILE, 128), BF16)
    top = lax.broadcasted_iota(jnp.int32, (128, TILE), 0) < HEAD_DIM

    def of_head(block, head):
        return jnp.where(low, block, none) if head == 0 else jnp.where(low, none, block)

    @pl.loop(0, 12)
    def _(step):
        pl.when(step == 8)(third_heads)
        pair, part = step // 4, step % 4
        cols = pl.ds(pl.multiple_of(part * TILE, TILE), TILE)
        query_block = heads[pair, cols, :]
        terms, sums, mosts = [], [], []
        for head in range(2):
            scores = dims(of_head(query_block, head), heads[3 + pair], 1, 1).reshape(4, BLOCK, 1024)
            bias = bias_q[pair, head, part].reshape(4, 1, 1024)
            scores = (scores * (SCORE_SCALE * LOG2E) + bias).reshape(TILE, 1024)
            most = jnp.max(scores, axis=1, keepdims=True)
            term = jnp.exp2(scores - most)
            sums.append(jnp.sum(term, axis=1, keepdims=True))
            terms.append(term.astype(BF16))
            mosts.append(most)
        both = dims(jnp.concatenate(terms, 0), heads[6 + pair], 1, 0)
        mixed[pair, cols, :] = jnp.where(low, both[:TILE] / sums[0], both[TILE:] / sums[1]).astype(BF16)
        totals = [most + jnp.log2(total) for most, total in zip(mosts, sums)]
        turned_totals = jnp.where(low, totals[0], totals[1]).T
        lse[pair, 0, :, cols] = turned_totals[0:1]
        lse[pair, 1, :, cols] = turned_totals[HEAD_DIM : HEAD_DIM + 1]
        run_at(step, "f", 12)

    def beside(ref, indices, quarter):
        rows = pl.ds(pl.multiple_of(quarter * TILE, TILE), TILE)
        return jnp.concatenate([ref[index, rows, :] for index in indices], 1)

    def give(number, slot, block):
        send_buf[number % 2, slot] = block.astype(BF16)
        index = M_PART + 2 * number + slot
        send(index, send_buf.at[number % 2, slot], recv_buf.at[number % 2, slot], core_dev)

    def take(number, slot):
        arrived(M_PART + 2 * number + slot, recv_buf.at[number % 2, slot])
        return recv_buf[number % 2, slot].astype(F32)

    def given(number):
        for slot in range(2):
            left(M_PART + 2 * number + slot, send_buf.at[number % 2, slot])

    def share(kind, slot, ref):
        spot = ref.at[2 * slot + b]
        send(M_ROWS + 2 * kind + slot, spot, spot, core_dev)

    def shared(kind, slot, ref):
        arrived(M_ROWS + 2 * kind + slot, ref.at[2 * slot + 1 - b])

    def branch_part(quarter):
        return dims(beside(mixed, range(3), quarter), w_out[...], 1, 1)

    @pl.loop(0, 2)
    def _(slot):
        give(0, slot, branch_part(2 * slot + 1 - b))

    run("b0")

    @pl.loop(0, 2)
    def _(slot):
        quarter = 2 * slot + b
        own = branch_part(quarter)
        hidden = tokens[quarter].astype(F32) + own + take(0, slot) + vector(0)
        normed, factor = norm_of(hidden)
        hat_first[slot] = normed
        fac_first[slot] = factor
        first_low[quarter] = (normed * vector(1) + vector(2)).astype(BF16)
        share(0, slot, first_low)

    run("b1")
    for slot in range(2):
        turn_rows(first_turned, first_low, 2 * slot + b)
    run("b2")
    gather_end(2)

    def feed_up(quarter):
        @pl.loop(0, 2)
        def _(side):
            inner_buf[...] = (
                dims(first_low[quarter], wide[side, 0], 1, 0)
                + vec_all[side, 6:7, :].astype(F32)
            )

            @pl.loop(0, TILE // 32)
            def _(chunk):
                rows = pl.ds(pl.multiple_of(chunk * 32, 32), 32)
                inner = inner_buf[rows, :]
                normal = 0.5 * (1.0 + lax.erf(inner * 0.7071067811865476))
                density = jnp.exp2(inner * inner * (-0.5 * LOG2E)) * 0.3989422804014327
                active[side, quarter, rows, :] = (inner * normal).astype(BF16)
                slope[side, quarter, rows, :] = (normal + inner * density).astype(BF16)

    def feed_down(quarter):
        return dims(active[0, quarter], wide[0, 1], 1, 1) + dims(active[1, quarter], wide[1, 1], 1, 1)

    feed_up(b)
    run("u0")
    feed_up(2 + b)
    run("u1")
    for slot in range(2):
        shared(0, slot, first_low)
        feed_up(2 * slot + 1 - b)
        run("u" + str(2 + slot))
    gather_end(3)

    @pl.loop(0, 2)
    def _(slot):
        give(1, slot, feed_down(2 * slot + 1 - b))

    arrived(M_COT, cots.at[1 - a])
    vgrad[...] = jnp.zeros_like(vgrad)

    @pl.loop(0, 2)
    def _(slot):
        quarter = 2 * slot + b
        own = feed_down(quarter)
        second_in = hat_first[slot] * vector(1) + vector(2) + own + take(1, slot) + vector(3)
        normed, factor = norm_of(second_in)
        swap_out[slot] = (normed * vector(4) + vector(5)).astype(BF16)
        upstream = cots[slot].astype(F32)
        back = norm_pull(upstream, normed, factor, vector(4))
        back_rows[slot] = back
        feed_low[quarter] = back.astype(BF16)
        share(1, slot, feed_low)
        vgrad[0:1, :] += row_sum(upstream * normed)
        vgrad[1:2, :] += row_sum(upstream)
        vgrad[2:3, :] += row_sum(back)

    out_ref[a] = swap_out[a]
    send(M_OUT, swap_out.at[1 - a], out_ref.at[a], x_dev)
    for pack in range(4):
        gather_left(pack)

    def feed_back(quarter):
        for side in range(2):
            block = dims(feed_low[quarter], wide[side, 1], 1, 0) * slope[side, quarter].astype(F32)
            inner_low = block.astype(BF16)
            slope[side, quarter] = inner_low
            vgrad[6 + side : 7 + side, :] += row_sum(inner_low.astype(F32))

    def rest_back(quarter):
        return dims(slope[0, quarter], wide[0, 0], 1, 1) + dims(slope[1, quarter], wide[1, 0], 1, 1)

    def tall(ref, cols):
        return ref[:, :, cols].reshape(4 * TILE, TILE)

    sides = (1 - a, a)

    def down_grad(side, part):
        @pl.loop(0, 3)
        def _(piece_rows):
            rows = pl.ds(pl.multiple_of(piece_rows * TILE, TILE), TILE)
            right = active[side, :, :, 384 * part : 384 * part + 384].reshape(4 * TILE, 384)
            half[side, part, rows, :] = dims(tall(feed_low, rows), right, 0, 0).astype(BF16)


    @pl.loop(0, 2)
    def _(slot):
        feed_back(2 * slot + b)

    for slot in range(2):
        shared(1, slot, feed_low)
    for part in range(2):
        down_grad(sides[0], part)
        scatter_first(3 + part)
        down_grad(sides[1], part)
        scatter_start(3 + part)

    @pl.loop(0, 2)
    def _(slot):
        feed_back(2 * slot + 1 - b)

    given(0)

    @pl.loop(0, 2)
    def _(slot):
        give(2, slot, rest_back(2 * slot + 1 - b))

    for slot in range(2):
        turn_rows(first_turned, first_low, 2 * slot + 1 - b)
    run("r0")

    @pl.loop(0, 2)
    def _(slot):
        quarter = 2 * slot + b
        own = rest_back(quarter)
        upstream = back_rows[slot] + own + take(2, slot)
        normed = hat_first[slot]
        back = norm_pull(upstream, normed, fac_first[slot], vector(1))
        back_rows[slot] = back
        branch_low[quarter] = back.astype(BF16)
        share(2, slot, branch_low)
        vgrad[3:4, :] += row_sum(upstream * normed)
        vgrad[4:5, :] += row_sum(upstream)
        vgrad[5:6, :] += row_sum(back)

    run("r1")
    for side in sides:
        @pl.loop(0, 3)
        def _(part):
            rows = pl.ds(pl.multiple_of(part * TILE, TILE), TILE)
            right = slope[side].reshape(4 * TILE, 768)
            wide[side, 0, rows, :] = dims(first_turned[rows, :], right, 1, 0).astype(BF16)
        if side is sides[0]:
            scatter_first(2)
    scatter_start(2)
    run("r2")

    for slot in range(2):
        shared(2, slot, branch_low)

    @pl.loop(0, 4)
    def _(quarter):
        rows = pl.ds(pl.multiple_of(quarter * TILE, TILE), TILE)
        block = dims(branch_low[quarter], w_out[...], 1, 0).astype(BF16)
        for pair in range(3):
            mixed_back[pair, rows, :] = block[:, 128 * pair : 128 * pair + 128]

    run("r3")

    @pl.loop(0, 3)
    def _(part):
        rows = pl.ds(pl.multiple_of(part * TILE, TILE), TILE)
        right = jnp.concatenate([mixed[pair] for pair in range(3)], 1)
        out_grad[rows, :] = dims(tall(branch_low, rows), right, 0, 0).astype(BF16)
    run("r4")

    def heads_grad(pair, rows):
        right = jnp.concatenate([heads_back[3 * kind + pair] for kind in range(3)], 1)
        return dims(tokens_turned[rows, :], right, 1, 0)

    def first_heads_grad(side):
        @pl.loop(0, 3)
        def _(part):
            rows = pl.ds(pl.multiple_of(part * TILE, TILE), TILE)
            wide[side, 1, rows, 0:384] = heads_grad(side, rows).astype(BF16)

    @pl.loop(0, 12)
    def _(step):
        pair, part = step // 4, step % 4

        @pl.when(part == 0)
        def _():
            pick = (
                lax.broadcasted_iota(jnp.int32, (8, 128), 1) // HEAD_DIM
                == lax.broadcasted_iota(jnp.int32, (8, 128), 0)
            )
            pick = jnp.where(pick, 1.0, 0.0).astype(BF16)
            product = mixed[pair].astype(F32) * mixed_back[pair].astype(F32)
            high = product.astype(BF16)
            rest = (product - high.astype(F32)).astype(BF16)
            centre[...] = dims(pick, high, 1, 1) + dims(pick, rest, 1, 1)
            key_sum[...] = jnp.zeros_like(key_sum)
            value_sum[...] = jnp.zeros_like(value_sum)

        cols = pl.ds(pl.multiple_of(part * TILE, TILE), TILE)
        query_block, back_block = heads[pair, cols, :], mixed_back[pair, cols, :]
        value_block = heads[6 + pair]
        weights, score_backs, queries, backs, query_back = [], [], [], [], []
        for head in range(2):
            query_head, back_head = of_head(query_block, head), of_head(back_block, head)
            bias = bias_k[pair, head, :, cols] - lse[pair, head, :, cols]
            scores = dims(heads[3 + pair], query_head, 1, 1).reshape(16, BLOCK, TILE)
            scores = scores * (SCORE_SCALE * LOG2E) + bias.reshape(16, 1, TILE)
            weight = jnp.exp2(scores.reshape(1024, TILE))
            weight_back = dims(value_block, back_head, 1, 1)
            score_back = (weight * (weight_back - centre[head : head + 1, cols])).astype(BF16)
            weights.append(weight.astype(BF16))
            score_backs.append(score_back)
            queries.append(query_head)
            backs.append(back_head)
            query_back.append(dims(keys_turned[pair], score_back, 1, 0))
        value_sum[...] += dims(jnp.concatenate(weights, 1), jnp.concatenate(backs, 0), 1, 0)
        key_sum[...] += dims(jnp.concatenate(score_backs, 1), jnp.concatenate(queries, 0), 1, 0)
        query_grad = jnp.where(top, query_back[0], query_back[1]).T * SCORE_SCALE
        heads_back[pair, cols, :] = query_grad.astype(BF16)

        @pl.when(part == 3)
        def _():
            heads_back[3 + pair] = (key_sum[...] * SCORE_SCALE).astype(BF16)
            heads_back[6 + pair] = value_sum[...].astype(BF16)

        @pl.when(step == 7)
        def _():
            for side in range(2):
                first_heads_grad(side)
            scatter_first(0)
            scatter_start(0)

        run_at(step, "k", 12)

    @pl.loop(0, 3)
    def _(part):
        rows = pl.ds(pl.multiple_of(part * TILE, TILE), TILE)
        first, second = packs_of(heads_grad(2, rows), out_grad[rows, :].astype(F32))
        wide[0, 1, rows, 384:768] = first.astype(BF16)
        wide[1, 1, rows, 384:768] = second.astype(BF16)

    scatter_first(1)
    scatter_start(1)
    run("t0")
    for pair in range(3):
        vgrad[8:9, 128 * pair : 128 * pair + 128] = row_sum(heads_back[pair].astype(F32))
        vgrad[8:9, 384 + 128 * pair : 512 + 128 * pair] = row_sum(heads_back[6 + pair].astype(F32))
    send(M_VG, vgrad, vrecv.at[0], core_dev)

    def input_part(quarter):
        return sum(
            dims(beside(heads_back, (pair, 3 + pair, 6 + pair), quarter), w_in[pair], 1, 1)
            for pair in range(3)
        )

    given(1)

    @pl.loop(0, 2)
    def _(slot):
        give(3, slot, input_part(2 * slot + 1 - b))

    run("t1")
    arrived(M_VG, vrecv.at[0])
    mine = lax.broadcasted_iota(jnp.int32, (16, 768), 0) < 6
    vsend[0] = vgrad[...] + jnp.where(mine, vrecv[0], 0.0)
    send(M_VG + 1, vsend.at[0], vrecv.at[1], x_dev)

    @pl.loop(0, 2)
    def _(slot):
        own = input_part(2 * slot + b)
        back_rows[slot] = back_rows[slot] + own + take(3, slot)

    cots[0] = back_rows[1 - a].astype(BF16)
    send(M_GRAD, cots.at[0], cots.at[1], x_dev)
    grad_ref[a] = back_rows[a]
    arrived(M_VG + 1, vrecv.at[1])
    vsend[1] = vsend[0] + vrecv[1]
    send(M_VG + 2, vsend.at[1], vrecv.at[2], y_dev)
    run("t2")
    arrived(M_VG + 2, vrecv.at[2])
    vsend[2] = vsend[1] + vrecv[2]
    for j in range(1, 4):
        send(M_VG + 2 + j, vsend.at[2], vrecv.at[2 + j], z_dev(j))
    for pack in (3, 4, 2, 0):
        scatter_end(pack)
    run("t3")
    every = vsend[2]
    for j in range(1, 4):
        arrived(M_VG + 2 + j, vrecv.at[2 + j])
        every = every + vrecv[2 + j]
    vout_ref[...] = pltpu.roll(every, (8 - dp) % 8 * 96, 1)
    heads_row = every[8:9, :]
    for kind in range(2):
        row = heads_row[:, 384 * kind : 384 * kind + 384]
        low_row = low_lanes((1, 128))
        third = jnp.where(a == 0, row[:, 256:384], half_turn(row[:, 256:384]))
        both = jnp.concatenate(
            (jnp.where(a == 0, row[:, :128], row[:, 128:256]), jnp.where(low_row, third, 0.0)), 1
        )
        vout_ref[8 + kind : 9 + kind, 0:256] = pltpu.roll(both, (256 - dp * 24) % 256, 1)
    vout_ref[6:7, :] = jnp.where(a == 0, vout_ref[6:7, :], vout_ref[7:8, :])
    arrived(M_GRAD, cots.at[1])
    grad_ref[1 - a] = cots[1].astype(F32)
    arrived(M_OUT, out_ref.at[1 - a])
    scatter_end(1)

    for pack in range(5):
        scatter_left(pack)
    given(2)
    given(3)
    left(M_MASK, mask_ref)
    left(M_IN, in_ref.at[0])
    left(M_COT, cot_ref.at[0])
    left(M_OUT, swap_out.at[0])
    left(M_GRAD, cots.at[0])
    for j in range(3):
        left(M_VZ + j, vec_ref)
    left(M_VY, vec_y.at[0])
    left(M_VX, vec_all.at[0])
    for slot in range(2):
        left(M_TOK + slot, tokens.at[0])
        for kind in range(3):
            left(M_ROWS + 2 * kind + slot, first_low.at[0])
    for index in range(6):
        left(M_VG + index, vsend.at[0])


def finish_kernel(
    gout_half,
    gout_wide,
    vout_ref,
    query_ref,
    key_ref,
    value_ref,
    project_ref,
    up_ref,
    down_ref,
    query_bias_ref,
    value_bias_ref,
    *row_refs
):
    first, last = gout_half[0], gout_half[1]
    query_ref[...] = jnp.concatenate((first[:, 0:128], last[:, 0:64]), 1)
    key_ref[...] = jnp.concatenate((first[:, 128:256], last[:, 64:128]), 1)
    value_ref[...] = jnp.concatenate((first[:, 256:384], last[:, 128:192]), 1)
    gap = jnp.zeros((32, 256), F32)
    project = jnp.concatenate((last[:, 256:384], last[:, 128:256]), 1)
    project = jnp.concatenate((project, gap), 0).T
    project_ref[0:128, :] = project[0:128, :96]
    project_ref[128:192, :] = project[192:256, :96]
    up_ref[...] = gout_wide[0]
    down_ref[...] = jnp.concatenate((gout_half[2], gout_half[3]), 1)
    query_bias_ref[...] = vout_ref[8, 0:24]
    value_bias_ref[...] = vout_ref[9, 0:24]
    for row, ref in enumerate(row_refs):
        ref[...] = vout_ref[row, 0:96]


def layer_call(weights, rows, biases, random_blocks, tokens, cotangent):
    vmem = pltpu.VMEM
    anywhere = pl.BlockSpec(memory_space=pltpu.VMEM)
    shape = jax.ShapeDtypeStruct
    def both(*dims_, kind=BF16):
        return (vmem((4,) + dims_ + (384,), kind), vmem((1,) + dims_ + (768,), kind))

    scratch = [
        vmem((2, 96, 384), BF16),
        vmem((16, 768), BF16),
        vmem((48, 128), BF16),
        vmem((2, 2, 768, 384), BF16),
        vmem((2, 2, 768, 768), BF16),
        vmem((3, 16, 768), BF16),
        vmem((2, 16, 768), BF16),
        vmem((2, 16, 768), BF16),
        vmem((2, 48, 128), BF16),
        vmem((4, TILE, 768), BF16),
        vmem((768, 4 * TILE), BF16),
        vmem((2, TILE, 768), BF16),
        vmem((3, 768, 384), BF16),
        vmem((768, 384), BF16),
        vmem((3, 2, 4, 4, 1024), F32),
        vmem((3, 2, 16, 1024), F32),
        vmem((9, 1024, 128), BF16),
        vmem((3, 128, 1024), BF16),
        vmem((3, 1024, 128), BF16),
        vmem((3, 2, 1, 1024), F32),
        vmem((8, 1024), F32),
        vmem((4, TILE, 768), BF16),
        vmem((768, 4 * TILE), BF16),
        vmem((4, TILE, 768), BF16),
        vmem((4, TILE, 768), BF16),
        vmem((2, TILE, 768), F32),
        vmem((2, TILE, 1), F32),
        vmem((2, TILE, 768), F32),
        vmem((2, 4, TILE, 768), BF16),
        vmem((2, 4, TILE, 768), BF16),
        vmem((TILE, 768), F32),
        vmem((2, 2, TILE, 768), BF16),
        vmem((2, 2, TILE, 768), BF16),
        vmem((3, 1024, 128), BF16),
        vmem((1024, 128), F32),
        vmem((1024, 128), F32),
        vmem((9, 1024, 128), BF16),
        vmem((768, 384), BF16),
        both(4, 48),
        both(4, 48),
        both(4, 96),
        both(4, 96),
        both(3, 96 - LEAN),
        both(3, 4, LEAN),
        both(96, kind=F32),
        vmem((2, TILE, 768), BF16),
        vmem((16, 768), F32),
        vmem((3, 16, 768), F32),
        vmem((6, 16, 768), F32),
        pltpu.SemaphoreType.DMA((MESSAGES,)),
        pltpu.SemaphoreType.DMA((MESSAGES,)),
    ]
    return pl.pallas_call(
        layer_kernel,
        out_shape=(
            shape(tokens.shape, BF16),
            shape(tokens.shape, F32),
            shape((4, 96, 384), F32),
            shape((1, 96, 768), F32),
            shape((16, 768), F32),
        ),
        in_specs=[anywhere] * 6 + [(anywhere,) * 7] + [anywhere] * 5,
        out_specs=(anywhere,) * 5,
        scratch_shapes=scratch,
        compiler_params=pltpu.CompilerParams(
            collective_id=0, has_side_effects=True, vmem_limit_bytes=63 << 20
        ),
    )(*weights, rows, *biases, random_blocks, tokens, cotangent)


def local_fast(
    inputs,
    random_blocks,
    query_weight,
    query_bias,
    key_weight,
    value_weight,
    value_bias,
    out_weight,
    out_bias,
    first_gain,
    first_shift,
    up_weight,
    up_bias,
    down_weight,
    down_bias,
    second_gain,
    second_shift,
    cotangent,
):
    output, input_grad, half_grads, wide_grads, sums = layer_call(
        (query_weight, key_weight, value_weight, down_weight.T, up_weight, out_weight),
        (out_bias, first_gain, first_shift, down_bias, second_gain, second_shift, up_bias),
        (query_bias, value_bias),
        random_blocks.transpose(0, 2, 1),
        inputs,
        cotangent,
    )
    like = lambda array: jax.ShapeDtypeStruct(array.shape, F32)
    whole = pl.BlockSpec(memory_space=pltpu.VMEM)
    outs = (query_weight, key_weight, value_weight, out_weight, up_weight, up_weight)
    outs += (query_bias, value_bias)
    outs += (second_gain, second_shift, down_bias, first_gain, first_shift, out_bias, up_bias)
    done = pl.pallas_call(
        finish_kernel,
        out_shape=tuple(like(array) for array in outs),
        in_specs=[whole] * 3,
        out_specs=(whole,) * len(outs),
    )(half_grads, wide_grads, sums)
    query_grad, key_grad, value_grad, out_grad, up_grad, down_grad = done[:6]
    query_bias_grad, value_bias_grad = done[6:8]
    second_gain_grad, second_shift_grad, down_bias_grad = done[8:11]
    first_gain_grad, first_shift_grad, out_bias_grad, up_bias_grad = done[11:]
    return (
        output,
        input_grad,
        query_grad,
        query_bias_grad,
        key_grad,
        value_grad,
        value_bias_grad,
        out_grad,
        out_bias_grad,
        first_gain_grad,
        first_shift_grad,
        up_grad,
        up_bias_grad,
        down_grad.T,
        down_bias_grad,
        second_gain_grad,
        second_shift_grad,
    )


def solution(mesh):
    sizes = mesh.shape
    fast = sizes["dp"] == 8 and sizes["tensor"] == 4
    return jax.shard_map(
        local_fast if fast else local,
        mesh=mesh,
        in_specs=(
            P("dp", "tensor", None),
            P("tensor", None, None),
            P("dp", "tensor"),
            P(("tensor", "dp")),
            P("dp", "tensor"),
            P("dp", "tensor"),
            P(("tensor", "dp")),
            P("tensor", "dp"),
            P("dp"),
            P("dp"),
            P("dp"),
            P("dp", "tensor"),
            P(("tensor", "dp")),
            P("tensor", "dp"),
            P("dp"),
            P("dp"),
            P("dp"),
            P("dp", "tensor", None),
        ),
        out_specs=(
            P("dp", "tensor", None),
            P("dp", "tensor", None),
            P("dp", "tensor"),
            P(("tensor", "dp")),
            P("dp", "tensor"),
            P("dp", "tensor"),
            P(("tensor", "dp")),
            P("tensor", "dp"),
            P("dp"),
            P("dp"),
            P("dp"),
            P("dp", "tensor"),
            P(("tensor", "dp")),
            P("tensor", "dp"),
            P("dp"),
            P("dp"),
            P("dp"),
        ),
        check_vma=False,
    )
```

```python
from functools import partial

import jax
import jax.numpy as jnp
from jax import lax
from jax.experimental import pallas as pl
from jax.experimental.pallas import tpu as pltpu
from jax.sharding import PartitionSpec as P

HEAD_DIM = 64
BLOCK = 64


norm_eps = 1e-12


def gather_weights(shards):
    return (
        lax.all_gather(shards[0], "dp", axis=0, tiled=True),
        lax.all_gather(shards[1], "dp", axis=0, tiled=True),
        lax.all_gather(shards[2], "dp", axis=0, tiled=True),
        lax.all_gather(shards[3], "dp", axis=0, tiled=True),
        lax.all_gather(shards[4], "dp", axis=0, tiled=True),
        lax.all_gather(shards[5], "dp", axis=1, tiled=True),
        lax.all_gather(shards[6], "dp", axis=0, tiled=True),
        lax.all_gather(shards[7], "dp", axis=0, tiled=True),
        lax.all_gather(shards[8], "dp", axis=0, tiled=True),
        lax.all_gather(shards[9], "dp", axis=0, tiled=True),
        lax.all_gather(shards[10], "dp", axis=0, tiled=True),
        lax.all_gather(shards[11], "dp", axis=1, tiled=True),
        lax.all_gather(shards[12], "dp", axis=0, tiled=True),
        lax.all_gather(shards[13], "dp", axis=0, tiled=True),
        lax.all_gather(shards[14], "dp", axis=0, tiled=True),
    )


def reduce_grads(grads):
    return (
        lax.psum_scatter(grads[0], "dp", scatter_dimension=0, tiled=True),
        lax.psum_scatter(grads[1], "dp", scatter_dimension=0, tiled=True),
        lax.psum_scatter(grads[2], "dp", scatter_dimension=0, tiled=True),
        lax.psum_scatter(grads[3], "dp", scatter_dimension=0, tiled=True),
        lax.psum_scatter(grads[4], "dp", scatter_dimension=0, tiled=True),
        lax.psum_scatter(grads[5], "dp", scatter_dimension=1, tiled=True),
        lax.psum_scatter(grads[6], "dp", scatter_dimension=0, tiled=True),
        lax.psum_scatter(grads[7], "dp", scatter_dimension=0, tiled=True),
        lax.psum_scatter(grads[8], "dp", scatter_dimension=0, tiled=True),
        lax.psum_scatter(grads[9], "dp", scatter_dimension=0, tiled=True),
        lax.psum_scatter(grads[10], "dp", scatter_dimension=0, tiled=True),
        lax.psum_scatter(grads[11], "dp", scatter_dimension=1, tiled=True),
        lax.psum_scatter(grads[12], "dp", scatter_dimension=0, tiled=True),
        lax.psum_scatter(grads[13], "dp", scatter_dimension=0, tiled=True),
        lax.psum_scatter(grads[14], "dp", scatter_dimension=0, tiled=True),
    )


def full_rows(block):
    return lax.all_gather(block, "tensor", axis=0, tiled=True)


def column_sums(partial_terms):
    return lax.psum_scatter(
        partial_terms.astype(jnp.bfloat16), "tensor", scatter_dimension=0, tiled=True
    ).astype(jnp.float32)


def block_allowed(random_blocks, block_count):
    row_ids = jnp.arange(block_count, dtype=jnp.int32)[:, None]
    col_ids = jnp.arange(block_count, dtype=jnp.int32)[None, :]
    fixed = (
        (jnp.abs(row_ids - col_ids) <= 1)
        | (col_ids == 0)
        | (col_ids == block_count - 1)
        | (row_ids == 0)
        | (row_ids == block_count - 1)
    )
    picked = jnp.any(
        random_blocks[:, :, :, None]
        == jnp.arange(block_count, dtype=jnp.int32)[None, None, None, :],
        axis=2,
    )
    return fixed[None, :, :] | picked


def layer_norm(values, gain, shift):
    mean = jnp.mean(values, axis=1, keepdims=True)
    spread = jnp.mean(values * values, axis=1, keepdims=True) - mean * mean
    factor = lax.rsqrt(spread + norm_eps)
    normed = (values - mean) * factor
    return (normed * gain + shift, normed, factor)


def norm_back(upstream, normed, factor, gain):
    scaled = upstream * gain
    plain = jnp.mean(scaled, axis=1, keepdims=True)
    along = jnp.mean(scaled * normed, axis=1, keepdims=True)
    back = factor * (scaled - plain - normed * along)
    return (back, jnp.sum(upstream * normed, axis=0), jnp.sum(upstream, axis=0))


def row_parts(array, span):
    return array.reshape((array.shape[0] // span, span) + array.shape[1:])


def mask_parts(allowed, span):
    return allowed.reshape(allowed.shape[0], -1, span // BLOCK, allowed.shape[2]).transpose(
        1, 0, 2, 3
    )


def block_scores(query_block, key_heads, mask_block):
    products = jnp.einsum(
        "qhd,khd->hqk", query_block, key_heads, preferred_element_type=jnp.float32
    )
    head_count, row_count, key_count = products.shape
    scaled = (products * HEAD_DIM ** (-0.5)).reshape(
        head_count, row_count // BLOCK, BLOCK, key_count // BLOCK, BLOCK
    )
    masked = jnp.where(mask_block[:, :, None, :, None], scaled, -1000000000.0)
    return masked.reshape(head_count, row_count, key_count)


def attend(query_heads, key_heads, value_heads, allowed):
    length = query_heads.shape[0]
    span = min(512, length)

    def one_part(items):
        query_block, mask_block = items
        scores = block_scores(query_block, key_heads, mask_block)
        largest = jnp.max(scores, axis=-1, keepdims=True)
        log_total = largest + jnp.log(jnp.sum(jnp.exp(scores - largest), axis=-1, keepdims=True))
        weights_low = jnp.exp(scores - log_total).astype(jnp.bfloat16)
        mixed = jnp.einsum(
            "hqk,khd->qhd", weights_low, value_heads, preferred_element_type=jnp.float32
        )
        return (mixed, log_total[..., 0])

    mixed, log_totals = lax.map(one_part, (row_parts(query_heads, span), mask_parts(allowed, span)))
    return (mixed.reshape(length, -1).astype(jnp.bfloat16), log_totals)


def attend_back(query_heads, key_heads, value_heads, mixed_back, log_totals, allowed):
    length = query_heads.shape[0]
    span = min(512, length)

    def one_part(carry, items):
        key_sum, value_sum = carry
        query_block, back_block, log_total, mask_block = items
        scores = block_scores(query_block, key_heads, mask_block)
        weights = jnp.exp(scores - log_total[..., None])
        weights_low = weights.astype(jnp.bfloat16)
        weights_back = jnp.einsum(
            "qhd,khd->hqk", back_block, value_heads, preferred_element_type=jnp.float32
        )
        centre = jnp.sum(weights_back * weights, axis=-1, keepdims=True)
        scores_back = (weights * (weights_back - centre) * HEAD_DIM ** (-0.5)).astype(jnp.bfloat16)
        query_back = jnp.einsum(
            "hqk,khd->qhd", scores_back, key_heads, preferred_element_type=jnp.float32
        )
        key_sum = key_sum + jnp.einsum(
            "hqk,qhd->khd", scores_back, query_block, preferred_element_type=jnp.float32
        )
        value_sum = value_sum + jnp.einsum(
            "hqk,qhd->khd", weights_low, back_block, preferred_element_type=jnp.float32
        )
        return ((key_sum, value_sum), query_back)

    empty = jnp.zeros(key_heads.shape, jnp.float32)
    (key_back, value_back), query_back = lax.scan(
        one_part,
        (empty, empty),
        (
            row_parts(query_heads, span),
            row_parts(mixed_back, span),
            log_totals,
            mask_parts(allowed, span),
        ),
    )
    return (
        query_back.reshape(length, -1).astype(jnp.bfloat16),
        key_back.reshape(length, -1).astype(jnp.bfloat16),
        value_back.reshape(length, -1).astype(jnp.bfloat16),
    )


def forward_pass(weights, token_block, allowed):
    (
        query_weight,
        query_bias,
        key_weight,
        value_weight,
        value_bias,
        out_weight,
        out_bias,
        first_gain,
        first_shift,
        up_weight,
        up_bias,
        down_weight,
        down_bias,
        second_gain,
        second_shift,
    ) = weights
    token_rows = full_rows(token_block)
    length = token_rows.shape[0]

    def heads_of(product):
        return product.astype(jnp.bfloat16).reshape(length, -1, HEAD_DIM)

    query_heads = heads_of(
        jnp.dot(token_rows, query_weight, preferred_element_type=jnp.float32) + query_bias
    )
    key_heads = heads_of(jnp.dot(token_rows, key_weight, preferred_element_type=jnp.float32))
    value_heads = heads_of(
        jnp.dot(token_rows, value_weight, preferred_element_type=jnp.float32) + value_bias
    )
    mixed, log_totals = attend(query_heads, key_heads, value_heads, allowed)
    branch_terms = jnp.dot(mixed, out_weight, preferred_element_type=jnp.float32)
    hidden = token_block.astype(jnp.float32) + column_sums(branch_terms) + out_bias
    first_norm, first_normed, first_factor = layer_norm(hidden, first_gain, first_shift)
    first_rows = full_rows(first_norm.astype(jnp.bfloat16))
    inner = jnp.dot(first_rows, up_weight, preferred_element_type=jnp.float32) + up_bias
    active = jax.nn.gelu(inner, approximate=False).astype(jnp.bfloat16)
    second_in = (
        first_norm
        + column_sums(jnp.dot(active, down_weight, preferred_element_type=jnp.float32))
        + down_bias
    )
    result, second_normed, second_factor = layer_norm(second_in, second_gain, second_shift)
    kept = (
        token_rows,
        query_heads,
        key_heads,
        value_heads,
        log_totals,
        mixed,
        first_normed,
        first_factor,
        first_rows,
        inner,
        active,
        second_normed,
        second_factor,
    )
    return (result, kept)


def backward_pass(weights, kept, upstream_block, allowed):
    (
        query_weight,
        query_bias,
        key_weight,
        value_weight,
        value_bias,
        out_weight,
        out_bias,
        first_gain,
        first_shift,
        up_weight,
        up_bias,
        down_weight,
        down_bias,
        second_gain,
        second_shift,
    ) = weights
    (
        token_rows,
        query_heads,
        key_heads,
        value_heads,
        log_totals,
        mixed,
        first_normed,
        first_factor,
        first_rows,
        inner,
        active,
        second_normed,
        second_factor,
    ) = kept
    length = token_rows.shape[0]
    upstream = upstream_block.astype(jnp.float32)
    second_back, second_gain_grad, second_shift_grad = norm_back(
        upstream, second_normed, second_factor, second_gain
    )
    down_bias_grad = jnp.sum(second_back, axis=0)
    feed_rows = full_rows(second_back.astype(jnp.bfloat16))
    down_weight_grad = jnp.einsum(
        "tf,td->fd", active, feed_rows, preferred_element_type=jnp.float32
    )
    active_back = jnp.einsum(
        "td,fd->tf", feed_rows, down_weight, preferred_element_type=jnp.float32
    )
    inner_back = jax.vjp(partial(jax.nn.gelu, approximate=False), inner)[1](active_back)[0].astype(
        jnp.bfloat16
    )
    up_bias_grad = jnp.sum(inner_back, axis=0, dtype=jnp.float32)
    up_weight_grad = jnp.einsum(
        "td,tf->df", first_rows, inner_back, preferred_element_type=jnp.float32
    )
    first_back = second_back + column_sums(
        jnp.einsum("tf,df->td", inner_back, up_weight, preferred_element_type=jnp.float32)
    )
    hidden_back, first_gain_grad, first_shift_grad = norm_back(
        first_back, first_normed, first_factor, first_gain
    )
    out_bias_grad = jnp.sum(hidden_back, axis=0)
    branch_rows = full_rows(hidden_back.astype(jnp.bfloat16))
    out_weight_grad = jnp.einsum(
        "tc,td->cd", mixed, branch_rows, preferred_element_type=jnp.float32
    )
    mixed_back = jnp.einsum(
        "td,cd->tc", branch_rows, out_weight, preferred_element_type=jnp.float32
    ).astype(jnp.bfloat16)
    query_back, key_back, value_back = attend_back(
        query_heads,
        key_heads,
        value_heads,
        mixed_back.reshape(length, -1, HEAD_DIM),
        log_totals,
        allowed,
    )
    query_weight_grad = jnp.einsum(
        "td,tc->dc", token_rows, query_back, preferred_element_type=jnp.float32
    )
    key_weight_grad = jnp.einsum(
        "td,tc->dc", token_rows, key_back, preferred_element_type=jnp.float32
    )
    value_weight_grad = jnp.einsum(
        "td,tc->dc", token_rows, value_back, preferred_element_type=jnp.float32
    )
    query_bias_grad = jnp.sum(query_back, axis=0, dtype=jnp.float32)
    value_bias_grad = jnp.sum(value_back, axis=0, dtype=jnp.float32)
    projected = (
        jnp.einsum("tc,dc->td", query_back, query_weight, preferred_element_type=jnp.float32)
        + jnp.einsum("tc,dc->td", key_back, key_weight, preferred_element_type=jnp.float32)
        + jnp.einsum("tc,dc->td", value_back, value_weight, preferred_element_type=jnp.float32)
    )
    input_back = hidden_back + column_sums(projected)
    grads = (
        query_weight_grad,
        query_bias_grad,
        key_weight_grad,
        value_weight_grad,
        value_bias_grad,
        out_weight_grad,
        out_bias_grad,
        first_gain_grad,
        first_shift_grad,
        up_weight_grad,
        up_bias_grad,
        down_weight_grad,
        down_bias_grad,
        second_gain_grad,
        second_shift_grad,
    )
    return (input_back, grads)


def local(
    inputs,
    random_blocks,
    query_weight,
    query_bias,
    key_weight,
    value_weight,
    value_bias,
    out_weight,
    out_bias,
    first_gain,
    first_shift,
    up_weight,
    up_bias,
    down_weight,
    down_bias,
    second_gain,
    second_shift,
    cotangent,
):
    shards = (
        query_weight,
        query_bias,
        key_weight,
        value_weight,
        value_bias,
        out_weight,
        out_bias,
        first_gain,
        first_shift,
        up_weight,
        up_bias,
        down_weight,
        down_bias,
        second_gain,
        second_shift,
    )
    allowed = block_allowed(random_blocks, random_blocks.shape[1])
    resident = gather_weights(shards)
    growth = lax.axis_size("dp")
    grown_dims = (0, 0, 0, 0, 0, 1, 0, 0, 0, 0, 0, 1, 0, 0, 0)
    start = tuple(
        (
            jnp.zeros(
                tuple(
                    (
                        extent * growth if position == grown_dim else extent
                        for position, extent in enumerate(shard.shape)
                    )
                ),
                jnp.float32,
            )
            for shard, grown_dim in zip(shards, grown_dims)
        )
    )

    def one_sequence(totals, items):
        token_block, upstream_block = items
        result, kept = forward_pass(resident, token_block, allowed)
        input_back, grads = backward_pass(resident, kept, upstream_block, allowed)
        totals = tuple((summed + update for summed, update in zip(totals, grads)))
        return (totals, (result.astype(jnp.bfloat16), input_back))

    totals, (results, input_backs) = lax.scan(one_sequence, start, (inputs, cotangent))
    shares = reduce_grads(totals)
    vectors = lax.psum(
        (shares[6], shares[7], shares[8], shares[12], shares[13], shares[14]), "tensor"
    )
    return (
        results,
        input_backs,
        shares[0],
        shares[1],
        shares[2],
        shares[3],
        shares[4],
        shares[5],
        vectors[0],
        vectors[1],
        vectors[2],
        shares[9],
        shares[10],
        shares[11],
        vectors[3],
        vectors[4],
        vectors[5],
    )


MESH = pl.DeviceIdType.MESH
(
    START,
    SPREAD,
    OVER_Y,
    OVER_X,
    DEEP,
    BACK_DEEP,
    BACK_Y,
    BACK_X,
    BACK_LINE,
    COT,
) = range(10)
PLAN = {
    "pre": (
        (START, 1, 0),
        (OVER_Y, 0, 0),
        (SPREAD, 0, 1),
        (OVER_Y, 1, 0),
        (SPREAD, 0, 2),
    ),
    "tok": (
        (SPREAD, 0, 3),
        (SPREAD, 1, 1),
        (OVER_X, 1, 0),
    ),
    "p0": (
        (OVER_X, 0, 1),
        (SPREAD, 1, 2),
        (OVER_X, 0, 0),
        (DEEP, 0, 0),
        (OVER_Y, 0, 3),
        (OVER_X, 0, 2),
        (OVER_Y, 0, 2),
        (OVER_Y, 0, 1),
        (START, 2, 0),
        (OVER_X, 0, 3),
        (OVER_Y, 1, 2),
        (DEEP, 1, 0),
        (START, 3, 0),
        (OVER_X, 1, 1),
        (OVER_X, 1, 2),
    ),
    "q0": (
        (SPREAD, 1, 3),
        (SPREAD, 2, 1),
    ),
    "q1": (
        (OVER_Y, 2, 0),
        (SPREAD, 2, 3),
        (OVER_X, 1, 3),
        (OVER_Y, 1, 3),
        (DEEP, 2, 0),
        (OVER_Y, 1, 1),
    ),
    "f1": (
        (OVER_X, 2, 0),
        (OVER_X, 2, 1),
        (SPREAD, 2, 2),
    ),
    "f3": (
        (OVER_Y, 2, 1),
        (OVER_X, 2, 3),
    ),
    "f4": (
        (COT, 0, 0),
    ),
    "f7": (
        (OVER_X, 3, 0),
    ),
    "p1": (
        (SPREAD, 3, 1),
    ),
    "f9": (
        (OVER_X, 2, 2),
    ),
    "f10": (
        (OVER_Y, 2, 3),
        (OVER_Y, 3, 0),
        (SPREAD, 3, 3),
    ),
    "f11": (
        (OVER_Y, 2, 2),
        (SPREAD, 3, 2),
    ),
    "b0": (
        (OVER_X, 3, 1),
        (OVER_Y, 3, 1),
    ),
    "b1": (
        (OVER_Y, 3, 3),
    ),
    "u0": (
        (OVER_X, 3, 3),
    ),
    "u1": (
        (OVER_X, 3, 2),
        (DEEP, 3, 0),
        (OVER_Y, 3, 2),
    ),
    "r0": (
        (BACK_X, 3, 2),
        (BACK_Y, 3, 3),
        (BACK_Y, 3, 2),
        (BACK_X, 4, 3),
        (BACK_X, 3, 3),
        (BACK_X, 4, 1),
        (BACK_DEEP, 3, 0),
        (BACK_Y, 4, 3),
        (BACK_X, 3, 1),
        (BACK_Y, 4, 1),
    ),
    "r1": (
        (BACK_LINE, 3, 2),
        (BACK_X, 4, 2),
        (BACK_DEEP, 4, 0),
    ),
    "r2": (
        (BACK_X, 3, 0),
        (BACK_X, 4, 0),
        (BACK_Y, 3, 1),
        (BACK_LINE, 3, 3),
        (BACK_Y, 3, 0),
    ),
    "r3": (
        (BACK_Y, 4, 2),
        (BACK_Y, 4, 0),
    ),
    "k0": (
        (BACK_LINE, 4, 3),
    ),
    "k1": (
        (BACK_X, 2, 2),
        (BACK_X, 2, 3),
    ),
    "k2": (
        (BACK_LINE, 3, 1),
    ),
    "k3": (
        (BACK_LINE, 4, 1),
        (BACK_Y, 2, 2),
        (BACK_LINE, 4, 2),
    ),
    "k4": (
        (BACK_X, 2, 1),
        (BACK_DEEP, 2, 0),
    ),
    "k5": (
        (BACK_Y, 2, 1),
        (BACK_Y, 2, 3),
    ),
    "k7": (
        (BACK_LINE, 2, 2),
        (BACK_Y, 2, 0),
    ),
    "k8": (
        (BACK_Y, 0, 2),
        (BACK_X, 2, 0),
    ),
    "k9": (
        (BACK_Y, 0, 3),
        (BACK_X, 0, 2),
    ),
    "k10": (
        (BACK_X, 0, 1),
    ),
    "k11": (
        (BACK_X, 0, 3),
    ),
    "t0": (
        (BACK_LINE, 3, 0),
        (BACK_LINE, 4, 0),
        (BACK_DEEP, 0, 0),
    ),
    "t1": (
        (BACK_LINE, 0, 2),
        (BACK_LINE, 2, 1),
        (BACK_Y, 0, 1),
        (BACK_LINE, 2, 3),
        (BACK_X, 1, 2),
        (BACK_X, 1, 3),
        (BACK_Y, 1, 1),
        (BACK_X, 0, 0),
        (BACK_X, 1, 1),
        (BACK_LINE, 2, 0),
        (BACK_Y, 1, 3),
    ),
    "t2": (
        (BACK_LINE, 0, 1),
        (BACK_Y, 1, 2),
        (BACK_LINE, 1, 1),
        (BACK_LINE, 0, 3),
        (BACK_Y, 0, 0),
        (BACK_LINE, 1, 2),
        (BACK_LINE, 1, 3),
        (BACK_DEEP, 1, 0),
        (BACK_LINE, 0, 0),
    ),
    "t3": (
        (BACK_X, 1, 0),
        (BACK_Y, 1, 0),
        (BACK_LINE, 1, 0),
    ),
}
F32 = jnp.float32
BF16 = jnp.bfloat16
LOG2E = 1.4426950408889634
SCORE_SCALE = HEAD_DIM ** (-0.5)
TILE = 256
MESSAGES = 272
LEAN = 16
TURN = 32
BEND = 48


def dims(left, right, left_dim, right_dim):
    return lax.dot_general(
        left, right, (((left_dim,), (right_dim,)), ((), ())), preferred_element_type=F32
    )


def low_lanes(shape):
    return lax.broadcasted_iota(jnp.int32, shape, len(shape) - 1) < HEAD_DIM


def half_turn(block):
    return pltpu.roll(block.astype(F32), HEAD_DIM, 1).astype(block.dtype)


def pairs_of(first, second):
    tile = lambda pack, index: pack[:, 128 * index : 128 * index + 128]
    low = low_lanes((first.shape[0], 128))
    e0, e1, f0, f1 = tile(first, 0), tile(second, 0), tile(first, 1), tile(second, 1)
    third = (
        jnp.where(low, e0, half_turn(e1)),
        jnp.where(low, half_turn(e0), e1),
        jnp.where(low, f0, half_turn(f1)),
    )
    out = (tile(first, 2), tile(second, 2), jnp.where(low, half_turn(f0), f1))
    return jnp.concatenate(third, 1), jnp.concatenate(out, 1)


def packs_of(third, out):
    tile = lambda block, index: block[:, 128 * index : 128 * index + 128]
    query, key, value = (tile(third, index) for index in range(3))
    low = low_lanes(query.shape)
    first = (
        jnp.where(low, query, half_turn(key)),
        jnp.where(low, value, half_turn(tile(out, 2))),
        tile(out, 0),
    )
    second = (
        jnp.where(low, half_turn(query), key),
        jnp.where(low, half_turn(value), tile(out, 2)),
        tile(out, 1),
    )
    return jnp.concatenate(first, 1), jnp.concatenate(second, 1)


def norm_of(values):
    mean = jnp.mean(values, axis=1, keepdims=True)
    spread = jnp.mean(values * values, axis=1, keepdims=True) - mean * mean
    factor = lax.rsqrt(spread + norm_eps)
    return (values - mean) * factor, factor


def norm_pull(upstream, normed, factor, gain):
    scaled = upstream * gain
    plain = jnp.mean(scaled, axis=1, keepdims=True)
    along = jnp.mean(scaled * normed, axis=1, keepdims=True)
    return factor * (scaled - plain - normed * along)


def row_sum(block):
    return jnp.sum(block, axis=0, keepdims=True)


def layer_kernel(
    query_far,
    key_far,
    value_far,
    down_far,
    up_far,
    project_far,
    rows_far,
    query_bias_far,
    value_bias_far,
    picks_far,
    in_far,
    cot_far,
    out_ref,
    grad_ref,
    gout_half,
    gout_wide,
    vout_ref,
    query_ref,
    key_ref,
    value_ref,
    down_ref,
    up_ref,
    project_ref,
    row_refs,
    query_bias_ref,
    value_bias_ref,
    picks_ref,
    in_ref,
    cot_ref,
    pack_ref,
    vec_ref,
    mask_ref,
    half,
    wide,
    vec_z,
    vec_y,
    vec_all,
    masks,
    tokens,
    tokens_turned,
    cots,
    w_in,
    w_out,
    bias_q,
    bias_k,
    heads,
    keys_turned,
    mixed,
    lse,
    centre,
    first_low,
    first_turned,
    feed_low,
    branch_low,
    hat_first,
    fac_first,
    back_rows,
    active,
    slope,
    inner_buf,
    send_buf,
    recv_buf,
    mixed_back,
    key_sum,
    value_sum,
    heads_back,
    out_grad,
    diag_x,
    diag_y,
    near_x,
    near_y,
    near_z,
    deep_z,
    total,
    swap_out,
    vgrad,
    vsend,
    vrecv,
    send_sem,
    recv_sem,
    local_sem,
):
    dp, tensor = lax.axis_index("dp"), lax.axis_index("tensor")
    z, y = dp // 2, dp % 2
    a, b = tensor // 2, tensor % 2
    core_dev = (dp, tensor + 1 - 2 * b)
    x_dev = (dp, tensor + 2 - 4 * a)
    y_dev = (dp + 1 - 2 * y, tensor)

    def z_at(shift):
        return (z + shift) % 4

    def z_dev(shift):
        return (z_at(shift) * 2 + y, tensor)

    barrier = pltpu.get_barrier_semaphore()
    for dev in (core_dev, x_dev, y_dev, z_dev(1), z_dev(2), z_dev(3)):
        pl.semaphore_signal(barrier, inc=1, device_id=dev, device_id_type=MESH)
    loads = [
        (query_far, query_ref),
        (key_far, key_ref),
        (value_far, value_ref),
        (in_far, in_ref),
        (project_far, project_ref),
        (picks_far, picks_ref),
        (query_bias_far, query_bias_ref),
        (value_bias_far, value_bias_ref),
        *zip(rows_far, row_refs),
        (up_far, up_ref),
        (down_far, down_ref),
        (cot_far, cot_ref),
    ]
    loads = [
        pltpu.make_async_copy(src, goal, local_sem.at[index])
        for index, (src, goal) in enumerate(loads)
    ]
    for load in loads:
        load.start()

    def store_far(index, src, goal):
        return pltpu.make_async_copy(src, goal, local_sem.at[index])

    for load in loads:
        load.wait()
    pl.semaphore_wait(barrier, 6)

    def copy(index, src, dst, dev):
        return pltpu.make_async_remote_copy(
            src_ref=src,
            dst_ref=dst,
            send_sem=send_sem.at[index],
            recv_sem=recv_sem.at[index],
            device_id=dev,
            device_id_type=MESH,
        )

    def send(index, src, dst, dev):
        copy(index, src, dst, dev).start()

    def arrived(index, region):
        copy(index, region, region, core_dev).wait_recv()

    def left(index, region):
        copy(index, region, region, core_dev).wait_send()

    def store(pack):
        return (half, wide)[pack // 2], pack % 2

    def chip_rows(chip, start=0, size=96):
        first = pl.multiple_of(chip * 96, 16) + start
        return pl.ds(pl.multiple_of(first, 16), size)

    def piece(side, pack, chip, start=0, size=96):
        ref, slot = store(pack)
        return ref.at[side, slot, chip_rows(chip, start, size), :]

    def back_store(pack):
        if pack == 2:
            return wide, 0, slice(0, 768)
        if pack > 2:
            return half, pack - 3, slice(0, 384)
        return wide, 1, slice(384 * pack, 384 * pack + 384)

    def back_piece(side, pack, chip, start=0, size=96):
        ref, slot, cols = back_store(pack)
        return ref.at[side, slot, chip_rows(chip, start, size), cols]

    def part_of(refs, pack):
        return refs[1].at[0] if pack == 2 else refs[0].at[(0, 1, None, 2, 3)[pack]]

    def gather_id(pack, kind, j):
        return pack * 28 + 4 * kind + j

    def scatter_id(pack, kind, i):
        return 112 + pack * 24 + 4 * kind + i

    M_IN, M_COT, M_MASK, M_VZ, M_VY, M_VX = 232, 233, 234, 235, 238, 239
    M_TOK, M_OUT, M_GRAD, M_VG = 240, 242, 243, 244
    M_ROWS, M_PART = 250, 256
    Z_OWN, X_NEAR, Y_NEAR, X_CORNER, Y_CORNER, Z_X, Z_Y = range(7)

    def corner_id(pack, j):
        return gather_id(pack, (Z_OWN, Z_X, Z_Y)[j - 1], 0)

    D_X, D_Y, N_X, N_Y, L_Z, Q_Z = range(6)

    def gather_start(pack):
        own = (pack_ref.at[0], pack_ref.at[1], up_ref, down_ref)[pack]
        for j in (1, 3, 2):
            send(gather_id(pack, Z_OWN, j), own, piece(a, pack, dp), z_dev(j))
        send(gather_id(pack, X_NEAR, 0), own, piece(a, pack, dp), x_dev)
        send(gather_id(pack, Y_NEAR, 0), own, piece(a, pack, dp), y_dev)
        ref, slot = store(pack)
        ref[a, slot, chip_rows(dp), :] = own[...]

    def gather_spread(pack, j):
        chip = z_at(-j) * 2 + y
        arrived(gather_id(pack, Z_OWN, j), piece(a, pack, chip))
        spot = piece(a, pack, chip, LEAN, 96 - LEAN)
        send(gather_id(pack, X_NEAR, j), spot, spot, x_dev)
        send(gather_id(pack, Y_NEAR, j), spot, spot, y_dev)

    def gather_over_y(pack, j):
        first = 0 if j == 0 else LEAN
        chip = z_at(-j) * 2 + 1 - y
        arrived(gather_id(pack, Y_NEAR, j), piece(a, pack, chip, first, 96 - first))
        spot = piece(a, pack, chip, first, TURN - first)
        send(gather_id(pack, X_CORNER, j), spot, spot, x_dev)
        if j == 0:
            for step in (1, 3, 2):
                spot = piece(a, pack, chip, 0, LEAN)
                send(gather_id(pack, Z_Y, step), spot, spot, z_dev(step))

    def gather_over_x(pack, j):
        first = 0 if j == 0 else LEAN
        chip = z_at(-j) * 2 + y
        arrived(gather_id(pack, X_NEAR, j), piece(1 - a, pack, chip, first, 96 - first))
        spot = piece(1 - a, pack, chip, TURN, 96 - TURN)
        send(gather_id(pack, Y_CORNER, j), spot, spot, y_dev)
        if j == 0:
            for step in (1, 3, 2):
                spot = piece(1 - a, pack, chip, 0, LEAN)
                send(gather_id(pack, Z_X, step), spot, spot, z_dev(step))

    def gather_deep(pack, _):
        chip = z * 2 + 1 - y
        arrived(gather_id(pack, X_CORNER, 0), piece(1 - a, pack, chip, 0, TURN))
        spot = piece(1 - a, pack, chip, 0, LEAN)
        for step in (1, 3, 2):
            send(corner_id(pack, step), spot, spot, z_dev(step))

    def gather_end(pack):
        for j in range(4):
            over_y, over_x = z_at(-j) * 2 + 1 - y, z_at(-j) * 2 + y
            arrived(gather_id(pack, Y_CORNER, j), piece(1 - a, pack, over_y, TURN, 96 - TURN))
            if j > 0:
                arrived(gather_id(pack, X_CORNER, j), piece(1 - a, pack, over_y, LEAN, TURN - LEAN))
                arrived(gather_id(pack, Z_Y, j), piece(a, pack, over_y, 0, LEAN))
                arrived(gather_id(pack, Z_X, j), piece(1 - a, pack, over_x, 0, LEAN))
                arrived(corner_id(pack, j), piece(1 - a, pack, over_y, 0, LEAN))

    def gather_left(pack):
        def rows(size):
            return piece(a, pack, dp, 0, size)

        for j in range(4):
            first = 0 if j == 0 else LEAN
            left(gather_id(pack, X_NEAR, j), rows(96 - first))
            left(gather_id(pack, Y_NEAR, j), rows(96 - first))
            left(gather_id(pack, X_CORNER, j), rows(TURN - first))
            left(gather_id(pack, Y_CORNER, j), rows(96 - TURN))
            if j > 0:
                left(gather_id(pack, Z_OWN, j), rows(96))
                left(gather_id(pack, Z_Y, j), rows(LEAN))
                left(gather_id(pack, Z_X, j), rows(LEAN))
                left(corner_id(pack, j), rows(LEAN))

    def add_to(side, pack, chip, start, *blocks):
        ref, slot, cols = back_store(pack)
        rows = chip_rows(chip, start, blocks[0].shape[0])
        summed = ref[side, slot, rows, cols].astype(F32)
        for block in blocks:
            summed = summed + block.astype(F32)
        ref[side, slot, rows, cols] = summed.astype(BF16)

    def scatter_corner(pack, i):
        first = 0 if i == 0 else LEAN
        chip = z_at(i) * 2 + 1 - y
        over_x = part_of(diag_x, pack).at[i, pl.ds(0, BEND - first), :]
        send(scatter_id(pack, D_X, i), back_piece(1 - a, pack, chip, first, BEND - first), over_x, x_dev)
        over_y = part_of(diag_y, pack).at[i]
        send(scatter_id(pack, D_Y, i), back_piece(1 - a, pack, chip, BEND, 96 - BEND), over_y, y_dev)

    def scatter_first(pack):
        for i in (2, 1, 3):
            scatter_corner(pack, i)

    def scatter_start(pack):
        for i in (2, 1, 3):
            for side in range(2):
                for line in range(2):
                    spot = back_piece(side, pack, z_at(i) * 2 + line, 0, LEAN)
                    slot = part_of(deep_z, pack).at[i - 1, 2 * side + line]
                    send(scatter_id(pack, Q_Z, i), spot, slot, z_dev(i))

    def scatter_deep(pack, _):
        parts = part_of(deep_z, pack)
        for i in range(1, 4):
            arrived(scatter_id(pack, Q_Z, i), parts.at[i - 1])
        for side in range(2):
            for line in range(2):
                terms = [parts[i, 2 * side + line] for i in range(3)]
                add_to(side, pack, z * 2 + line, 0, *terms)
        scatter_corner(pack, 0)

    def scatter_near_y(pack, i):
        first = 0 if i == 0 else LEAN
        chip = z_at(i) * 2 + 1 - y
        over_x = part_of(diag_x, pack).at[i, pl.ds(0, BEND - first), :]
        arrived(scatter_id(pack, D_X, i), over_x)
        add_to(a, pack, chip, first, over_x[...])
        spot = back_piece(a, pack, chip, first, 96 - first)
        goal = part_of(near_y, pack).at[i, pl.ds(0, 96 - first), :]
        send(scatter_id(pack, N_Y, i), spot, goal, y_dev)

    def scatter_near_x(pack, i):
        first = 0 if i == 0 else LEAN
        chip = z_at(i) * 2 + y
        over_y = part_of(diag_y, pack).at[i]
        arrived(scatter_id(pack, D_Y, i), over_y)
        add_to(1 - a, pack, chip, BEND, over_y[...])
        spot = back_piece(1 - a, pack, chip, first, 96 - first)
        goal = part_of(near_x, pack).at[i, pl.ds(0, 96 - first), :]
        send(scatter_id(pack, N_X, i), spot, goal, x_dev)

    def scatter_line(pack, i):
        first = 0 if i == 0 else LEAN
        size = 96 - first
        from_x = part_of(near_x, pack).at[i, pl.ds(0, size), :]
        from_y = part_of(near_y, pack).at[i, pl.ds(0, size), :]
        arrived(scatter_id(pack, N_X, i), from_x)
        arrived(scatter_id(pack, N_Y, i), from_y)
        chip = z_at(i) * 2 + y
        ref, slot, cols = back_store(pack)
        rows = chip_rows(chip, first, size)
        own = ref[a, slot, rows, cols].astype(F32) + from_x[...].astype(F32) + from_y[...].astype(F32)
        if i == 0:
            part_of(total, pack)[...] = own
        else:
            ref[a, slot, rows, cols] = own.astype(BF16)
            spot = back_piece(a, pack, chip, first, size)
            send(scatter_id(pack, L_Z, i), spot, part_of(near_z, pack).at[i - 1], z_dev(i))

    def scatter_end(pack):
        parts, sums = part_of(near_z, pack), part_of(total, pack)
        for i in range(1, 4):
            arrived(scatter_id(pack, L_Z, i), parts.at[i - 1])
        goal = part_of((gout_half, gout_wide), pack)
        goal[0:LEAN, :] = sums[0:LEAN, :]
        own = sums[LEAN:96, :]
        for i in range(3):
            own = own + parts[i].astype(F32)
        goal[LEAN:96, :] = own

    def scatter_left(pack):
        def rows(size):
            return back_piece(a, pack, dp, 0, size)

        for i in range(4):
            first = 0 if i == 0 else LEAN
            left(scatter_id(pack, D_X, i), rows(BEND - first))
            left(scatter_id(pack, D_Y, i), rows(96 - BEND))
            left(scatter_id(pack, N_X, i), rows(96 - first))
            left(scatter_id(pack, N_Y, i), rows(96 - first))
            if i > 0:
                left(scatter_id(pack, L_Z, i), rows(96 - LEAN))
                left(scatter_id(pack, Q_Z, i), rows(4 * LEAN))

    def send_cot(pack, _):
        send(M_COT, cot_ref.at[1 - a], cots.at[a], x_dev)

    moves = (
        lambda pack, _: gather_start(pack),
        gather_spread,
        gather_over_y,
        gather_over_x,
        gather_deep,
        scatter_deep,
        scatter_near_y,
        scatter_near_x,
        scatter_line,
        send_cot,
    )

    def run(label):
        for kind, pack, place in PLAN.get(label, ()):
            moves[kind](pack, place)

    def run_at(step, prefix, count):
        for index in range(count):
            if PLAN.get(prefix + str(index)):
                pl.when(step == index)(lambda: run(prefix + str(index)))

    def turned(ref):
        block = ref[...].astype(F32)
        gap = jnp.zeros((block.shape[0], 128 - block.shape[1]), F32)
        return jnp.concatenate((block, gap), 1).T[: block.shape[1], :].astype(BF16)

    def placed(rows, width):
        gap = jnp.zeros((rows.shape[0], width - rows.shape[1]), F32)
        return pltpu.roll(jnp.concatenate((rows, gap), 1), dp * rows.shape[1], 1)

    project = turned(project_ref)
    pack_ref[0] = jnp.concatenate((query_ref[:, :128], key_ref[:, :128], value_ref[:, :128]), 1)
    pack_ref[1] = jnp.concatenate(
        (
            query_ref[:, 128:],
            key_ref[:, 128:],
            value_ref[:, 128:],
            project[:, 128:],
            project[:, :128],
        ),
        1,
    )
    rows = jnp.concatenate([ref[...].reshape(1, 96).astype(F32) for ref in row_refs], 0)
    query_row = placed(query_bias_ref[...].reshape(1, 24).astype(F32), 256)
    value_row = placed(value_bias_ref[...].reshape(1, 24).astype(F32), 256)
    gap = jnp.zeros((1, 128), F32)
    in_row = jnp.concatenate(
        (query_row[:, :128], gap, value_row[:, :128], query_row[:, 128:], value_row[:, 128:], gap), 1
    )
    vec_ref[...] = jnp.concatenate((placed(rows, 768), in_row, jnp.zeros((8, 768), F32)), 0).astype(
        BF16
    )
    column = lax.broadcasted_iota(jnp.int32, (16, 128), 1)
    row = lax.broadcasted_iota(jnp.int32, (16, 128), 0)
    fixed = (
        ((column - row <= 1) & (row - column <= 1))
        | (column == 0)
        | (column == 15)
        | (row == 0)
        | (row == 15)
    )
    for head in range(3):
        allowed = fixed
        for pick in range(picks_ref.shape[1]):
            picks = picks_ref[head, pick : pick + 1, :]
            picks = jnp.concatenate((picks, jnp.full((1, 112), -1, jnp.int32)), 1)
            allowed = allowed | (picks == row)
        mask_ref[16 * head : 16 * head + 16, :] = jnp.where(allowed, 1.0, 0.0).astype(BF16)
    send(M_MASK, mask_ref, masks.at[a], x_dev)
    send(M_IN, in_ref.at[1 - a], tokens.at[tensor], x_dev)
    for j in range(1, 4):
        send(M_VZ + j - 1, vec_ref, vec_z.at[j - 1], z_dev(j))
    gather_start(0)
    tokens[tensor] = in_ref[a]
    masks[a] = mask_ref[...]
    cots[a] = cot_ref[a]
    send(M_TOK, tokens.at[tensor], tokens.at[tensor], core_dev)
    vec_own = vec_ref[...].astype(F32)
    for j in range(1, 4):
        arrived(M_VZ + j - 1, vec_z.at[j - 1])
        vec_own = vec_own + vec_z[j - 1].astype(F32)
    vec_y[0] = vec_own.astype(BF16)
    send(M_VY, vec_y.at[0], vec_y.at[1], y_dev)
    arrived(M_MASK, masks.at[1 - a])
    spread = (
        lax.broadcasted_iota(jnp.int32, (128, 16 * BLOCK), 1) // BLOCK
        == lax.broadcasted_iota(jnp.int32, (128, 16 * BLOCK), 0)
    )
    spread = jnp.where(spread, 1.0, 0.0).astype(BF16)
    for side in range(2):
        bias = (dims(masks[side], spread, 1, 0) - 1.0) * 1e9
        for head in range(3):
            pair, place = (side, head) if head < 2 else (2, side)
            bias_k[pair, place] = bias[16 * head : 16 * head + 16]
            rows = masks[side, 16 * head : 16 * head + 16, :]
            turned_bias = (dims(rows, spread[:16], 0, 0) - 1.0) * 1e9
            for part in range(4):
                bias_q[pair, place, part] = turned_bias[4 * part : 4 * part + 4]
    run("pre")
    arrived(M_VY, vec_y.at[1])
    vec_all[a] = (vec_own + vec_y[1].astype(F32)).astype(BF16)
    send(M_VX, vec_all.at[a], vec_all.at[a], x_dev)
    other = (tensor + 2) % 4
    arrived(M_IN, tokens.at[other])
    send(M_TOK + 1, tokens.at[other], tokens.at[other], core_dev)
    run("tok")

    def vector(row):
        return vec_all[0, row : row + 1, :].astype(F32)

    def turn_rows(goal, ref, quarter):
        cols = pl.ds(pl.multiple_of(quarter * TILE, TILE), TILE)
        goal[:, cols] = ref[quarter].astype(F32).T.astype(BF16)

    arrived(M_TOK, tokens.at[0])
    arrived(M_TOK + 1, tokens.at[0])

    @pl.loop(0, 4)
    def _(quarter):
        turn_rows(tokens_turned, tokens, quarter)

    def project_heads(pair, bias):
        @pl.loop(0, 4)
        def _(quarter):
            rows = pl.ds(pl.multiple_of(quarter * TILE, TILE), TILE)
            block = dims(tokens[quarter], w_in[pair], 1, 0) + bias
            for kind in range(3):
                tile = block[:, 128 * kind : 128 * kind + 128]
                heads[3 * kind + pair, rows, :] = tile.astype(BF16)
                if kind == 1:
                    keys_turned[pair, :, rows] = tile.T.astype(BF16)

    run("p0")
    gather_end(0)
    arrived(M_VX, vec_all.at[1 - a])
    for side in range(2):
        w_in[side] = half[side, 0]
        project_heads(side, vec_all[side, 7:8, 0:384].astype(F32))
        run("q" + str(side))

    def third_heads():
        run("p1")
        gather_end(1)

        @pl.loop(0, 3)
        def _(part):
            rows = pl.ds(pl.multiple_of(part * TILE, TILE), TILE)
            third, out = pairs_of(half[0, 1, rows, :], half[1, 1, rows, :])
            w_in[2, rows, :] = third
            w_out[rows, :] = out

        vecs = [vec_all[side, :, 384:768].astype(F32) for side in range(2)]
        project_heads(2, pairs_of(vecs[0], vecs[1])[0][7:8])

    low = low_lanes((TILE, 128))
    none = jnp.zeros((TILE, 128), BF16)
    top = lax.broadcasted_iota(jnp.int32, (128, TILE), 0) < HEAD_DIM

    def of_head(block, head):
        return jnp.where(low, block, none) if head == 0 else jnp.where(low, none, block)

    @pl.loop(0, 12)
    def _(step):
        pl.when(step == 8)(third_heads)
        pair, part = step // 4, step % 4
        cols = pl.ds(pl.multiple_of(part * TILE, TILE), TILE)
        query_block = heads[pair, cols, :]
        terms, sums, mosts = [], [], []
        for head in range(2):
            scores = dims(of_head(query_block, head), heads[3 + pair], 1, 1).reshape(4, BLOCK, 1024)
            bias = bias_q[pair, head, part].reshape(4, 1, 1024)
            scores = (scores * (SCORE_SCALE * LOG2E) + bias).reshape(TILE, 1024)
            most = jnp.max(scores, axis=1, keepdims=True)
            term = jnp.exp2(scores - most)
            sums.append(jnp.sum(term, axis=1, keepdims=True))
            terms.append(term.astype(BF16))
            mosts.append(most)
        both = dims(jnp.concatenate(terms, 0), heads[6 + pair], 1, 0)
        mixed[pair, cols, :] = jnp.where(low, both[:TILE] / sums[0], both[TILE:] / sums[1]).astype(BF16)
        totals = [most + jnp.log2(total) for most, total in zip(mosts, sums)]
        turned_totals = jnp.where(low, totals[0], totals[1]).T
        lse[pair, 0, :, cols] = turned_totals[0:1]
        lse[pair, 1, :, cols] = turned_totals[HEAD_DIM : HEAD_DIM + 1]
        run_at(step, "f", 12)

    def beside(ref, indices, quarter):
        rows = pl.ds(pl.multiple_of(quarter * TILE, TILE), TILE)
        return jnp.concatenate([ref[index, rows, :] for index in indices], 1)

    def give(number, slot, block):
        send_buf[number % 2, slot] = block.astype(BF16)
        index = M_PART + 2 * number + slot
        send(index, send_buf.at[number % 2, slot], recv_buf.at[number % 2, slot], core_dev)

    def take(number, slot):
        arrived(M_PART + 2 * number + slot, recv_buf.at[number % 2, slot])
        return recv_buf[number % 2, slot].astype(F32)

    def given(number):
        for slot in range(2):
            left(M_PART + 2 * number + slot, send_buf.at[number % 2, slot])

    def share(kind, slot, ref):
        spot = ref.at[2 * slot + b]
        send(M_ROWS + 2 * kind + slot, spot, spot, core_dev)

    def shared(kind, slot, ref):
        arrived(M_ROWS + 2 * kind + slot, ref.at[2 * slot + 1 - b])

    def branch_part(quarter):
        return dims(beside(mixed, range(3), quarter), w_out[...], 1, 1)

    @pl.loop(0, 2)
    def _(slot):
        give(0, slot, branch_part(2 * slot + 1 - b))

    run("b0")

    @pl.loop(0, 2)
    def _(slot):
        quarter = 2 * slot + b
        own = branch_part(quarter)
        hidden = tokens[quarter].astype(F32) + own + take(0, slot) + vector(0)
        normed, factor = norm_of(hidden)
        hat_first[slot] = normed
        fac_first[slot] = factor
        first_low[quarter] = (normed * vector(1) + vector(2)).astype(BF16)
        share(0, slot, first_low)

    run("b1")
    for slot in range(2):
        turn_rows(first_turned, first_low, 2 * slot + b)
    run("b2")
    gather_end(2)

    def feed_up(quarter):
        @pl.loop(0, 2)
        def _(side):
            inner_buf[...] = (
                dims(first_low[quarter], wide[side, 0], 1, 0)
                + vec_all[side, 6:7, :].astype(F32)
            )

            @pl.loop(0, TILE // 32)
            def _(chunk):
                rows = pl.ds(pl.multiple_of(chunk * 32, 32), 32)
                inner = inner_buf[rows, :]
                normal = 0.5 * (1.0 + lax.erf(inner * 0.7071067811865476))
                density = jnp.exp2(inner * inner * (-0.5 * LOG2E)) * 0.3989422804014327
                active[side, quarter, rows, :] = (inner * normal).astype(BF16)
                slope[side, quarter, rows, :] = (normal + inner * density).astype(BF16)

    def feed_down(quarter):
        return dims(active[0, quarter], wide[0, 1], 1, 1) + dims(active[1, quarter], wide[1, 1], 1, 1)

    feed_up(b)
    run("u0")
    feed_up(2 + b)
    run("u1")
    for slot in range(2):
        shared(0, slot, first_low)
        feed_up(2 * slot + 1 - b)
        run("u" + str(2 + slot))
    gather_end(3)

    @pl.loop(0, 2)
    def _(slot):
        give(1, slot, feed_down(2 * slot + 1 - b))

    arrived(M_COT, cots.at[1 - a])
    vgrad[...] = jnp.zeros_like(vgrad)

    @pl.loop(0, 2)
    def _(slot):
        quarter = 2 * slot + b
        own = feed_down(quarter)
        second_in = hat_first[slot] * vector(1) + vector(2) + own + take(1, slot) + vector(3)
        normed, factor = norm_of(second_in)
        swap_out[slot] = (normed * vector(4) + vector(5)).astype(BF16)
        upstream = cots[slot].astype(F32)
        back = norm_pull(upstream, normed, factor, vector(4))
        back_rows[slot] = back
        feed_low[quarter] = back.astype(BF16)
        share(1, slot, feed_low)
        vgrad[0:1, :] += row_sum(upstream * normed)
        vgrad[1:2, :] += row_sum(upstream)
        vgrad[2:3, :] += row_sum(back)

    store_far(20, swap_out.at[a], out_ref.at[a]).start()
    send(M_OUT, swap_out.at[1 - a], out_ref.at[a], x_dev)
    for pack in range(4):
        gather_left(pack)

    def feed_back(quarter):
        for side in range(2):
            block = dims(feed_low[quarter], wide[side, 1], 1, 0) * slope[side, quarter].astype(F32)
            inner_low = block.astype(BF16)
            slope[side, quarter] = inner_low
            vgrad[6 + side : 7 + side, :] += row_sum(inner_low.astype(F32))

    def rest_back(quarter):
        return dims(slope[0, quarter], wide[0, 0], 1, 1) + dims(slope[1, quarter], wide[1, 0], 1, 1)

    def tall(ref, cols):
        return ref[:, :, cols].reshape(4 * TILE, TILE)

    sides = (1 - a, a)

    def down_grad(side, part):
        @pl.loop(0, 3)
        def _(piece_rows):
            rows = pl.ds(pl.multiple_of(piece_rows * TILE, TILE), TILE)
            right = active[side, :, :, 384 * part : 384 * part + 384].reshape(4 * TILE, 384)
            half[side, part, rows, :] = dims(tall(feed_low, rows), right, 0, 0).astype(BF16)


    @pl.loop(0, 2)
    def _(slot):
        feed_back(2 * slot + b)

    for slot in range(2):
        shared(1, slot, feed_low)
    for part in range(2):
        down_grad(sides[0], part)
        scatter_first(3 + part)
        down_grad(sides[1], part)
        scatter_start(3 + part)

    @pl.loop(0, 2)
    def _(slot):
        feed_back(2 * slot + 1 - b)

    given(0)

    @pl.loop(0, 2)
    def _(slot):
        give(2, slot, rest_back(2 * slot + 1 - b))

    for slot in range(2):
        turn_rows(first_turned, first_low, 2 * slot + 1 - b)
    run("r0")

    @pl.loop(0, 2)
    def _(slot):
        quarter = 2 * slot + b
        own = rest_back(quarter)
        upstream = back_rows[slot] + own + take(2, slot)
        normed = hat_first[slot]
        back = norm_pull(upstream, normed, fac_first[slot], vector(1))
        back_rows[slot] = back
        branch_low[quarter] = back.astype(BF16)
        share(2, slot, branch_low)
        vgrad[3:4, :] += row_sum(upstream * normed)
        vgrad[4:5, :] += row_sum(upstream)
        vgrad[5:6, :] += row_sum(back)

    run("r1")
    for side in sides:
        @pl.loop(0, 3)
        def _(part):
            rows = pl.ds(pl.multiple_of(part * TILE, TILE), TILE)
            right = slope[side].reshape(4 * TILE, 768)
            wide[side, 0, rows, :] = dims(first_turned[rows, :], right, 1, 0).astype(BF16)
        if side is sides[0]:
            scatter_first(2)
    scatter_start(2)
    run("r2")

    for slot in range(2):
        shared(2, slot, branch_low)

    @pl.loop(0, 4)
    def _(quarter):
        rows = pl.ds(pl.multiple_of(quarter * TILE, TILE), TILE)
        block = dims(branch_low[quarter], w_out[...], 1, 0).astype(BF16)
        for pair in range(3):
            mixed_back[pair, rows, :] = block[:, 128 * pair : 128 * pair + 128]

    run("r3")

    @pl.loop(0, 3)
    def _(part):
        rows = pl.ds(pl.multiple_of(part * TILE, TILE), TILE)
        right = jnp.concatenate([mixed[pair] for pair in range(3)], 1)
        out_grad[rows, :] = dims(tall(branch_low, rows), right, 0, 0).astype(BF16)
    run("r4")

    def heads_grad(pair, rows):
        right = jnp.concatenate([heads_back[3 * kind + pair] for kind in range(3)], 1)
        return dims(tokens_turned[rows, :], right, 1, 0)

    def first_heads_grad(side):
        @pl.loop(0, 3)
        def _(part):
            rows = pl.ds(pl.multiple_of(part * TILE, TILE), TILE)
            wide[side, 1, rows, 0:384] = heads_grad(side, rows).astype(BF16)

    @pl.loop(0, 12)
    def _(step):
        pair, part = step // 4, step % 4

        @pl.when(part == 0)
        def _():
            pick = (
                lax.broadcasted_iota(jnp.int32, (8, 128), 1) // HEAD_DIM
                == lax.broadcasted_iota(jnp.int32, (8, 128), 0)
            )
            pick = jnp.where(pick, 1.0, 0.0).astype(BF16)
            product = mixed[pair].astype(F32) * mixed_back[pair].astype(F32)
            high = product.astype(BF16)
            rest = (product - high.astype(F32)).astype(BF16)
            centre[...] = dims(pick, high, 1, 1) + dims(pick, rest, 1, 1)
            key_sum[...] = jnp.zeros_like(key_sum)
            value_sum[...] = jnp.zeros_like(value_sum)

        cols = pl.ds(pl.multiple_of(part * TILE, TILE), TILE)
        query_block, back_block = heads[pair, cols, :], mixed_back[pair, cols, :]
        value_block = heads[6 + pair]
        weights, score_backs, queries, backs, query_back = [], [], [], [], []
        for head in range(2):
            query_head, back_head = of_head(query_block, head), of_head(back_block, head)
            bias = bias_k[pair, head, :, cols] - lse[pair, head, :, cols]
            scores = dims(heads[3 + pair], query_head, 1, 1).reshape(16, BLOCK, TILE)
            scores = scores * (SCORE_SCALE * LOG2E) + bias.reshape(16, 1, TILE)
            weight = jnp.exp2(scores.reshape(1024, TILE))
            weight_back = dims(value_block, back_head, 1, 1)
            score_back = (weight * (weight_back - centre[head : head + 1, cols])).astype(BF16)
            weights.append(weight.astype(BF16))
            score_backs.append(score_back)
            queries.append(query_head)
            backs.append(back_head)
            query_back.append(dims(keys_turned[pair], score_back, 1, 0))
        value_sum[...] += dims(jnp.concatenate(weights, 1), jnp.concatenate(backs, 0), 1, 0)
        key_sum[...] += dims(jnp.concatenate(score_backs, 1), jnp.concatenate(queries, 0), 1, 0)
        query_grad = jnp.where(top, query_back[0], query_back[1]).T * SCORE_SCALE
        heads_back[pair, cols, :] = query_grad.astype(BF16)

        @pl.when(part == 3)
        def _():
            heads_back[3 + pair] = (key_sum[...] * SCORE_SCALE).astype(BF16)
            heads_back[6 + pair] = value_sum[...].astype(BF16)

        @pl.when(step == 7)
        def _():
            for side in range(2):
                first_heads_grad(side)
            scatter_first(0)
            scatter_start(0)

        run_at(step, "k", 12)

    @pl.loop(0, 3)
    def _(part):
        rows = pl.ds(pl.multiple_of(part * TILE, TILE), TILE)
        first, second = packs_of(heads_grad(2, rows), out_grad[rows, :].astype(F32))
        wide[0, 1, rows, 384:768] = first.astype(BF16)
        wide[1, 1, rows, 384:768] = second.astype(BF16)

    scatter_first(1)
    scatter_start(1)
    run("t0")
    for pair in range(3):
        vgrad[8:9, 128 * pair : 128 * pair + 128] = row_sum(heads_back[pair].astype(F32))
        vgrad[8:9, 384 + 128 * pair : 512 + 128 * pair] = row_sum(heads_back[6 + pair].astype(F32))
    send(M_VG, vgrad, vrecv.at[0], core_dev)

    def input_part(quarter):
        return sum(
            dims(beside(heads_back, (pair, 3 + pair, 6 + pair), quarter), w_in[pair], 1, 1)
            for pair in range(3)
        )

    given(1)

    @pl.loop(0, 2)
    def _(slot):
        give(3, slot, input_part(2 * slot + 1 - b))

    run("t1")
    arrived(M_VG, vrecv.at[0])
    mine = lax.broadcasted_iota(jnp.int32, (16, 768), 0) < 6
    vsend[0] = vgrad[...] + jnp.where(mine, vrecv[0], 0.0)
    send(M_VG + 1, vsend.at[0], vrecv.at[1], x_dev)

    @pl.loop(0, 2)
    def _(slot):
        own = input_part(2 * slot + b)
        back_rows[slot] = back_rows[slot] + own + take(3, slot)

    cots[0] = back_rows[1 - a].astype(BF16)
    send(M_GRAD, cots.at[0], cots.at[1], x_dev)
    store_far(21, back_rows.at[a], grad_ref.at[a]).start()
    arrived(M_VG + 1, vrecv.at[1])
    vsend[1] = vsend[0] + vrecv[1]
    send(M_VG + 2, vsend.at[1], vrecv.at[2], y_dev)
    run("t2")
    arrived(M_VG + 2, vrecv.at[2])
    vsend[2] = vsend[1] + vrecv[2]
    for j in range(1, 4):
        send(M_VG + 2 + j, vsend.at[2], vrecv.at[2 + j], z_dev(j))
    for pack in (3, 4, 2, 0):
        scatter_end(pack)
    run("t3")
    every = vsend[2]
    for j in range(1, 4):
        arrived(M_VG + 2 + j, vrecv.at[2 + j])
        every = every + vrecv[2 + j]
    vout_ref[...] = pltpu.roll(every, (8 - dp) % 8 * 96, 1)
    heads_row = every[8:9, :]
    for kind in range(2):
        row = heads_row[:, 384 * kind : 384 * kind + 384]
        low_row = low_lanes((1, 128))
        third = jnp.where(a == 0, row[:, 256:384], half_turn(row[:, 256:384]))
        both = jnp.concatenate(
            (jnp.where(a == 0, row[:, :128], row[:, 128:256]), jnp.where(low_row, third, 0.0)), 1
        )
        vout_ref[8 + kind : 9 + kind, 0:256] = pltpu.roll(both, (256 - dp * 24) % 256, 1)
    vout_ref[6:7, :] = jnp.where(a == 0, vout_ref[6:7, :], vout_ref[7:8, :])
    arrived(M_GRAD, cots.at[1])
    hat_first[0] = cots[1].astype(F32)
    store_far(22, hat_first.at[0], grad_ref.at[1 - a]).start()
    arrived(M_OUT, out_ref.at[1 - a])
    scatter_end(1)

    store_far(20, swap_out.at[a], out_ref.at[a]).wait()
    store_far(21, back_rows.at[a], grad_ref.at[a]).wait()
    store_far(22, hat_first.at[0], grad_ref.at[1 - a]).wait()

    for pack in range(5):
        scatter_left(pack)
    given(2)
    given(3)
    left(M_MASK, mask_ref)
    left(M_IN, in_ref.at[0])
    left(M_COT, cot_ref.at[0])
    left(M_OUT, swap_out.at[0])
    left(M_GRAD, cots.at[0])
    for j in range(3):
        left(M_VZ + j, vec_ref)
    left(M_VY, vec_y.at[0])
    left(M_VX, vec_all.at[0])
    for slot in range(2):
        left(M_TOK + slot, tokens.at[0])
        for kind in range(3):
            left(M_ROWS + 2 * kind + slot, first_low.at[0])
    for index in range(6):
        left(M_VG + index, vsend.at[0])


def finish_kernel(
    gout_half,
    gout_wide,
    vout_ref,
    from_output,
    from_grad,
    query_ref,
    key_ref,
    value_ref,
    project_ref,
    up_ref,
    down_ref,
    query_bias_ref,
    value_bias_ref,
    second_gain_ref,
    second_shift_ref,
    down_bias_ref,
    first_gain_ref,
    first_shift_ref,
    out_bias_ref,
    up_bias_ref,
    to_output,
    to_grad,
):
    row_refs = (
        second_gain_ref,
        second_shift_ref,
        down_bias_ref,
        first_gain_ref,
        first_shift_ref,
        out_bias_ref,
        up_bias_ref,
    )
    to_output[...] = from_output[...]
    to_grad[...] = from_grad[...]
    first, last = gout_half[0], gout_half[1]
    query_ref[...] = jnp.concatenate((first[:, 0:128], last[:, 0:64]), 1)
    key_ref[...] = jnp.concatenate((first[:, 128:256], last[:, 64:128]), 1)
    value_ref[...] = jnp.concatenate((first[:, 256:384], last[:, 128:192]), 1)
    gap = jnp.zeros((32, 256), F32)
    project = jnp.concatenate((last[:, 256:384], last[:, 128:256]), 1)
    project = jnp.concatenate((project, gap), 0).T
    project_ref[0:128, :] = project[0:128, :96]
    project_ref[128:192, :] = project[192:256, :96]
    up_ref[...] = gout_wide[0]
    down_ref[...] = jnp.concatenate((gout_half[2], gout_half[3]), 1)
    query_bias_ref[...] = vout_ref[8, 0:24]
    value_bias_ref[...] = vout_ref[9, 0:24]
    for row, ref in enumerate(row_refs):
        ref[...] = vout_ref[row, 0:96]


def layer_call(weights, rows, biases, random_blocks, tokens, cotangent):
    vmem = pltpu.VMEM
    anywhere = pl.BlockSpec(memory_space=pltpu.VMEM)
    far = pl.BlockSpec(memory_space=pl.ANY)
    shape = jax.ShapeDtypeStruct
    def both(*dims_, kind=BF16):
        return (vmem((4,) + dims_ + (384,), kind), vmem((1,) + dims_ + (768,), kind))

    like = lambda array: vmem(array.shape, array.dtype)
    scratch = [
        *(like(array) for array in weights),
        tuple(like(array) for array in rows),
        *(like(array) for array in (*biases, random_blocks, tokens, cotangent)),
        vmem((2, 96, 384), BF16),
        vmem((16, 768), BF16),
        vmem((48, 128), BF16),
        vmem((2, 2, 768, 384), BF16),
        vmem((2, 2, 768, 768), BF16),
        vmem((3, 16, 768), BF16),
        vmem((2, 16, 768), BF16),
        vmem((2, 16, 768), BF16),
        vmem((2, 48, 128), BF16),
        vmem((4, TILE, 768), BF16),
        vmem((768, 4 * TILE), BF16),
        vmem((2, TILE, 768), BF16),
        vmem((3, 768, 384), BF16),
        vmem((768, 384), BF16),
        vmem((3, 2, 4, 4, 1024), F32),
        vmem((3, 2, 16, 1024), F32),
        vmem((9, 1024, 128), BF16),
        vmem((3, 128, 1024), BF16),
        vmem((3, 1024, 128), BF16),
        vmem((3, 2, 1, 1024), F32),
        vmem((8, 1024), F32),
        vmem((4, TILE, 768), BF16),
        vmem((768, 4 * TILE), BF16),
        vmem((4, TILE, 768), BF16),
        vmem((4, TILE, 768), BF16),
        vmem((2, TILE, 768), F32),
        vmem((2, TILE, 1), F32),
        vmem((2, TILE, 768), F32),
        vmem((2, 4, TILE, 768), BF16),
        vmem((2, 4, TILE, 768), BF16),
        vmem((TILE, 768), F32),
        vmem((2, 2, TILE, 768), BF16),
        vmem((2, 2, TILE, 768), BF16),
        vmem((3, 1024, 128), BF16),
        vmem((1024, 128), F32),
        vmem((1024, 128), F32),
        vmem((9, 1024, 128), BF16),
        vmem((768, 384), BF16),
        both(4, 48),
        both(4, 48),
        both(4, 96),
        both(4, 96),
        both(3, 96 - LEAN),
        both(3, 4, LEAN),
        both(96, kind=F32),
        vmem((2, TILE, 768), BF16),
        vmem((16, 768), F32),
        vmem((3, 16, 768), F32),
        vmem((6, 16, 768), F32),
        pltpu.SemaphoreType.DMA((MESSAGES,)),
        pltpu.SemaphoreType.DMA((MESSAGES,)),
        pltpu.SemaphoreType.DMA((24,)),
    ]
    return pl.pallas_call(
        layer_kernel,
        out_shape=(
            shape(tokens.shape, BF16),
            shape(tokens.shape, F32),
            shape((4, 96, 384), F32),
            shape((1, 96, 768), F32),
            shape((16, 768), F32),
        ),
        in_specs=[far] * 6 + [(far,) * 7] + [far] * 5,
        out_specs=(far,) * 2 + (anywhere,) * 3,
        scratch_shapes=scratch,
        compiler_params=pltpu.CompilerParams(
            collective_id=0, has_side_effects=True, vmem_limit_bytes=63 << 20
        ),
    )(*weights, rows, *biases, random_blocks, tokens, cotangent)


def local_fast(
    inputs,
    random_blocks,
    query_weight,
    query_bias,
    key_weight,
    value_weight,
    value_bias,
    out_weight,
    out_bias,
    first_gain,
    first_shift,
    up_weight,
    up_bias,
    down_weight,
    down_bias,
    second_gain,
    second_shift,
    cotangent,
):
    output, input_grad, half_grads, wide_grads, sums = layer_call(
        (query_weight, key_weight, value_weight, down_weight.T, up_weight, out_weight),
        (out_bias, first_gain, first_shift, down_bias, second_gain, second_shift, up_bias),
        (query_bias, value_bias),
        random_blocks.transpose(0, 2, 1),
        inputs,
        cotangent,
    )
    like = lambda array: jax.ShapeDtypeStruct(array.shape, F32)
    whole = pl.BlockSpec(memory_space=pltpu.VMEM)
    outs = (query_weight, key_weight, value_weight, out_weight, up_weight, up_weight)
    outs += (query_bias, value_bias)
    outs += (second_gain, second_shift, down_bias, first_gain, first_shift, out_bias, up_bias)
    done = pl.pallas_call(
        finish_kernel,
        out_shape=tuple(like(array) for array in outs)
        + tuple(jax.ShapeDtypeStruct(array.shape, array.dtype) for array in (output, input_grad)),
        in_specs=[whole] * 5,
        out_specs=(whole,) * (len(outs) + 2),
    )(half_grads, wide_grads, sums, output, input_grad)
    query_grad, key_grad, value_grad, out_grad, up_grad, down_grad = done[:6]
    query_bias_grad, value_bias_grad = done[6:8]
    second_gain_grad, second_shift_grad, down_bias_grad = done[8:11]
    first_gain_grad, first_shift_grad, out_bias_grad, up_bias_grad = done[11:15]
    output, input_grad = done[15:]
    return (
        output,
        input_grad,
        query_grad,
        query_bias_grad,
        key_grad,
        value_grad,
        value_bias_grad,
        out_grad,
        out_bias_grad,
        first_gain_grad,
        first_shift_grad,
        up_grad,
        up_bias_grad,
        down_grad.T,
        down_bias_grad,
        second_gain_grad,
        second_shift_grad,
    )


def solution(mesh):
    sizes = mesh.shape
    fast = sizes["dp"] == 8 and sizes["tensor"] == 4
    return jax.shard_map(
        local_fast if fast else local,
        mesh=mesh,
        in_specs=(
            P("dp", "tensor", None),
            P("tensor", None, None),
            P("dp", "tensor"),
            P(("tensor", "dp")),
            P("dp", "tensor"),
            P("dp", "tensor"),
            P(("tensor", "dp")),
            P("tensor", "dp"),
            P("dp"),
            P("dp"),
            P("dp"),
            P("dp", "tensor"),
            P(("tensor", "dp")),
            P("tensor", "dp"),
            P("dp"),
            P("dp"),
            P("dp"),
            P("dp", "tensor", None),
        ),
        out_specs=(
            P("dp", "tensor", None),
            P("dp", "tensor", None),
            P("dp", "tensor"),
            P(("tensor", "dp")),
            P("dp", "tensor"),
            P("dp", "tensor"),
            P(("tensor", "dp")),
            P("tensor", "dp"),
            P("dp"),
            P("dp"),
            P("dp"),
            P("dp", "tensor"),
            P(("tensor", "dp")),
            P("tensor", "dp"),
            P("dp"),
            P("dp"),
            P("dp"),
        ),
        check_vma=False,
    )
```

```python
from functools import partial

import jax
import jax.numpy as jnp
from jax import lax
from jax.experimental import pallas as pl
from jax.experimental.pallas import tpu as pltpu
from jax.sharding import PartitionSpec as P

HEAD_DIM = 64
BLOCK = 64


norm_eps = 1e-12


def gather_weights(shards):
    return (
        lax.all_gather(shards[0], "dp", axis=0, tiled=True),
        lax.all_gather(shards[1], "dp", axis=0, tiled=True),
        lax.all_gather(shards[2], "dp", axis=0, tiled=True),
        lax.all_gather(shards[3], "dp", axis=0, tiled=True),
        lax.all_gather(shards[4], "dp", axis=0, tiled=True),
        lax.all_gather(shards[5], "dp", axis=1, tiled=True),
        lax.all_gather(shards[6], "dp", axis=0, tiled=True),
        lax.all_gather(shards[7], "dp", axis=0, tiled=True),
        lax.all_gather(shards[8], "dp", axis=0, tiled=True),
        lax.all_gather(shards[9], "dp", axis=0, tiled=True),
        lax.all_gather(shards[10], "dp", axis=0, tiled=True),
        lax.all_gather(shards[11], "dp", axis=1, tiled=True),
        lax.all_gather(shards[12], "dp", axis=0, tiled=True),
        lax.all_gather(shards[13], "dp", axis=0, tiled=True),
        lax.all_gather(shards[14], "dp", axis=0, tiled=True),
    )


def reduce_grads(grads):
    return (
        lax.psum_scatter(grads[0], "dp", scatter_dimension=0, tiled=True),
        lax.psum_scatter(grads[1], "dp", scatter_dimension=0, tiled=True),
        lax.psum_scatter(grads[2], "dp", scatter_dimension=0, tiled=True),
        lax.psum_scatter(grads[3], "dp", scatter_dimension=0, tiled=True),
        lax.psum_scatter(grads[4], "dp", scatter_dimension=0, tiled=True),
        lax.psum_scatter(grads[5], "dp", scatter_dimension=1, tiled=True),
        lax.psum_scatter(grads[6], "dp", scatter_dimension=0, tiled=True),
        lax.psum_scatter(grads[7], "dp", scatter_dimension=0, tiled=True),
        lax.psum_scatter(grads[8], "dp", scatter_dimension=0, tiled=True),
        lax.psum_scatter(grads[9], "dp", scatter_dimension=0, tiled=True),
        lax.psum_scatter(grads[10], "dp", scatter_dimension=0, tiled=True),
        lax.psum_scatter(grads[11], "dp", scatter_dimension=1, tiled=True),
        lax.psum_scatter(grads[12], "dp", scatter_dimension=0, tiled=True),
        lax.psum_scatter(grads[13], "dp", scatter_dimension=0, tiled=True),
        lax.psum_scatter(grads[14], "dp", scatter_dimension=0, tiled=True),
    )


def full_rows(block):
    return lax.all_gather(block, "tensor", axis=0, tiled=True)


def column_sums(partial_terms):
    return lax.psum_scatter(
        partial_terms.astype(jnp.bfloat16), "tensor", scatter_dimension=0, tiled=True
    ).astype(jnp.float32)


def block_allowed(random_blocks, block_count):
    row_ids = jnp.arange(block_count, dtype=jnp.int32)[:, None]
    col_ids = jnp.arange(block_count, dtype=jnp.int32)[None, :]
    fixed = (
        (jnp.abs(row_ids - col_ids) <= 1)
        | (col_ids == 0)
        | (col_ids == block_count - 1)
        | (row_ids == 0)
        | (row_ids == block_count - 1)
    )
    picked = jnp.any(
        random_blocks[:, :, :, None]
        == jnp.arange(block_count, dtype=jnp.int32)[None, None, None, :],
        axis=2,
    )
    return fixed[None, :, :] | picked


def layer_norm(values, gain, shift):
    mean = jnp.mean(values, axis=1, keepdims=True)
    spread = jnp.mean(values * values, axis=1, keepdims=True) - mean * mean
    factor = lax.rsqrt(spread + norm_eps)
    normed = (values - mean) * factor
    return (normed * gain + shift, normed, factor)


def norm_back(upstream, normed, factor, gain):
    scaled = upstream * gain
    plain = jnp.mean(scaled, axis=1, keepdims=True)
    along = jnp.mean(scaled * normed, axis=1, keepdims=True)
    back = factor * (scaled - plain - normed * along)
    return (back, jnp.sum(upstream * normed, axis=0), jnp.sum(upstream, axis=0))


def row_parts(array, span):
    return array.reshape((array.shape[0] // span, span) + array.shape[1:])


def mask_parts(allowed, span):
    return allowed.reshape(allowed.shape[0], -1, span // BLOCK, allowed.shape[2]).transpose(
        1, 0, 2, 3
    )


def block_scores(query_block, key_heads, mask_block):
    products = jnp.einsum(
        "qhd,khd->hqk", query_block, key_heads, preferred_element_type=jnp.float32
    )
    head_count, row_count, key_count = products.shape
    scaled = (products * HEAD_DIM ** (-0.5)).reshape(
        head_count, row_count // BLOCK, BLOCK, key_count // BLOCK, BLOCK
    )
    masked = jnp.where(mask_block[:, :, None, :, None], scaled, -1000000000.0)
    return masked.reshape(head_count, row_count, key_count)


def attend(query_heads, key_heads, value_heads, allowed):
    length = query_heads.shape[0]
    span = min(512, length)

    def one_part(items):
        query_block, mask_block = items
        scores = block_scores(query_block, key_heads, mask_block)
        largest = jnp.max(scores, axis=-1, keepdims=True)
        log_total = largest + jnp.log(jnp.sum(jnp.exp(scores - largest), axis=-1, keepdims=True))
        weights_low = jnp.exp(scores - log_total).astype(jnp.bfloat16)
        mixed = jnp.einsum(
            "hqk,khd->qhd", weights_low, value_heads, preferred_element_type=jnp.float32
        )
        return (mixed, log_total[..., 0])

    mixed, log_totals = lax.map(one_part, (row_parts(query_heads, span), mask_parts(allowed, span)))
    return (mixed.reshape(length, -1).astype(jnp.bfloat16), log_totals)


def attend_back(query_heads, key_heads, value_heads, mixed_back, log_totals, allowed):
    length = query_heads.shape[0]
    span = min(512, length)

    def one_part(carry, items):
        key_sum, value_sum = carry
        query_block, back_block, log_total, mask_block = items
        scores = block_scores(query_block, key_heads, mask_block)
        weights = jnp.exp(scores - log_total[..., None])
        weights_low = weights.astype(jnp.bfloat16)
        weights_back = jnp.einsum(
            "qhd,khd->hqk", back_block, value_heads, preferred_element_type=jnp.float32
        )
        centre = jnp.sum(weights_back * weights, axis=-1, keepdims=True)
        scores_back = (weights * (weights_back - centre) * HEAD_DIM ** (-0.5)).astype(jnp.bfloat16)
        query_back = jnp.einsum(
            "hqk,khd->qhd", scores_back, key_heads, preferred_element_type=jnp.float32
        )
        key_sum = key_sum + jnp.einsum(
            "hqk,qhd->khd", scores_back, query_block, preferred_element_type=jnp.float32
        )
        value_sum = value_sum + jnp.einsum(
            "hqk,qhd->khd", weights_low, back_block, preferred_element_type=jnp.float32
        )
        return ((key_sum, value_sum), query_back)

    empty = jnp.zeros(key_heads.shape, jnp.float32)
    (key_back, value_back), query_back = lax.scan(
        one_part,
        (empty, empty),
        (
            row_parts(query_heads, span),
            row_parts(mixed_back, span),
            log_totals,
            mask_parts(allowed, span),
        ),
    )
    return (
        query_back.reshape(length, -1).astype(jnp.bfloat16),
        key_back.reshape(length, -1).astype(jnp.bfloat16),
        value_back.reshape(length, -1).astype(jnp.bfloat16),
    )


def forward_pass(weights, token_block, allowed):
    (
        query_weight,
        query_bias,
        key_weight,
        value_weight,
        value_bias,
        out_weight,
        out_bias,
        first_gain,
        first_shift,
        up_weight,
        up_bias,
        down_weight,
        down_bias,
        second_gain,
        second_shift,
    ) = weights
    token_rows = full_rows(token_block)
    length = token_rows.shape[0]

    def heads_of(product):
        return product.astype(jnp.bfloat16).reshape(length, -1, HEAD_DIM)

    query_heads = heads_of(
        jnp.dot(token_rows, query_weight, preferred_element_type=jnp.float32) + query_bias
    )
    key_heads = heads_of(jnp.dot(token_rows, key_weight, preferred_element_type=jnp.float32))
    value_heads = heads_of(
        jnp.dot(token_rows, value_weight, preferred_element_type=jnp.float32) + value_bias
    )
    mixed, log_totals = attend(query_heads, key_heads, value_heads, allowed)
    branch_terms = jnp.dot(mixed, out_weight, preferred_element_type=jnp.float32)
    hidden = token_block.astype(jnp.float32) + column_sums(branch_terms) + out_bias
    first_norm, first_normed, first_factor = layer_norm(hidden, first_gain, first_shift)
    first_rows = full_rows(first_norm.astype(jnp.bfloat16))
    inner = jnp.dot(first_rows, up_weight, preferred_element_type=jnp.float32) + up_bias
    active = jax.nn.gelu(inner, approximate=False).astype(jnp.bfloat16)
    second_in = (
        first_norm
        + column_sums(jnp.dot(active, down_weight, preferred_element_type=jnp.float32))
        + down_bias
    )
    result, second_normed, second_factor = layer_norm(second_in, second_gain, second_shift)
    kept = (
        token_rows,
        query_heads,
        key_heads,
        value_heads,
        log_totals,
        mixed,
        first_normed,
        first_factor,
        first_rows,
        inner,
        active,
        second_normed,
        second_factor,
    )
    return (result, kept)


def backward_pass(weights, kept, upstream_block, allowed):
    (
        query_weight,
        query_bias,
        key_weight,
        value_weight,
        value_bias,
        out_weight,
        out_bias,
        first_gain,
        first_shift,
        up_weight,
        up_bias,
        down_weight,
        down_bias,
        second_gain,
        second_shift,
    ) = weights
    (
        token_rows,
        query_heads,
        key_heads,
        value_heads,
        log_totals,
        mixed,
        first_normed,
        first_factor,
        first_rows,
        inner,
        active,
        second_normed,
        second_factor,
    ) = kept
    length = token_rows.shape[0]
    upstream = upstream_block.astype(jnp.float32)
    second_back, second_gain_grad, second_shift_grad = norm_back(
        upstream, second_normed, second_factor, second_gain
    )
    down_bias_grad = jnp.sum(second_back, axis=0)
    feed_rows = full_rows(second_back.astype(jnp.bfloat16))
    down_weight_grad = jnp.einsum(
        "tf,td->fd", active, feed_rows, preferred_element_type=jnp.float32
    )
    active_back = jnp.einsum(
        "td,fd->tf", feed_rows, down_weight, preferred_element_type=jnp.float32
    )
    inner_back = jax.vjp(partial(jax.nn.gelu, approximate=False), inner)[1](active_back)[0].astype(
        jnp.bfloat16
    )
    up_bias_grad = jnp.sum(inner_back, axis=0, dtype=jnp.float32)
    up_weight_grad = jnp.einsum(
        "td,tf->df", first_rows, inner_back, preferred_element_type=jnp.float32
    )
    first_back = second_back + column_sums(
        jnp.einsum("tf,df->td", inner_back, up_weight, preferred_element_type=jnp.float32)
    )
    hidden_back, first_gain_grad, first_shift_grad = norm_back(
        first_back, first_normed, first_factor, first_gain
    )
    out_bias_grad = jnp.sum(hidden_back, axis=0)
    branch_rows = full_rows(hidden_back.astype(jnp.bfloat16))
    out_weight_grad = jnp.einsum(
        "tc,td->cd", mixed, branch_rows, preferred_element_type=jnp.float32
    )
    mixed_back = jnp.einsum(
        "td,cd->tc", branch_rows, out_weight, preferred_element_type=jnp.float32
    ).astype(jnp.bfloat16)
    query_back, key_back, value_back = attend_back(
        query_heads,
        key_heads,
        value_heads,
        mixed_back.reshape(length, -1, HEAD_DIM),
        log_totals,
        allowed,
    )
    query_weight_grad = jnp.einsum(
        "td,tc->dc", token_rows, query_back, preferred_element_type=jnp.float32
    )
    key_weight_grad = jnp.einsum(
        "td,tc->dc", token_rows, key_back, preferred_element_type=jnp.float32
    )
    value_weight_grad = jnp.einsum(
        "td,tc->dc", token_rows, value_back, preferred_element_type=jnp.float32
    )
    query_bias_grad = jnp.sum(query_back, axis=0, dtype=jnp.float32)
    value_bias_grad = jnp.sum(value_back, axis=0, dtype=jnp.float32)
    projected = (
        jnp.einsum("tc,dc->td", query_back, query_weight, preferred_element_type=jnp.float32)
        + jnp.einsum("tc,dc->td", key_back, key_weight, preferred_element_type=jnp.float32)
        + jnp.einsum("tc,dc->td", value_back, value_weight, preferred_element_type=jnp.float32)
    )
    input_back = hidden_back + column_sums(projected)
    grads = (
        query_weight_grad,
        query_bias_grad,
        key_weight_grad,
        value_weight_grad,
        value_bias_grad,
        out_weight_grad,
        out_bias_grad,
        first_gain_grad,
        first_shift_grad,
        up_weight_grad,
        up_bias_grad,
        down_weight_grad,
        down_bias_grad,
        second_gain_grad,
        second_shift_grad,
    )
    return (input_back, grads)


def local(
    inputs,
    random_blocks,
    query_weight,
    query_bias,
    key_weight,
    value_weight,
    value_bias,
    out_weight,
    out_bias,
    first_gain,
    first_shift,
    up_weight,
    up_bias,
    down_weight,
    down_bias,
    second_gain,
    second_shift,
    cotangent,
):
    shards = (
        query_weight,
        query_bias,
        key_weight,
        value_weight,
        value_bias,
        out_weight,
        out_bias,
        first_gain,
        first_shift,
        up_weight,
        up_bias,
        down_weight,
        down_bias,
        second_gain,
        second_shift,
    )
    allowed = block_allowed(random_blocks, random_blocks.shape[1])
    resident = gather_weights(shards)
    growth = lax.axis_size("dp")
    grown_dims = (0, 0, 0, 0, 0, 1, 0, 0, 0, 0, 0, 1, 0, 0, 0)
    start = tuple(
        (
            jnp.zeros(
                tuple(
                    (
                        extent * growth if position == grown_dim else extent
                        for position, extent in enumerate(shard.shape)
                    )
                ),
                jnp.float32,
            )
            for shard, grown_dim in zip(shards, grown_dims)
        )
    )

    def one_sequence(totals, items):
        token_block, upstream_block = items
        result, kept = forward_pass(resident, token_block, allowed)
        input_back, grads = backward_pass(resident, kept, upstream_block, allowed)
        totals = tuple((summed + update for summed, update in zip(totals, grads)))
        return (totals, (result.astype(jnp.bfloat16), input_back))

    totals, (results, input_backs) = lax.scan(one_sequence, start, (inputs, cotangent))
    shares = reduce_grads(totals)
    vectors = lax.psum(
        (shares[6], shares[7], shares[8], shares[12], shares[13], shares[14]), "tensor"
    )
    return (
        results,
        input_backs,
        shares[0],
        shares[1],
        shares[2],
        shares[3],
        shares[4],
        shares[5],
        vectors[0],
        vectors[1],
        vectors[2],
        shares[9],
        shares[10],
        shares[11],
        vectors[3],
        vectors[4],
        vectors[5],
    )


MESH = pl.DeviceIdType.MESH
(
    START,
    SPREAD,
    OVER_Y,
    OVER_X,
    DEEP,
    BACK_DEEP,
    BACK_Y,
    BACK_X,
    BACK_LINE,
    COT,
) = range(10)
PLAN = {
    "pre": (
        (START, 1, 0),
        (OVER_Y, 0, 0),
        (SPREAD, 0, 1),
        (OVER_Y, 1, 0),
        (SPREAD, 0, 2),
    ),
    "tok": (
        (SPREAD, 0, 3),
        (SPREAD, 1, 1),
        (OVER_X, 1, 0),
    ),
    "p0": (
        (OVER_X, 0, 1),
        (SPREAD, 1, 2),
        (OVER_X, 0, 0),
        (DEEP, 0, 0),
        (OVER_Y, 0, 3),
        (OVER_X, 0, 2),
        (OVER_Y, 0, 2),
        (OVER_Y, 0, 1),
        (START, 2, 0),
        (OVER_X, 0, 3),
        (OVER_Y, 1, 2),
        (DEEP, 1, 0),
        (START, 3, 0),
        (OVER_X, 1, 1),
        (OVER_X, 1, 2),
    ),
    "q0": (
        (SPREAD, 1, 3),
        (SPREAD, 2, 1),
    ),
    "q1": (
        (OVER_Y, 2, 0),
        (SPREAD, 2, 3),
        (OVER_X, 1, 3),
        (OVER_Y, 1, 3),
        (DEEP, 2, 0),
        (OVER_Y, 1, 1),
    ),
    "f1": (
        (OVER_X, 2, 0),
        (OVER_X, 2, 1),
        (SPREAD, 2, 2),
    ),
    "f3": (
        (OVER_Y, 2, 1),
        (OVER_X, 2, 3),
    ),
    "f4": (
        (COT, 0, 0),
    ),
    "f7": (
        (OVER_X, 3, 0),
    ),
    "p1": (
        (SPREAD, 3, 1),
    ),
    "f9": (
        (OVER_X, 2, 2),
    ),
    "f10": (
        (OVER_Y, 2, 3),
        (OVER_Y, 3, 0),
        (SPREAD, 3, 3),
    ),
    "f11": (
        (OVER_Y, 2, 2),
        (SPREAD, 3, 2),
    ),
    "b0": (
        (OVER_X, 3, 1),
        (OVER_Y, 3, 1),
    ),
    "b1": (
        (OVER_Y, 3, 3),
    ),
    "u0": (
        (OVER_X, 3, 3),
    ),
    "u1": (
        (OVER_X, 3, 2),
        (DEEP, 3, 0),
        (OVER_Y, 3, 2),
    ),
    "r0": (
        (BACK_X, 3, 2),
        (BACK_Y, 3, 3),
        (BACK_Y, 3, 2),
        (BACK_X, 4, 3),
        (BACK_X, 3, 3),
        (BACK_X, 4, 1),
        (BACK_DEEP, 3, 0),
        (BACK_Y, 4, 3),
        (BACK_X, 3, 1),
        (BACK_Y, 4, 1),
    ),
    "r1": (
        (BACK_LINE, 3, 2),
        (BACK_X, 4, 2),
        (BACK_DEEP, 4, 0),
    ),
    "r2": (
        (BACK_X, 3, 0),
        (BACK_X, 4, 0),
        (BACK_Y, 3, 1),
        (BACK_LINE, 3, 3),
        (BACK_Y, 3, 0),
    ),
    "r3": (
        (BACK_Y, 4, 2),
        (BACK_Y, 4, 0),
    ),
    "k0": (
        (BACK_LINE, 4, 3),
    ),
    "k1": (
        (BACK_X, 2, 2),
        (BACK_X, 2, 3),
    ),
    "k2": (
        (BACK_LINE, 3, 1),
    ),
    "k3": (
        (BACK_LINE, 4, 1),
        (BACK_Y, 2, 2),
        (BACK_LINE, 4, 2),
    ),
    "k4": (
        (BACK_X, 2, 1),
        (BACK_DEEP, 2, 0),
    ),
    "k5": (
        (BACK_Y, 2, 1),
        (BACK_Y, 2, 3),
    ),
    "k7": (
        (BACK_LINE, 2, 2),
        (BACK_Y, 2, 0),
    ),
    "k8": (
        (BACK_Y, 0, 2),
        (BACK_X, 2, 0),
    ),
    "k9": (
        (BACK_Y, 0, 3),
        (BACK_X, 0, 2),
    ),
    "k10": (
        (BACK_X, 0, 1),
    ),
    "k11": (
        (BACK_X, 0, 3),
    ),
    "t0": (
        (BACK_LINE, 3, 0),
        (BACK_LINE, 4, 0),
        (BACK_DEEP, 0, 0),
    ),
    "t1": (
        (BACK_LINE, 0, 2),
        (BACK_LINE, 2, 1),
        (BACK_Y, 0, 1),
        (BACK_LINE, 2, 3),
        (BACK_X, 1, 2),
        (BACK_X, 1, 3),
        (BACK_Y, 1, 1),
        (BACK_X, 0, 0),
        (BACK_X, 1, 1),
        (BACK_LINE, 2, 0),
        (BACK_Y, 1, 3),
    ),
    "t2": (
        (BACK_LINE, 0, 1),
        (BACK_Y, 1, 2),
        (BACK_LINE, 1, 1),
        (BACK_LINE, 0, 3),
        (BACK_Y, 0, 0),
        (BACK_LINE, 1, 2),
        (BACK_LINE, 1, 3),
        (BACK_DEEP, 1, 0),
        (BACK_LINE, 0, 0),
    ),
    "t3": (
        (BACK_X, 1, 0),
        (BACK_Y, 1, 0),
        (BACK_LINE, 1, 0),
    ),
}
F32 = jnp.float32
BF16 = jnp.bfloat16
LOG2E = 1.4426950408889634
SCORE_SCALE = HEAD_DIM ** (-0.5)
TILE = 256
MESSAGES = 272
LEAN = 16
TURN = 32
BEND = 48


def dims(left, right, left_dim, right_dim):
    return lax.dot_general(
        left, right, (((left_dim,), (right_dim,)), ((), ())), preferred_element_type=F32
    )


def low_lanes(shape):
    return lax.broadcasted_iota(jnp.int32, shape, len(shape) - 1) < HEAD_DIM


def half_turn(block):
    return pltpu.roll(block.astype(F32), HEAD_DIM, 1).astype(block.dtype)


def pairs_of(first, second):
    tile = lambda pack, index: pack[:, 128 * index : 128 * index + 128]
    low = low_lanes((first.shape[0], 128))
    e0, e1, f0, f1 = tile(first, 0), tile(second, 0), tile(first, 1), tile(second, 1)
    third = (
        jnp.where(low, e0, half_turn(e1)),
        jnp.where(low, half_turn(e0), e1),
        jnp.where(low, f0, half_turn(f1)),
    )
    out = (tile(first, 2), tile(second, 2), jnp.where(low, half_turn(f0), f1))
    return jnp.concatenate(third, 1), jnp.concatenate(out, 1)


def packs_of(third, out):
    tile = lambda block, index: block[:, 128 * index : 128 * index + 128]
    query, key, value = (tile(third, index) for index in range(3))
    low = low_lanes(query.shape)
    first = (
        jnp.where(low, query, half_turn(key)),
        jnp.where(low, value, half_turn(tile(out, 2))),
        tile(out, 0),
    )
    second = (
        jnp.where(low, half_turn(query), key),
        jnp.where(low, half_turn(value), tile(out, 2)),
        tile(out, 1),
    )
    return jnp.concatenate(first, 1), jnp.concatenate(second, 1)


def norm_of(values):
    mean = jnp.mean(values, axis=1, keepdims=True)
    spread = jnp.mean(values * values, axis=1, keepdims=True) - mean * mean
    factor = lax.rsqrt(spread + norm_eps)
    return (values - mean) * factor, factor


def norm_pull(upstream, normed, factor, gain):
    scaled = upstream * gain
    plain = jnp.mean(scaled, axis=1, keepdims=True)
    along = jnp.mean(scaled * normed, axis=1, keepdims=True)
    return factor * (scaled - plain - normed * along)


def row_sum(block):
    return jnp.sum(block, axis=0, keepdims=True)


def layer_kernel(
    query_far,
    key_far,
    value_far,
    down_far,
    up_far,
    project_far,
    rows_far,
    query_bias_far,
    value_bias_far,
    picks_far,
    in_far,
    cot_far,
    out_ref,
    grad_ref,
    gout_half,
    gout_wide,
    vout_ref,
    query_ref,
    key_ref,
    value_ref,
    down_ref,
    up_ref,
    project_ref,
    row_refs,
    query_bias_ref,
    value_bias_ref,
    picks_ref,
    in_ref,
    cot_ref,
    pack_ref,
    vec_ref,
    mask_ref,
    half,
    wide,
    vec_z,
    vec_y,
    vec_all,
    masks,
    tokens,
    tokens_turned,
    cots,
    w_in,
    w_out,
    bias_q,
    bias_k,
    heads,
    keys_turned,
    mixed,
    lse,
    centre,
    first_low,
    first_turned,
    feed_low,
    branch_low,
    hat_first,
    fac_first,
    back_rows,
    active,
    slope,
    inner_buf,
    send_buf,
    recv_buf,
    mixed_back,
    key_sum,
    value_sum,
    heads_back,
    out_grad,
    diag_x,
    diag_y,
    near_x,
    near_y,
    near_z,
    deep_z,
    total,
    swap_out,
    vgrad,
    vsend,
    vrecv,
    send_sem,
    recv_sem,
    local_sem,
):
    dp, tensor = lax.axis_index("dp"), lax.axis_index("tensor")
    z, y = dp // 2, dp % 2
    a, b = tensor // 2, tensor % 2
    core_dev = (dp, tensor + 1 - 2 * b)
    x_dev = (dp, tensor + 2 - 4 * a)
    y_dev = (dp + 1 - 2 * y, tensor)

    def z_at(shift):
        return (z + shift) % 4

    def z_dev(shift):
        return (z_at(shift) * 2 + y, tensor)

    barrier = pltpu.get_barrier_semaphore()
    for dev in (core_dev, x_dev, y_dev, z_dev(1), z_dev(2), z_dev(3)):
        pl.semaphore_signal(barrier, inc=1, device_id=dev, device_id_type=MESH)
    loads = [
        (query_far, query_ref),
        (key_far, key_ref),
        (value_far, value_ref),
        (in_far, in_ref),
        (project_far, project_ref),
        (picks_far, picks_ref),
        (query_bias_far, query_bias_ref),
        (value_bias_far, value_bias_ref),
        *zip(rows_far, row_refs),
        (up_far, up_ref),
        (down_far, down_ref),
        (cot_far, cot_ref),
    ]
    loads = [
        pltpu.make_async_copy(src, goal, local_sem.at[index])
        for index, (src, goal) in enumerate(loads)
    ]
    for load in loads:
        load.start()

    def store_far(index, src, goal):
        return pltpu.make_async_copy(src, goal, local_sem.at[index])

    for load in loads:
        load.wait()

    def copy(index, src, dst, dev):
        return pltpu.make_async_remote_copy(
            src_ref=src,
            dst_ref=dst,
            send_sem=send_sem.at[index],
            recv_sem=recv_sem.at[index],
            device_id=dev,
            device_id_type=MESH,
        )

    def send(index, src, dst, dev):
        copy(index, src, dst, dev).start()

    def arrived(index, region):
        copy(index, region, region, core_dev).wait_recv()

    def left(index, region):
        copy(index, region, region, core_dev).wait_send()

    def store(pack):
        return (half, wide)[pack // 2], pack % 2

    def chip_rows(chip, start=0, size=96):
        first = pl.multiple_of(chip * 96, 16) + start
        return pl.ds(pl.multiple_of(first, 16), size)

    def piece(side, pack, chip, start=0, size=96):
        ref, slot = store(pack)
        return ref.at[side, slot, chip_rows(chip, start, size), :]

    def back_store(pack):
        if pack == 2:
            return wide, 0, slice(0, 768)
        if pack > 2:
            return half, pack - 3, slice(0, 384)
        return wide, 1, slice(384 * pack, 384 * pack + 384)

    def back_piece(side, pack, chip, start=0, size=96):
        ref, slot, cols = back_store(pack)
        return ref.at[side, slot, chip_rows(chip, start, size), cols]

    def part_of(refs, pack):
        return refs[1].at[0] if pack == 2 else refs[0].at[(0, 1, None, 2, 3)[pack]]

    def gather_id(pack, kind, j):
        return pack * 28 + 4 * kind + j

    def scatter_id(pack, kind, i):
        return 112 + pack * 24 + 4 * kind + i

    M_IN, M_COT, M_MASK, M_VZ, M_VY, M_VX = 232, 233, 234, 235, 238, 239
    M_TOK, M_OUT, M_GRAD, M_VG = 240, 242, 243, 244
    M_ROWS, M_PART = 250, 256
    Z_OWN, X_NEAR, Y_NEAR, X_CORNER, Y_CORNER, Z_X, Z_Y = range(7)

    def corner_id(pack, j):
        return gather_id(pack, (Z_OWN, Z_X, Z_Y)[j - 1], 0)

    D_X, D_Y, N_X, N_Y, L_Z, Q_Z = range(6)

    def gather_start(pack):
        own = (pack_ref.at[0], pack_ref.at[1], up_ref, down_ref)[pack]
        for j in (1, 3, 2):
            send(gather_id(pack, Z_OWN, j), own, piece(a, pack, dp), z_dev(j))
        send(gather_id(pack, X_NEAR, 0), own, piece(a, pack, dp), x_dev)
        send(gather_id(pack, Y_NEAR, 0), own, piece(a, pack, dp), y_dev)
        ref, slot = store(pack)
        ref[a, slot, chip_rows(dp), :] = own[...]

    def gather_spread(pack, j):
        chip = z_at(-j) * 2 + y
        arrived(gather_id(pack, Z_OWN, j), piece(a, pack, chip))
        spot = piece(a, pack, chip, LEAN, 96 - LEAN)
        send(gather_id(pack, X_NEAR, j), spot, spot, x_dev)
        send(gather_id(pack, Y_NEAR, j), spot, spot, y_dev)

    def gather_over_y(pack, j):
        first = 0 if j == 0 else LEAN
        chip = z_at(-j) * 2 + 1 - y
        arrived(gather_id(pack, Y_NEAR, j), piece(a, pack, chip, first, 96 - first))
        spot = piece(a, pack, chip, first, TURN - first)
        send(gather_id(pack, X_CORNER, j), spot, spot, x_dev)
        if j == 0:
            for step in (1, 3, 2):
                spot = piece(a, pack, chip, 0, LEAN)
                send(gather_id(pack, Z_Y, step), spot, spot, z_dev(step))

    def gather_over_x(pack, j):
        first = 0 if j == 0 else LEAN
        chip = z_at(-j) * 2 + y
        arrived(gather_id(pack, X_NEAR, j), piece(1 - a, pack, chip, first, 96 - first))
        spot = piece(1 - a, pack, chip, TURN, 96 - TURN)
        send(gather_id(pack, Y_CORNER, j), spot, spot, y_dev)
        if j == 0:
            for step in (1, 3, 2):
                spot = piece(1 - a, pack, chip, 0, LEAN)
                send(gather_id(pack, Z_X, step), spot, spot, z_dev(step))

    def gather_deep(pack, _):
        chip = z * 2 + 1 - y
        arrived(gather_id(pack, X_CORNER, 0), piece(1 - a, pack, chip, 0, TURN))
        spot = piece(1 - a, pack, chip, 0, LEAN)
        for step in (1, 3, 2):
            send(corner_id(pack, step), spot, spot, z_dev(step))

    def gather_end(pack):
        for j in range(4):
            over_y, over_x = z_at(-j) * 2 + 1 - y, z_at(-j) * 2 + y
            arrived(gather_id(pack, Y_CORNER, j), piece(1 - a, pack, over_y, TURN, 96 - TURN))
            if j > 0:
                arrived(gather_id(pack, X_CORNER, j), piece(1 - a, pack, over_y, LEAN, TURN - LEAN))
                arrived(gather_id(pack, Z_Y, j), piece(a, pack, over_y, 0, LEAN))
                arrived(gather_id(pack, Z_X, j), piece(1 - a, pack, over_x, 0, LEAN))
                arrived(corner_id(pack, j), piece(1 - a, pack, over_y, 0, LEAN))

    def gather_left(pack):
        def rows(size):
            return piece(a, pack, dp, 0, size)

        for j in range(4):
            first = 0 if j == 0 else LEAN
            left(gather_id(pack, X_NEAR, j), rows(96 - first))
            left(gather_id(pack, Y_NEAR, j), rows(96 - first))
            left(gather_id(pack, X_CORNER, j), rows(TURN - first))
            left(gather_id(pack, Y_CORNER, j), rows(96 - TURN))
            if j > 0:
                left(gather_id(pack, Z_OWN, j), rows(96))
                left(gather_id(pack, Z_Y, j), rows(LEAN))
                left(gather_id(pack, Z_X, j), rows(LEAN))
                left(corner_id(pack, j), rows(LEAN))

    def add_to(side, pack, chip, start, *blocks):
        ref, slot, cols = back_store(pack)
        rows = chip_rows(chip, start, blocks[0].shape[0])
        summed = ref[side, slot, rows, cols].astype(F32)
        for block in blocks:
            summed = summed + block.astype(F32)
        ref[side, slot, rows, cols] = summed.astype(BF16)

    def scatter_corner(pack, i):
        first = 0 if i == 0 else LEAN
        chip = z_at(i) * 2 + 1 - y
        over_x = part_of(diag_x, pack).at[i, pl.ds(0, BEND - first), :]
        send(scatter_id(pack, D_X, i), back_piece(1 - a, pack, chip, first, BEND - first), over_x, x_dev)
        over_y = part_of(diag_y, pack).at[i]
        send(scatter_id(pack, D_Y, i), back_piece(1 - a, pack, chip, BEND, 96 - BEND), over_y, y_dev)

    def scatter_first(pack):
        for i in (2, 1, 3):
            scatter_corner(pack, i)

    def scatter_start(pack):
        for i in (2, 1, 3):
            for side in range(2):
                for line in range(2):
                    spot = back_piece(side, pack, z_at(i) * 2 + line, 0, LEAN)
                    slot = part_of(deep_z, pack).at[i - 1, 2 * side + line]
                    send(scatter_id(pack, Q_Z, i), spot, slot, z_dev(i))

    def scatter_deep(pack, _):
        parts = part_of(deep_z, pack)
        for i in range(1, 4):
            arrived(scatter_id(pack, Q_Z, i), parts.at[i - 1])
        for side in range(2):
            for line in range(2):
                terms = [parts[i, 2 * side + line] for i in range(3)]
                add_to(side, pack, z * 2 + line, 0, *terms)
        scatter_corner(pack, 0)

    def scatter_near_y(pack, i):
        first = 0 if i == 0 else LEAN
        chip = z_at(i) * 2 + 1 - y
        over_x = part_of(diag_x, pack).at[i, pl.ds(0, BEND - first), :]
        arrived(scatter_id(pack, D_X, i), over_x)
        add_to(a, pack, chip, first, over_x[...])
        spot = back_piece(a, pack, chip, first, 96 - first)
        goal = part_of(near_y, pack).at[i, pl.ds(0, 96 - first), :]
        send(scatter_id(pack, N_Y, i), spot, goal, y_dev)

    def scatter_near_x(pack, i):
        first = 0 if i == 0 else LEAN
        chip = z_at(i) * 2 + y
        over_y = part_of(diag_y, pack).at[i]
        arrived(scatter_id(pack, D_Y, i), over_y)
        add_to(1 - a, pack, chip, BEND, over_y[...])
        spot = back_piece(1 - a, pack, chip, first, 96 - first)
        goal = part_of(near_x, pack).at[i, pl.ds(0, 96 - first), :]
        send(scatter_id(pack, N_X, i), spot, goal, x_dev)

    def scatter_line(pack, i):
        first = 0 if i == 0 else LEAN
        size = 96 - first
        from_x = part_of(near_x, pack).at[i, pl.ds(0, size), :]
        from_y = part_of(near_y, pack).at[i, pl.ds(0, size), :]
        arrived(scatter_id(pack, N_X, i), from_x)
        arrived(scatter_id(pack, N_Y, i), from_y)
        chip = z_at(i) * 2 + y
        ref, slot, cols = back_store(pack)
        rows = chip_rows(chip, first, size)
        own = ref[a, slot, rows, cols].astype(F32) + from_x[...].astype(F32) + from_y[...].astype(F32)
        if i == 0:
            part_of(total, pack)[...] = own
        else:
            ref[a, slot, rows, cols] = own.astype(BF16)
            spot = back_piece(a, pack, chip, first, size)
            send(scatter_id(pack, L_Z, i), spot, part_of(near_z, pack).at[i - 1], z_dev(i))

    def scatter_end(pack):
        parts, sums = part_of(near_z, pack), part_of(total, pack)
        for i in range(1, 4):
            arrived(scatter_id(pack, L_Z, i), parts.at[i - 1])
        goal = part_of((gout_half, gout_wide), pack)
        goal[0:LEAN, :] = sums[0:LEAN, :]
        own = sums[LEAN:96, :]
        for i in range(3):
            own = own + parts[i].astype(F32)
        goal[LEAN:96, :] = own

    def scatter_left(pack):
        def rows(size):
            return back_piece(a, pack, dp, 0, size)

        for i in range(4):
            first = 0 if i == 0 else LEAN
            left(scatter_id(pack, D_X, i), rows(BEND - first))
            left(scatter_id(pack, D_Y, i), rows(96 - BEND))
            left(scatter_id(pack, N_X, i), rows(96 - first))
            left(scatter_id(pack, N_Y, i), rows(96 - first))
            if i > 0:
                left(scatter_id(pack, L_Z, i), rows(96 - LEAN))
                left(scatter_id(pack, Q_Z, i), rows(4 * LEAN))

    def send_cot(pack, _):
        send(M_COT, cot_ref.at[1 - a], cots.at[a], x_dev)

    moves = (
        lambda pack, _: gather_start(pack),
        gather_spread,
        gather_over_y,
        gather_over_x,
        gather_deep,
        scatter_deep,
        scatter_near_y,
        scatter_near_x,
        scatter_line,
        send_cot,
    )

    def run(label):
        for kind, pack, place in PLAN.get(label, ()):
            moves[kind](pack, place)

    def run_at(step, prefix, count):
        for index in range(count):
            if PLAN.get(prefix + str(index)):
                pl.when(step == index)(lambda: run(prefix + str(index)))

    def turned(ref):
        block = ref[...].astype(F32)
        gap = jnp.zeros((block.shape[0], 128 - block.shape[1]), F32)
        return jnp.concatenate((block, gap), 1).T[: block.shape[1], :].astype(BF16)

    def placed(rows, width):
        gap = jnp.zeros((rows.shape[0], width - rows.shape[1]), F32)
        return pltpu.roll(jnp.concatenate((rows, gap), 1), dp * rows.shape[1], 1)

    project = turned(project_ref)
    pack_ref[0] = jnp.concatenate((query_ref[:, :128], key_ref[:, :128], value_ref[:, :128]), 1)
    pack_ref[1] = jnp.concatenate(
        (
            query_ref[:, 128:],
            key_ref[:, 128:],
            value_ref[:, 128:],
            project[:, 128:],
            project[:, :128],
        ),
        1,
    )
    rows = jnp.concatenate([ref[...].reshape(1, 96).astype(F32) for ref in row_refs], 0)
    query_row = placed(query_bias_ref[...].reshape(1, 24).astype(F32), 256)
    value_row = placed(value_bias_ref[...].reshape(1, 24).astype(F32), 256)
    gap = jnp.zeros((1, 128), F32)
    in_row = jnp.concatenate(
        (query_row[:, :128], gap, value_row[:, :128], query_row[:, 128:], value_row[:, 128:], gap), 1
    )
    vec_ref[...] = jnp.concatenate((placed(rows, 768), in_row, jnp.zeros((8, 768), F32)), 0).astype(
        BF16
    )
    column = lax.broadcasted_iota(jnp.int32, (16, 128), 1)
    row = lax.broadcasted_iota(jnp.int32, (16, 128), 0)
    fixed = (
        ((column - row <= 1) & (row - column <= 1))
        | (column == 0)
        | (column == 15)
        | (row == 0)
        | (row == 15)
    )
    for head in range(3):
        allowed = fixed
        for pick in range(picks_ref.shape[1]):
            picks = picks_ref[head, pick : pick + 1, :]
            picks = jnp.concatenate((picks, jnp.full((1, 112), -1, jnp.int32)), 1)
            allowed = allowed | (picks == row)
        mask_ref[16 * head : 16 * head + 16, :] = jnp.where(allowed, 1.0, 0.0).astype(BF16)
    pl.semaphore_wait(barrier, 6)
    send(M_MASK, mask_ref, masks.at[a], x_dev)
    send(M_IN, in_ref.at[1 - a], tokens.at[tensor], x_dev)
    for j in range(1, 4):
        send(M_VZ + j - 1, vec_ref, vec_z.at[j - 1], z_dev(j))
    gather_start(0)
    tokens[tensor] = in_ref[a]
    masks[a] = mask_ref[...]
    cots[a] = cot_ref[a]
    send(M_TOK, tokens.at[tensor], tokens.at[tensor], core_dev)
    vec_own = vec_ref[...].astype(F32)
    for j in range(1, 4):
        arrived(M_VZ + j - 1, vec_z.at[j - 1])
        vec_own = vec_own + vec_z[j - 1].astype(F32)
    vec_y[0] = vec_own.astype(BF16)
    send(M_VY, vec_y.at[0], vec_y.at[1], y_dev)
    arrived(M_MASK, masks.at[1 - a])
    spread = (
        lax.broadcasted_iota(jnp.int32, (128, 16 * BLOCK), 1) // BLOCK
        == lax.broadcasted_iota(jnp.int32, (128, 16 * BLOCK), 0)
    )
    spread = jnp.where(spread, 1.0, 0.0).astype(BF16)
    for side in range(2):
        bias = (dims(masks[side], spread, 1, 0) - 1.0) * 1e9
        for head in range(3):
            pair, place = (side, head) if head < 2 else (2, side)
            bias_k[pair, place] = bias[16 * head : 16 * head + 16]
            rows = masks[side, 16 * head : 16 * head + 16, :]
            turned_bias = (dims(rows, spread[:16], 0, 0) - 1.0) * 1e9
            for part in range(4):
                bias_q[pair, place, part] = turned_bias[4 * part : 4 * part + 4]
    run("pre")
    arrived(M_VY, vec_y.at[1])
    vec_all[a] = (vec_own + vec_y[1].astype(F32)).astype(BF16)
    send(M_VX, vec_all.at[a], vec_all.at[a], x_dev)
    other = (tensor + 2) % 4
    arrived(M_IN, tokens.at[other])
    send(M_TOK + 1, tokens.at[other], tokens.at[other], core_dev)
    run("tok")

    def vector(row):
        return vec_all[0, row : row + 1, :].astype(F32)

    def turn_rows(goal, ref, quarter):
        cols = pl.ds(pl.multiple_of(quarter * TILE, TILE), TILE)
        goal[:, cols] = ref[quarter].astype(F32).T.astype(BF16)

    arrived(M_TOK, tokens.at[0])
    arrived(M_TOK + 1, tokens.at[0])

    @pl.loop(0, 4)
    def _(quarter):
        turn_rows(tokens_turned, tokens, quarter)

    def project_heads(pair, bias):
        @pl.loop(0, 4)
        def _(quarter):
            rows = pl.ds(pl.multiple_of(quarter * TILE, TILE), TILE)
            block = dims(tokens[quarter], w_in[pair], 1, 0) + bias
            for kind in range(3):
                tile = block[:, 128 * kind : 128 * kind + 128]
                heads[3 * kind + pair, rows, :] = tile.astype(BF16)
                if kind == 1:
                    keys_turned[pair, :, rows] = tile.T.astype(BF16)

    run("p0")
    gather_end(0)
    arrived(M_VX, vec_all.at[1 - a])
    for side in range(2):
        w_in[side] = half[side, 0]
        project_heads(side, vec_all[side, 7:8, 0:384].astype(F32))
        run("q" + str(side))

    def third_heads():
        run("p1")
        gather_end(1)

        @pl.loop(0, 3)
        def _(part):
            rows = pl.ds(pl.multiple_of(part * TILE, TILE), TILE)
            third, out = pairs_of(half[0, 1, rows, :], half[1, 1, rows, :])
            w_in[2, rows, :] = third
            w_out[rows, :] = out

        vecs = [vec_all[side, :, 384:768].astype(F32) for side in range(2)]
        project_heads(2, pairs_of(vecs[0], vecs[1])[0][7:8])

    low = low_lanes((TILE, 128))
    none = jnp.zeros((TILE, 128), BF16)
    top = lax.broadcasted_iota(jnp.int32, (128, TILE), 0) < HEAD_DIM

    def of_head(block, head):
        return jnp.where(low, block, none) if head == 0 else jnp.where(low, none, block)

    @pl.loop(0, 12)
    def _(step):
        pl.when(step == 8)(third_heads)
        pair, part = step // 4, step % 4
        cols = pl.ds(pl.multiple_of(part * TILE, TILE), TILE)
        query_block = heads[pair, cols, :]
        terms, sums, mosts = [], [], []
        for head in range(2):
            scores = dims(of_head(query_block, head), heads[3 + pair], 1, 1).reshape(4, BLOCK, 1024)
            bias = bias_q[pair, head, part].reshape(4, 1, 1024)
            scores = (scores * (SCORE_SCALE * LOG2E) + bias).reshape(TILE, 1024)
            most = jnp.max(scores, axis=1, keepdims=True)
            term = jnp.exp2(scores - most)
            sums.append(jnp.sum(term, axis=1, keepdims=True))
            terms.append(term.astype(BF16))
            mosts.append(most)
        both = dims(jnp.concatenate(terms, 0), heads[6 + pair], 1, 0)
        mixed[pair, cols, :] = jnp.where(low, both[:TILE] / sums[0], both[TILE:] / sums[1]).astype(BF16)
        totals = [most + jnp.log2(total) for most, total in zip(mosts, sums)]
        turned_totals = jnp.where(low, totals[0], totals[1]).T
        lse[pair, 0, :, cols] = turned_totals[0:1]
        lse[pair, 1, :, cols] = turned_totals[HEAD_DIM : HEAD_DIM + 1]
        run_at(step, "f", 12)

    def beside(ref, indices, quarter):
        rows = pl.ds(pl.multiple_of(quarter * TILE, TILE), TILE)
        return jnp.concatenate([ref[index, rows, :] for index in indices], 1)

    def give(number, slot, block):
        send_buf[number % 2, slot] = block.astype(BF16)
        index = M_PART + 2 * number + slot
        send(index, send_buf.at[number % 2, slot], recv_buf.at[number % 2, slot], core_dev)

    def take(number, slot):
        arrived(M_PART + 2 * number + slot, recv_buf.at[number % 2, slot])
        return recv_buf[number % 2, slot].astype(F32)

    def given(number):
        for slot in range(2):
            left(M_PART + 2 * number + slot, send_buf.at[number % 2, slot])

    def share(kind, slot, ref):
        spot = ref.at[2 * slot + b]
        send(M_ROWS + 2 * kind + slot, spot, spot, core_dev)

    def shared(kind, slot, ref):
        arrived(M_ROWS + 2 * kind + slot, ref.at[2 * slot + 1 - b])

    def branch_part(quarter):
        return dims(beside(mixed, range(3), quarter), w_out[...], 1, 1)

    @pl.loop(0, 2)
    def _(slot):
        give(0, slot, branch_part(2 * slot + 1 - b))

    run("b0")

    @pl.loop(0, 2)
    def _(slot):
        quarter = 2 * slot + b
        own = branch_part(quarter)
        hidden = tokens[quarter].astype(F32) + own + take(0, slot) + vector(0)
        normed, factor = norm_of(hidden)
        hat_first[slot] = normed
        fac_first[slot] = factor
        first_low[quarter] = (normed * vector(1) + vector(2)).astype(BF16)
        share(0, slot, first_low)

    run("b1")
    for slot in range(2):
        turn_rows(first_turned, first_low, 2 * slot + b)
    run("b2")
    gather_end(2)

    def feed_up(quarter):
        @pl.loop(0, 2)
        def _(side):
            inner_buf[...] = (
                dims(first_low[quarter], wide[side, 0], 1, 0)
                + vec_all[side, 6:7, :].astype(F32)
            )

            @pl.loop(0, TILE // 32)
            def _(chunk):
                rows = pl.ds(pl.multiple_of(chunk * 32, 32), 32)
                inner = inner_buf[rows, :]
                normal = 0.5 * (1.0 + lax.erf(inner * 0.7071067811865476))
                density = jnp.exp2(inner * inner * (-0.5 * LOG2E)) * 0.3989422804014327
                active[side, quarter, rows, :] = (inner * normal).astype(BF16)
                slope[side, quarter, rows, :] = (normal + inner * density).astype(BF16)

    def feed_down(quarter):
        return dims(active[0, quarter], wide[0, 1], 1, 1) + dims(active[1, quarter], wide[1, 1], 1, 1)

    feed_up(b)
    run("u0")
    feed_up(2 + b)
    run("u1")
    for slot in range(2):
        shared(0, slot, first_low)
        feed_up(2 * slot + 1 - b)
        run("u" + str(2 + slot))
    gather_end(3)

    @pl.loop(0, 2)
    def _(slot):
        give(1, slot, feed_down(2 * slot + 1 - b))

    arrived(M_COT, cots.at[1 - a])
    vgrad[...] = jnp.zeros_like(vgrad)

    @pl.loop(0, 2)
    def _(slot):
        quarter = 2 * slot + b
        own = feed_down(quarter)
        second_in = hat_first[slot] * vector(1) + vector(2) + own + take(1, slot) + vector(3)
        normed, factor = norm_of(second_in)
        swap_out[slot] = (normed * vector(4) + vector(5)).astype(BF16)
        upstream = cots[slot].astype(F32)
        back = norm_pull(upstream, normed, factor, vector(4))
        back_rows[slot] = back
        feed_low[quarter] = back.astype(BF16)
        share(1, slot, feed_low)
        vgrad[0:1, :] += row_sum(upstream * normed)
        vgrad[1:2, :] += row_sum(upstream)
        vgrad[2:3, :] += row_sum(back)

    store_far(20, swap_out.at[a], out_ref.at[a]).start()
    send(M_OUT, swap_out.at[1 - a], out_ref.at[a], x_dev)
    for pack in range(4):
        gather_left(pack)

    def feed_back(quarter):
        for side in range(2):
            block = dims(feed_low[quarter], wide[side, 1], 1, 0) * slope[side, quarter].astype(F32)
            inner_low = block.astype(BF16)
            slope[side, quarter] = inner_low
            vgrad[6 + side : 7 + side, :] += row_sum(inner_low.astype(F32))

    def rest_back(quarter):
        return dims(slope[0, quarter], wide[0, 0], 1, 1) + dims(slope[1, quarter], wide[1, 0], 1, 1)

    def tall(ref, cols):
        return ref[:, :, cols].reshape(4 * TILE, TILE)

    sides = (1 - a, a)

    def down_grad(side, part):
        @pl.loop(0, 3)
        def _(piece_rows):
            rows = pl.ds(pl.multiple_of(piece_rows * TILE, TILE), TILE)
            right = active[side, :, :, 384 * part : 384 * part + 384].reshape(4 * TILE, 384)
            half[side, part, rows, :] = dims(tall(feed_low, rows), right, 0, 0).astype(BF16)


    @pl.loop(0, 2)
    def _(slot):
        feed_back(2 * slot + b)

    for slot in range(2):
        shared(1, slot, feed_low)
    for part in range(2):
        down_grad(sides[0], part)
        scatter_first(3 + part)
        down_grad(sides[1], part)
        scatter_start(3 + part)

    @pl.loop(0, 2)
    def _(slot):
        feed_back(2 * slot + 1 - b)

    given(0)

    @pl.loop(0, 2)
    def _(slot):
        give(2, slot, rest_back(2 * slot + 1 - b))

    for slot in range(2):
        turn_rows(first_turned, first_low, 2 * slot + 1 - b)
    run("r0")

    @pl.loop(0, 2)
    def _(slot):
        quarter = 2 * slot + b
        own = rest_back(quarter)
        upstream = back_rows[slot] + own + take(2, slot)
        normed = hat_first[slot]
        back = norm_pull(upstream, normed, fac_first[slot], vector(1))
        back_rows[slot] = back
        branch_low[quarter] = back.astype(BF16)
        share(2, slot, branch_low)
        vgrad[3:4, :] += row_sum(upstream * normed)
        vgrad[4:5, :] += row_sum(upstream)
        vgrad[5:6, :] += row_sum(back)

    run("r1")
    for side in sides:
        @pl.loop(0, 3)
        def _(part):
            rows = pl.ds(pl.multiple_of(part * TILE, TILE), TILE)
            right = slope[side].reshape(4 * TILE, 768)
            wide[side, 0, rows, :] = dims(first_turned[rows, :], right, 1, 0).astype(BF16)
        if side is sides[0]:
            scatter_first(2)
    scatter_start(2)
    run("r2")

    for slot in range(2):
        shared(2, slot, branch_low)

    @pl.loop(0, 4)
    def _(quarter):
        rows = pl.ds(pl.multiple_of(quarter * TILE, TILE), TILE)
        block = dims(branch_low[quarter], w_out[...], 1, 0).astype(BF16)
        for pair in range(3):
            mixed_back[pair, rows, :] = block[:, 128 * pair : 128 * pair + 128]

    run("r3")

    @pl.loop(0, 3)
    def _(part):
        rows = pl.ds(pl.multiple_of(part * TILE, TILE), TILE)
        right = jnp.concatenate([mixed[pair] for pair in range(3)], 1)
        out_grad[rows, :] = dims(tall(branch_low, rows), right, 0, 0).astype(BF16)
    run("r4")

    def heads_grad(pair, rows):
        right = jnp.concatenate([heads_back[3 * kind + pair] for kind in range(3)], 1)
        return dims(tokens_turned[rows, :], right, 1, 0)

    def first_heads_grad(side):
        @pl.loop(0, 3)
        def _(part):
            rows = pl.ds(pl.multiple_of(part * TILE, TILE), TILE)
            wide[side, 1, rows, 0:384] = heads_grad(side, rows).astype(BF16)

    @pl.loop(0, 12)
    def _(step):
        pair, part = step // 4, step % 4

        @pl.when(part == 0)
        def _():
            pick = (
                lax.broadcasted_iota(jnp.int32, (8, 128), 1) // HEAD_DIM
                == lax.broadcasted_iota(jnp.int32, (8, 128), 0)
            )
            pick = jnp.where(pick, 1.0, 0.0).astype(BF16)
            product = mixed[pair].astype(F32) * mixed_back[pair].astype(F32)
            high = product.astype(BF16)
            rest = (product - high.astype(F32)).astype(BF16)
            centre[...] = dims(pick, high, 1, 1) + dims(pick, rest, 1, 1)
            key_sum[...] = jnp.zeros_like(key_sum)
            value_sum[...] = jnp.zeros_like(value_sum)

        cols = pl.ds(pl.multiple_of(part * TILE, TILE), TILE)
        query_block, back_block = heads[pair, cols, :], mixed_back[pair, cols, :]
        value_block = heads[6 + pair]
        weights, score_backs, queries, backs, query_back = [], [], [], [], []
        for head in range(2):
            query_head, back_head = of_head(query_block, head), of_head(back_block, head)
            bias = bias_k[pair, head, :, cols] - lse[pair, head, :, cols]
            scores = dims(heads[3 + pair], query_head, 1, 1).reshape(16, BLOCK, TILE)
            scores = scores * (SCORE_SCALE * LOG2E) + bias.reshape(16, 1, TILE)
            weight = jnp.exp2(scores.reshape(1024, TILE))
            weight_back = dims(value_block, back_head, 1, 1)
            score_back = (weight * (weight_back - centre[head : head + 1, cols])).astype(BF16)
            weights.append(weight.astype(BF16))
            score_backs.append(score_back)
            queries.append(query_head)
            backs.append(back_head)
            query_back.append(dims(keys_turned[pair], score_back, 1, 0))
        value_sum[...] += dims(jnp.concatenate(weights, 1), jnp.concatenate(backs, 0), 1, 0)
        key_sum[...] += dims(jnp.concatenate(score_backs, 1), jnp.concatenate(queries, 0), 1, 0)
        query_grad = jnp.where(top, query_back[0], query_back[1]).T * SCORE_SCALE
        heads_back[pair, cols, :] = query_grad.astype(BF16)

        @pl.when(part == 3)
        def _():
            heads_back[3 + pair] = (key_sum[...] * SCORE_SCALE).astype(BF16)
            heads_back[6 + pair] = value_sum[...].astype(BF16)

        @pl.when(step == 7)
        def _():
            for side in range(2):
                first_heads_grad(side)
            scatter_first(0)
            scatter_start(0)

        run_at(step, "k", 12)

    @pl.loop(0, 3)
    def _(part):
        rows = pl.ds(pl.multiple_of(part * TILE, TILE), TILE)
        first, second = packs_of(heads_grad(2, rows), out_grad[rows, :].astype(F32))
        wide[0, 1, rows, 384:768] = first.astype(BF16)
        wide[1, 1, rows, 384:768] = second.astype(BF16)

    scatter_first(1)
    scatter_start(1)
    run("t0")
    for pair in range(3):
        vgrad[8:9, 128 * pair : 128 * pair + 128] = row_sum(heads_back[pair].astype(F32))
        vgrad[8:9, 384 + 128 * pair : 512 + 128 * pair] = row_sum(heads_back[6 + pair].astype(F32))
    send(M_VG, vgrad, vrecv.at[0], core_dev)

    def input_part(quarter):
        return sum(
            dims(beside(heads_back, (pair, 3 + pair, 6 + pair), quarter), w_in[pair], 1, 1)
            for pair in range(3)
        )

    given(1)

    @pl.loop(0, 2)
    def _(slot):
        give(3, slot, input_part(2 * slot + 1 - b))

    run("t1")
    arrived(M_VG, vrecv.at[0])
    mine = lax.broadcasted_iota(jnp.int32, (16, 768), 0) < 6
    vsend[0] = vgrad[...] + jnp.where(mine, vrecv[0], 0.0)
    send(M_VG + 1, vsend.at[0], vrecv.at[1], x_dev)

    @pl.loop(0, 2)
    def _(slot):
        own = input_part(2 * slot + b)
        back_rows[slot] = back_rows[slot] + own + take(3, slot)

    cots[0] = back_rows[1 - a].astype(BF16)
    send(M_GRAD, cots.at[0], cots.at[1], x_dev)
    store_far(21, back_rows.at[a], grad_ref.at[a]).start()
    arrived(M_VG + 1, vrecv.at[1])
    vsend[1] = vsend[0] + vrecv[1]
    send(M_VG + 2, vsend.at[1], vrecv.at[2], y_dev)
    run("t2")
    arrived(M_VG + 2, vrecv.at[2])
    vsend[2] = vsend[1] + vrecv[2]
    for j in range(1, 4):
        send(M_VG + 2 + j, vsend.at[2], vrecv.at[2 + j], z_dev(j))
    for pack in (3, 4, 2, 0):
        scatter_end(pack)
    run("t3")
    every = vsend[2]
    for j in range(1, 4):
        arrived(M_VG + 2 + j, vrecv.at[2 + j])
        every = every + vrecv[2 + j]
    vout_ref[...] = pltpu.roll(every, (8 - dp) % 8 * 96, 1)
    heads_row = every[8:9, :]
    for kind in range(2):
        row = heads_row[:, 384 * kind : 384 * kind + 384]
        low_row = low_lanes((1, 128))
        third = jnp.where(a == 0, row[:, 256:384], half_turn(row[:, 256:384]))
        both = jnp.concatenate(
            (jnp.where(a == 0, row[:, :128], row[:, 128:256]), jnp.where(low_row, third, 0.0)), 1
        )
        vout_ref[8 + kind : 9 + kind, 0:256] = pltpu.roll(both, (256 - dp * 24) % 256, 1)
    vout_ref[6:7, :] = jnp.where(a == 0, vout_ref[6:7, :], vout_ref[7:8, :])
    arrived(M_GRAD, cots.at[1])
    hat_first[0] = cots[1].astype(F32)
    store_far(22, hat_first.at[0], grad_ref.at[1 - a]).start()
    arrived(M_OUT, out_ref.at[1 - a])
    scatter_end(1)

    store_far(20, swap_out.at[a], out_ref.at[a]).wait()
    store_far(21, back_rows.at[a], grad_ref.at[a]).wait()
    store_far(22, hat_first.at[0], grad_ref.at[1 - a]).wait()

    for pack in range(5):
        scatter_left(pack)
    given(2)
    given(3)
    left(M_MASK, mask_ref)
    left(M_IN, in_ref.at[0])
    left(M_COT, cot_ref.at[0])
    left(M_OUT, swap_out.at[0])
    left(M_GRAD, cots.at[0])
    for j in range(3):
        left(M_VZ + j, vec_ref)
    left(M_VY, vec_y.at[0])
    left(M_VX, vec_all.at[0])
    for slot in range(2):
        left(M_TOK + slot, tokens.at[0])
        for kind in range(3):
            left(M_ROWS + 2 * kind + slot, first_low.at[0])
    for index in range(6):
        left(M_VG + index, vsend.at[0])


def finish_kernel(
    gout_half,
    gout_wide,
    vout_ref,
    from_output,
    from_grad,
    query_ref,
    key_ref,
    value_ref,
    project_ref,
    up_ref,
    down_ref,
    query_bias_ref,
    value_bias_ref,
    second_gain_ref,
    second_shift_ref,
    down_bias_ref,
    first_gain_ref,
    first_shift_ref,
    out_bias_ref,
    up_bias_ref,
    to_output,
    to_grad,
):
    row_refs = (
        second_gain_ref,
        second_shift_ref,
        down_bias_ref,
        first_gain_ref,
        first_shift_ref,
        out_bias_ref,
        up_bias_ref,
    )
    to_output[...] = from_output[...]
    to_grad[...] = from_grad[...]
    first, last = gout_half[0], gout_half[1]
    query_ref[...] = jnp.concatenate((first[:, 0:128], last[:, 0:64]), 1)
    key_ref[...] = jnp.concatenate((first[:, 128:256], last[:, 64:128]), 1)
    value_ref[...] = jnp.concatenate((first[:, 256:384], last[:, 128:192]), 1)
    gap = jnp.zeros((32, 256), F32)
    project = jnp.concatenate((last[:, 256:384], last[:, 128:256]), 1)
    project = jnp.concatenate((project, gap), 0).T
    project_ref[0:128, :] = project[0:128, :96]
    project_ref[128:192, :] = project[192:256, :96]
    up_ref[...] = gout_wide[0]
    down_ref[...] = jnp.concatenate((gout_half[2], gout_half[3]), 1)
    query_bias_ref[...] = vout_ref[8, 0:24]
    value_bias_ref[...] = vout_ref[9, 0:24]
    for row, ref in enumerate(row_refs):
        ref[...] = vout_ref[row, 0:96]


def layer_call(weights, rows, biases, random_blocks, tokens, cotangent):
    vmem = pltpu.VMEM
    anywhere = pl.BlockSpec(memory_space=pltpu.VMEM)
    far = pl.BlockSpec(memory_space=pl.ANY)
    shape = jax.ShapeDtypeStruct
    def both(*dims_, kind=BF16):
        return (vmem((4,) + dims_ + (384,), kind), vmem((1,) + dims_ + (768,), kind))

    like = lambda array: vmem(array.shape, array.dtype)
    scratch = [
        *(like(array) for array in weights),
        tuple(like(array) for array in rows),
        *(like(array) for array in (*biases, random_blocks, tokens, cotangent)),
        vmem((2, 96, 384), BF16),
        vmem((16, 768), BF16),
        vmem((48, 128), BF16),
        vmem((2, 2, 768, 384), BF16),
        vmem((2, 2, 768, 768), BF16),
        vmem((3, 16, 768), BF16),
        vmem((2, 16, 768), BF16),
        vmem((2, 16, 768), BF16),
        vmem((2, 48, 128), BF16),
        vmem((4, TILE, 768), BF16),
        vmem((768, 4 * TILE), BF16),
        vmem((2, TILE, 768), BF16),
        vmem((3, 768, 384), BF16),
        vmem((768, 384), BF16),
        vmem((3, 2, 4, 4, 1024), F32),
        vmem((3, 2, 16, 1024), F32),
        vmem((9, 1024, 128), BF16),
        vmem((3, 128, 1024), BF16),
        vmem((3, 1024, 128), BF16),
        vmem((3, 2, 1, 1024), F32),
        vmem((8, 1024), F32),
        vmem((4, TILE, 768), BF16),
        vmem((768, 4 * TILE), BF16),
        vmem((4, TILE, 768), BF16),
        vmem((4, TILE, 768), BF16),
        vmem((2, TILE, 768), F32),
        vmem((2, TILE, 1), F32),
        vmem((2, TILE, 768), F32),
        vmem((2, 4, TILE, 768), BF16),
        vmem((2, 4, TILE, 768), BF16),
        vmem((TILE, 768), F32),
        vmem((2, 2, TILE, 768), BF16),
        vmem((2, 2, TILE, 768), BF16),
        vmem((3, 1024, 128), BF16),
        vmem((1024, 128), F32),
        vmem((1024, 128), F32),
        vmem((9, 1024, 128), BF16),
        vmem((768, 384), BF16),
        both(4, 48),
        both(4, 48),
        both(4, 96),
        both(4, 96),
        both(3, 96 - LEAN),
        both(3, 4, LEAN),
        both(96, kind=F32),
        vmem((2, TILE, 768), BF16),
        vmem((16, 768), F32),
        vmem((3, 16, 768), F32),
        vmem((6, 16, 768), F32),
        pltpu.SemaphoreType.DMA((MESSAGES,)),
        pltpu.SemaphoreType.DMA((MESSAGES,)),
        pltpu.SemaphoreType.DMA((24,)),
    ]
    return pl.pallas_call(
        layer_kernel,
        out_shape=(
            shape(tokens.shape, BF16),
            shape(tokens.shape, F32),
            shape((4, 96, 384), F32),
            shape((1, 96, 768), F32),
            shape((16, 768), F32),
        ),
        in_specs=[far] * 6 + [(far,) * 7] + [far] * 5,
        out_specs=(far,) * 2 + (anywhere,) * 3,
        scratch_shapes=scratch,
        compiler_params=pltpu.CompilerParams(
            collective_id=0, has_side_effects=True, vmem_limit_bytes=63 << 20
        ),
    )(*weights, rows, *biases, random_blocks, tokens, cotangent)


def local_fast(
    inputs,
    random_blocks,
    query_weight,
    query_bias,
    key_weight,
    value_weight,
    value_bias,
    out_weight,
    out_bias,
    first_gain,
    first_shift,
    up_weight,
    up_bias,
    down_weight,
    down_bias,
    second_gain,
    second_shift,
    cotangent,
):
    output, input_grad, half_grads, wide_grads, sums = layer_call(
        (query_weight, key_weight, value_weight, down_weight.T, up_weight, out_weight),
        (out_bias, first_gain, first_shift, down_bias, second_gain, second_shift, up_bias),
        (query_bias, value_bias),
        random_blocks.transpose(0, 2, 1),
        inputs,
        cotangent,
    )
    like = lambda array: jax.ShapeDtypeStruct(array.shape, F32)
    whole = pl.BlockSpec(memory_space=pltpu.VMEM)
    outs = (query_weight, key_weight, value_weight, out_weight, up_weight, up_weight)
    outs += (query_bias, value_bias)
    outs += (second_gain, second_shift, down_bias, first_gain, first_shift, out_bias, up_bias)
    done = pl.pallas_call(
        finish_kernel,
        out_shape=tuple(like(array) for array in outs)
        + tuple(jax.ShapeDtypeStruct(array.shape, array.dtype) for array in (output, input_grad)),
        in_specs=[whole] * 5,
        out_specs=(whole,) * (len(outs) + 2),
    )(half_grads, wide_grads, sums, output, input_grad)
    query_grad, key_grad, value_grad, out_grad, up_grad, down_grad = done[:6]
    query_bias_grad, value_bias_grad = done[6:8]
    second_gain_grad, second_shift_grad, down_bias_grad = done[8:11]
    first_gain_grad, first_shift_grad, out_bias_grad, up_bias_grad = done[11:15]
    output, input_grad = done[15:]
    return (
        output,
        input_grad,
        query_grad,
        query_bias_grad,
        key_grad,
        value_grad,
        value_bias_grad,
        out_grad,
        out_bias_grad,
        first_gain_grad,
        first_shift_grad,
        up_grad,
        up_bias_grad,
        down_grad.T,
        down_bias_grad,
        second_gain_grad,
        second_shift_grad,
    )


def solution(mesh):
    sizes = mesh.shape
    fast = sizes["dp"] == 8 and sizes["tensor"] == 4
    return jax.shard_map(
        local_fast if fast else local,
        mesh=mesh,
        in_specs=(
            P("dp", "tensor", None),
            P("tensor", None, None),
            P("dp", "tensor"),
            P(("tensor", "dp")),
            P("dp", "tensor"),
            P("dp", "tensor"),
            P(("tensor", "dp")),
            P("tensor", "dp"),
            P("dp"),
            P("dp"),
            P("dp"),
            P("dp", "tensor"),
            P(("tensor", "dp")),
            P("tensor", "dp"),
            P("dp"),
            P("dp"),
            P("dp"),
            P("dp", "tensor", None),
        ),
        out_specs=(
            P("dp", "tensor", None),
            P("dp", "tensor", None),
            P("dp", "tensor"),
            P(("tensor", "dp")),
            P("dp", "tensor"),
            P("dp", "tensor"),
            P(("tensor", "dp")),
            P("tensor", "dp"),
            P("dp"),
            P("dp"),
            P("dp"),
            P("dp", "tensor"),
            P(("tensor", "dp")),
            P("tensor", "dp"),
            P("dp"),
            P("dp"),
            P("dp"),
        ),
        check_vma=False,
    )
```

```python
from functools import partial

import jax
import jax.numpy as jnp
from jax import lax
from jax.experimental import pallas as pl
from jax.experimental.pallas import tpu as pltpu
from jax.sharding import PartitionSpec as P

HEAD_DIM = 64
BLOCK = 64


norm_eps = 1e-12


def gather_weights(shards):
    return (
        lax.all_gather(shards[0], "dp", axis=0, tiled=True),
        lax.all_gather(shards[1], "dp", axis=0, tiled=True),
        lax.all_gather(shards[2], "dp", axis=0, tiled=True),
        lax.all_gather(shards[3], "dp", axis=0, tiled=True),
        lax.all_gather(shards[4], "dp", axis=0, tiled=True),
        lax.all_gather(shards[5], "dp", axis=1, tiled=True),
        lax.all_gather(shards[6], "dp", axis=0, tiled=True),
        lax.all_gather(shards[7], "dp", axis=0, tiled=True),
        lax.all_gather(shards[8], "dp", axis=0, tiled=True),
        lax.all_gather(shards[9], "dp", axis=0, tiled=True),
        lax.all_gather(shards[10], "dp", axis=0, tiled=True),
        lax.all_gather(shards[11], "dp", axis=1, tiled=True),
        lax.all_gather(shards[12], "dp", axis=0, tiled=True),
        lax.all_gather(shards[13], "dp", axis=0, tiled=True),
        lax.all_gather(shards[14], "dp", axis=0, tiled=True),
    )


def reduce_grads(grads):
    return (
        lax.psum_scatter(grads[0], "dp", scatter_dimension=0, tiled=True),
        lax.psum_scatter(grads[1], "dp", scatter_dimension=0, tiled=True),
        lax.psum_scatter(grads[2], "dp", scatter_dimension=0, tiled=True),
        lax.psum_scatter(grads[3], "dp", scatter_dimension=0, tiled=True),
        lax.psum_scatter(grads[4], "dp", scatter_dimension=0, tiled=True),
        lax.psum_scatter(grads[5], "dp", scatter_dimension=1, tiled=True),
        lax.psum_scatter(grads[6], "dp", scatter_dimension=0, tiled=True),
        lax.psum_scatter(grads[7], "dp", scatter_dimension=0, tiled=True),
        lax.psum_scatter(grads[8], "dp", scatter_dimension=0, tiled=True),
        lax.psum_scatter(grads[9], "dp", scatter_dimension=0, tiled=True),
        lax.psum_scatter(grads[10], "dp", scatter_dimension=0, tiled=True),
        lax.psum_scatter(grads[11], "dp", scatter_dimension=1, tiled=True),
        lax.psum_scatter(grads[12], "dp", scatter_dimension=0, tiled=True),
        lax.psum_scatter(grads[13], "dp", scatter_dimension=0, tiled=True),
        lax.psum_scatter(grads[14], "dp", scatter_dimension=0, tiled=True),
    )


def full_rows(block):
    return lax.all_gather(block, "tensor", axis=0, tiled=True)


def column_sums(partial_terms):
    return lax.psum_scatter(
        partial_terms.astype(jnp.bfloat16), "tensor", scatter_dimension=0, tiled=True
    ).astype(jnp.float32)


def block_allowed(random_blocks, block_count):
    row_ids = jnp.arange(block_count, dtype=jnp.int32)[:, None]
    col_ids = jnp.arange(block_count, dtype=jnp.int32)[None, :]
    fixed = (
        (jnp.abs(row_ids - col_ids) <= 1)
        | (col_ids == 0)
        | (col_ids == block_count - 1)
        | (row_ids == 0)
        | (row_ids == block_count - 1)
    )
    picked = jnp.any(
        random_blocks[:, :, :, None]
        == jnp.arange(block_count, dtype=jnp.int32)[None, None, None, :],
        axis=2,
    )
    return fixed[None, :, :] | picked


def layer_norm(values, gain, shift):
    mean = jnp.mean(values, axis=1, keepdims=True)
    spread = jnp.mean(values * values, axis=1, keepdims=True) - mean * mean
    factor = lax.rsqrt(spread + norm_eps)
    normed = (values - mean) * factor
    return (normed * gain + shift, normed, factor)


def norm_back(upstream, normed, factor, gain):
    scaled = upstream * gain
    plain = jnp.mean(scaled, axis=1, keepdims=True)
    along = jnp.mean(scaled * normed, axis=1, keepdims=True)
    back = factor * (scaled - plain - normed * along)
    return (back, jnp.sum(upstream * normed, axis=0), jnp.sum(upstream, axis=0))


def row_parts(array, span):
    return array.reshape((array.shape[0] // span, span) + array.shape[1:])


def mask_parts(allowed, span):
    return allowed.reshape(allowed.shape[0], -1, span // BLOCK, allowed.shape[2]).transpose(
        1, 0, 2, 3
    )


def block_scores(query_block, key_heads, mask_block):
    products = jnp.einsum(
        "qhd,khd->hqk", query_block, key_heads, preferred_element_type=jnp.float32
    )
    head_count, row_count, key_count = products.shape
    scaled = (products * HEAD_DIM ** (-0.5)).reshape(
        head_count, row_count // BLOCK, BLOCK, key_count // BLOCK, BLOCK
    )
    masked = jnp.where(mask_block[:, :, None, :, None], scaled, -1000000000.0)
    return masked.reshape(head_count, row_count, key_count)


def attend(query_heads, key_heads, value_heads, allowed):
    length = query_heads.shape[0]
    span = min(512, length)

    def one_part(items):
        query_block, mask_block = items
        scores = block_scores(query_block, key_heads, mask_block)
        largest = jnp.max(scores, axis=-1, keepdims=True)
        log_total = largest + jnp.log(jnp.sum(jnp.exp(scores - largest), axis=-1, keepdims=True))
        weights_low = jnp.exp(scores - log_total).astype(jnp.bfloat16)
        mixed = jnp.einsum(
            "hqk,khd->qhd", weights_low, value_heads, preferred_element_type=jnp.float32
        )
        return (mixed, log_total[..., 0])

    mixed, log_totals = lax.map(one_part, (row_parts(query_heads, span), mask_parts(allowed, span)))
    return (mixed.reshape(length, -1).astype(jnp.bfloat16), log_totals)


def attend_back(query_heads, key_heads, value_heads, mixed_back, log_totals, allowed):
    length = query_heads.shape[0]
    span = min(512, length)

    def one_part(carry, items):
        key_sum, value_sum = carry
        query_block, back_block, log_total, mask_block = items
        scores = block_scores(query_block, key_heads, mask_block)
        weights = jnp.exp(scores - log_total[..., None])
        weights_low = weights.astype(jnp.bfloat16)
        weights_back = jnp.einsum(
            "qhd,khd->hqk", back_block, value_heads, preferred_element_type=jnp.float32
        )
        centre = jnp.sum(weights_back * weights, axis=-1, keepdims=True)
        scores_back = (weights * (weights_back - centre) * HEAD_DIM ** (-0.5)).astype(jnp.bfloat16)
        query_back = jnp.einsum(
            "hqk,khd->qhd", scores_back, key_heads, preferred_element_type=jnp.float32
        )
        key_sum = key_sum + jnp.einsum(
            "hqk,qhd->khd", scores_back, query_block, preferred_element_type=jnp.float32
        )
        value_sum = value_sum + jnp.einsum(
            "hqk,qhd->khd", weights_low, back_block, preferred_element_type=jnp.float32
        )
        return ((key_sum, value_sum), query_back)

    empty = jnp.zeros(key_heads.shape, jnp.float32)
    (key_back, value_back), query_back = lax.scan(
        one_part,
        (empty, empty),
        (
            row_parts(query_heads, span),
            row_parts(mixed_back, span),
            log_totals,
            mask_parts(allowed, span),
        ),
    )
    return (
        query_back.reshape(length, -1).astype(jnp.bfloat16),
        key_back.reshape(length, -1).astype(jnp.bfloat16),
        value_back.reshape(length, -1).astype(jnp.bfloat16),
    )


def forward_pass(weights, token_block, allowed):
    (
        query_weight,
        query_bias,
        key_weight,
        value_weight,
        value_bias,
        out_weight,
        out_bias,
        first_gain,
        first_shift,
        up_weight,
        up_bias,
        down_weight,
        down_bias,
        second_gain,
        second_shift,
    ) = weights
    token_rows = full_rows(token_block)
    length = token_rows.shape[0]

    def heads_of(product):
        return product.astype(jnp.bfloat16).reshape(length, -1, HEAD_DIM)

    query_heads = heads_of(
        jnp.dot(token_rows, query_weight, preferred_element_type=jnp.float32) + query_bias
    )
    key_heads = heads_of(jnp.dot(token_rows, key_weight, preferred_element_type=jnp.float32))
    value_heads = heads_of(
        jnp.dot(token_rows, value_weight, preferred_element_type=jnp.float32) + value_bias
    )
    mixed, log_totals = attend(query_heads, key_heads, value_heads, allowed)
    branch_terms = jnp.dot(mixed, out_weight, preferred_element_type=jnp.float32)
    hidden = token_block.astype(jnp.float32) + column_sums(branch_terms) + out_bias
    first_norm, first_normed, first_factor = layer_norm(hidden, first_gain, first_shift)
    first_rows = full_rows(first_norm.astype(jnp.bfloat16))
    inner = jnp.dot(first_rows, up_weight, preferred_element_type=jnp.float32) + up_bias
    active = jax.nn.gelu(inner, approximate=False).astype(jnp.bfloat16)
    second_in = (
        first_norm
        + column_sums(jnp.dot(active, down_weight, preferred_element_type=jnp.float32))
        + down_bias
    )
    result, second_normed, second_factor = layer_norm(second_in, second_gain, second_shift)
    kept = (
        token_rows,
        query_heads,
        key_heads,
        value_heads,
        log_totals,
        mixed,
        first_normed,
        first_factor,
        first_rows,
        inner,
        active,
        second_normed,
        second_factor,
    )
    return (result, kept)


def backward_pass(weights, kept, upstream_block, allowed):
    (
        query_weight,
        query_bias,
        key_weight,
        value_weight,
        value_bias,
        out_weight,
        out_bias,
        first_gain,
        first_shift,
        up_weight,
        up_bias,
        down_weight,
        down_bias,
        second_gain,
        second_shift,
    ) = weights
    (
        token_rows,
        query_heads,
        key_heads,
        value_heads,
        log_totals,
        mixed,
        first_normed,
        first_factor,
        first_rows,
        inner,
        active,
        second_normed,
        second_factor,
    ) = kept
    length = token_rows.shape[0]
    upstream = upstream_block.astype(jnp.float32)
    second_back, second_gain_grad, second_shift_grad = norm_back(
        upstream, second_normed, second_factor, second_gain
    )
    down_bias_grad = jnp.sum(second_back, axis=0)
    feed_rows = full_rows(second_back.astype(jnp.bfloat16))
    down_weight_grad = jnp.einsum(
        "tf,td->fd", active, feed_rows, preferred_element_type=jnp.float32
    )
    active_back = jnp.einsum(
        "td,fd->tf", feed_rows, down_weight, preferred_element_type=jnp.float32
    )
    inner_back = jax.vjp(partial(jax.nn.gelu, approximate=False), inner)[1](active_back)[0].astype(
        jnp.bfloat16
    )
    up_bias_grad = jnp.sum(inner_back, axis=0, dtype=jnp.float32)
    up_weight_grad = jnp.einsum(
        "td,tf->df", first_rows, inner_back, preferred_element_type=jnp.float32
    )
    first_back = second_back + column_sums(
        jnp.einsum("tf,df->td", inner_back, up_weight, preferred_element_type=jnp.float32)
    )
    hidden_back, first_gain_grad, first_shift_grad = norm_back(
        first_back, first_normed, first_factor, first_gain
    )
    out_bias_grad = jnp.sum(hidden_back, axis=0)
    branch_rows = full_rows(hidden_back.astype(jnp.bfloat16))
    out_weight_grad = jnp.einsum(
        "tc,td->cd", mixed, branch_rows, preferred_element_type=jnp.float32
    )
    mixed_back = jnp.einsum(
        "td,cd->tc", branch_rows, out_weight, preferred_element_type=jnp.float32
    ).astype(jnp.bfloat16)
    query_back, key_back, value_back = attend_back(
        query_heads,
        key_heads,
        value_heads,
        mixed_back.reshape(length, -1, HEAD_DIM),
        log_totals,
        allowed,
    )
    query_weight_grad = jnp.einsum(
        "td,tc->dc", token_rows, query_back, preferred_element_type=jnp.float32
    )
    key_weight_grad = jnp.einsum(
        "td,tc->dc", token_rows, key_back, preferred_element_type=jnp.float32
    )
    value_weight_grad = jnp.einsum(
        "td,tc->dc", token_rows, value_back, preferred_element_type=jnp.float32
    )
    query_bias_grad = jnp.sum(query_back, axis=0, dtype=jnp.float32)
    value_bias_grad = jnp.sum(value_back, axis=0, dtype=jnp.float32)
    projected = (
        jnp.einsum("tc,dc->td", query_back, query_weight, preferred_element_type=jnp.float32)
        + jnp.einsum("tc,dc->td", key_back, key_weight, preferred_element_type=jnp.float32)
        + jnp.einsum("tc,dc->td", value_back, value_weight, preferred_element_type=jnp.float32)
    )
    input_back = hidden_back + column_sums(projected)
    grads = (
        query_weight_grad,
        query_bias_grad,
        key_weight_grad,
        value_weight_grad,
        value_bias_grad,
        out_weight_grad,
        out_bias_grad,
        first_gain_grad,
        first_shift_grad,
        up_weight_grad,
        up_bias_grad,
        down_weight_grad,
        down_bias_grad,
        second_gain_grad,
        second_shift_grad,
    )
    return (input_back, grads)


def local(
    inputs,
    random_blocks,
    query_weight,
    query_bias,
    key_weight,
    value_weight,
    value_bias,
    out_weight,
    out_bias,
    first_gain,
    first_shift,
    up_weight,
    up_bias,
    down_weight,
    down_bias,
    second_gain,
    second_shift,
    cotangent,
):
    shards = (
        query_weight,
        query_bias,
        key_weight,
        value_weight,
        value_bias,
        out_weight,
        out_bias,
        first_gain,
        first_shift,
        up_weight,
        up_bias,
        down_weight,
        down_bias,
        second_gain,
        second_shift,
    )
    allowed = block_allowed(random_blocks, random_blocks.shape[1])
    resident = gather_weights(shards)
    growth = lax.axis_size("dp")
    grown_dims = (0, 0, 0, 0, 0, 1, 0, 0, 0, 0, 0, 1, 0, 0, 0)
    start = tuple(
        (
            jnp.zeros(
                tuple(
                    (
                        extent * growth if position == grown_dim else extent
                        for position, extent in enumerate(shard.shape)
                    )
                ),
                jnp.float32,
            )
            for shard, grown_dim in zip(shards, grown_dims)
        )
    )

    def one_sequence(totals, items):
        token_block, upstream_block = items
        result, kept = forward_pass(resident, token_block, allowed)
        input_back, grads = backward_pass(resident, kept, upstream_block, allowed)
        totals = tuple((summed + update for summed, update in zip(totals, grads)))
        return (totals, (result.astype(jnp.bfloat16), input_back))

    totals, (results, input_backs) = lax.scan(one_sequence, start, (inputs, cotangent))
    shares = reduce_grads(totals)
    vectors = lax.psum(
        (shares[6], shares[7], shares[8], shares[12], shares[13], shares[14]), "tensor"
    )
    return (
        results,
        input_backs,
        shares[0],
        shares[1],
        shares[2],
        shares[3],
        shares[4],
        shares[5],
        vectors[0],
        vectors[1],
        vectors[2],
        shares[9],
        shares[10],
        shares[11],
        vectors[3],
        vectors[4],
        vectors[5],
    )


MESH = pl.DeviceIdType.MESH
(
    START,
    SPREAD,
    OVER_Y,
    OVER_X,
    DEEP,
    BACK_DEEP,
    BACK_Y,
    BACK_X,
    BACK_LINE,
    COT,
) = range(10)
PLAN = {
    "pre": (
        (START, 1, 0),
        (OVER_Y, 0, 0),
        (SPREAD, 0, 1),
        (OVER_Y, 1, 0),
        (SPREAD, 0, 2),
    ),
    "tok": (
        (SPREAD, 0, 3),
        (SPREAD, 1, 1),
        (OVER_X, 1, 0),
    ),
    "p0": (
        (OVER_X, 0, 1),
        (SPREAD, 1, 2),
        (OVER_X, 0, 0),
        (DEEP, 0, 0),
        (OVER_Y, 0, 3),
        (OVER_X, 0, 2),
        (OVER_Y, 0, 2),
        (OVER_Y, 0, 1),
        (START, 2, 0),
        (OVER_X, 0, 3),
        (OVER_Y, 1, 2),
        (DEEP, 1, 0),
        (START, 3, 0),
        (OVER_X, 1, 1),
        (OVER_X, 1, 2),
    ),
    "q0": (
        (SPREAD, 1, 3),
        (SPREAD, 2, 1),
    ),
    "q1": (
        (OVER_Y, 2, 0),
        (SPREAD, 2, 3),
        (OVER_X, 1, 3),
        (OVER_Y, 1, 3),
        (DEEP, 2, 0),
        (OVER_Y, 1, 1),
    ),
    "f1": (
        (OVER_X, 2, 0),
        (OVER_X, 2, 1),
        (SPREAD, 2, 2),
    ),
    "f3": (
        (OVER_Y, 2, 1),
        (OVER_X, 2, 3),
    ),
    "f4": (
        (COT, 0, 0),
    ),
    "f7": (
        (OVER_X, 3, 0),
    ),
    "p1": (
        (SPREAD, 3, 1),
    ),
    "f9": (
        (OVER_X, 2, 2),
    ),
    "f10": (
        (OVER_Y, 2, 3),
        (OVER_Y, 3, 0),
        (SPREAD, 3, 3),
    ),
    "f11": (
        (OVER_Y, 2, 2),
        (SPREAD, 3, 2),
    ),
    "b0": (
        (OVER_X, 3, 1),
        (OVER_Y, 3, 1),
    ),
    "b1": (
        (OVER_Y, 3, 3),
    ),
    "u0": (
        (OVER_X, 3, 3),
    ),
    "u1": (
        (OVER_X, 3, 2),
        (DEEP, 3, 0),
        (OVER_Y, 3, 2),
    ),
    "r0": (
        (BACK_X, 3, 2),
        (BACK_Y, 3, 3),
        (BACK_Y, 3, 2),
        (BACK_X, 4, 3),
        (BACK_X, 3, 3),
        (BACK_X, 4, 1),
        (BACK_DEEP, 3, 0),
        (BACK_Y, 4, 3),
        (BACK_X, 3, 1),
        (BACK_Y, 4, 1),
    ),
    "r1": (
        (BACK_LINE, 3, 2),
        (BACK_X, 4, 2),
        (BACK_DEEP, 4, 0),
    ),
    "r2": (
        (BACK_X, 3, 0),
        (BACK_X, 4, 0),
        (BACK_Y, 3, 1),
        (BACK_LINE, 3, 3),
        (BACK_Y, 3, 0),
    ),
    "r3": (
        (BACK_Y, 4, 2),
        (BACK_Y, 4, 0),
    ),
    "k0": (
        (BACK_LINE, 4, 3),
    ),
    "k1": (
        (BACK_X, 2, 2),
        (BACK_X, 2, 3),
    ),
    "k2": (
        (BACK_LINE, 3, 1),
    ),
    "k3": (
        (BACK_LINE, 4, 1),
        (BACK_Y, 2, 2),
        (BACK_LINE, 4, 2),
    ),
    "k4": (
        (BACK_X, 2, 1),
        (BACK_DEEP, 2, 0),
    ),
    "k5": (
        (BACK_Y, 2, 1),
        (BACK_Y, 2, 3),
    ),
    "k7": (
        (BACK_LINE, 2, 2),
        (BACK_Y, 2, 0),
    ),
    "k8": (
        (BACK_Y, 0, 2),
        (BACK_X, 2, 0),
    ),
    "k9": (
        (BACK_Y, 0, 3),
        (BACK_X, 0, 2),
    ),
    "k10": (
        (BACK_X, 0, 1),
    ),
    "k11": (
        (BACK_X, 0, 3),
    ),
    "t0": (
        (BACK_LINE, 3, 0),
        (BACK_LINE, 4, 0),
        (BACK_DEEP, 0, 0),
    ),
    "t1": (
        (BACK_LINE, 0, 2),
        (BACK_LINE, 2, 1),
        (BACK_Y, 0, 1),
        (BACK_LINE, 2, 3),
        (BACK_X, 1, 2),
        (BACK_X, 1, 3),
        (BACK_Y, 1, 1),
        (BACK_X, 0, 0),
        (BACK_X, 1, 1),
        (BACK_LINE, 2, 0),
        (BACK_Y, 1, 3),
    ),
    "t2": (
        (BACK_LINE, 0, 1),
        (BACK_Y, 1, 2),
        (BACK_LINE, 1, 1),
        (BACK_LINE, 0, 3),
        (BACK_Y, 0, 0),
        (BACK_LINE, 1, 2),
        (BACK_LINE, 1, 3),
        (BACK_DEEP, 1, 0),
        (BACK_LINE, 0, 0),
    ),
    "t3": (
        (BACK_X, 1, 0),
        (BACK_Y, 1, 0),
        (BACK_LINE, 1, 0),
    ),
}
F32 = jnp.float32
BF16 = jnp.bfloat16
LOG2E = 1.4426950408889634
SCORE_SCALE = HEAD_DIM ** (-0.5)
TILE = 256
MESSAGES = 272
LEAN = 16
TURN = 32
BEND = 48


def dims(left, right, left_dim, right_dim):
    return lax.dot_general(
        left, right, (((left_dim,), (right_dim,)), ((), ())), preferred_element_type=F32
    )


def low_lanes(shape):
    return lax.broadcasted_iota(jnp.int32, shape, len(shape) - 1) < HEAD_DIM


def half_turn(block):
    return pltpu.roll(block.astype(F32), HEAD_DIM, 1).astype(block.dtype)


def pairs_of(first, second):
    tile = lambda pack, index: pack[:, 128 * index : 128 * index + 128]
    low = low_lanes((first.shape[0], 128))
    e0, e1, f0, f1 = tile(first, 0), tile(second, 0), tile(first, 1), tile(second, 1)
    third = (
        jnp.where(low, e0, half_turn(e1)),
        jnp.where(low, half_turn(e0), e1),
        jnp.where(low, f0, half_turn(f1)),
    )
    out = (tile(first, 2), tile(second, 2), jnp.where(low, half_turn(f0), f1))
    return jnp.concatenate(third, 1), jnp.concatenate(out, 1)


def packs_of(third, out):
    tile = lambda block, index: block[:, 128 * index : 128 * index + 128]
    query, key, value = (tile(third, index) for index in range(3))
    low = low_lanes(query.shape)
    first = (
        jnp.where(low, query, half_turn(key)),
        jnp.where(low, value, half_turn(tile(out, 2))),
        tile(out, 0),
    )
    second = (
        jnp.where(low, half_turn(query), key),
        jnp.where(low, half_turn(value), tile(out, 2)),
        tile(out, 1),
    )
    return jnp.concatenate(first, 1), jnp.concatenate(second, 1)


def norm_of(values):
    mean = jnp.mean(values, axis=1, keepdims=True)
    spread = jnp.mean(values * values, axis=1, keepdims=True) - mean * mean
    factor = lax.rsqrt(spread + norm_eps)
    return (values - mean) * factor, factor


def norm_pull(upstream, normed, factor, gain):
    scaled = upstream * gain
    plain = jnp.mean(scaled, axis=1, keepdims=True)
    along = jnp.mean(scaled * normed, axis=1, keepdims=True)
    return factor * (scaled - plain - normed * along)


def row_sum(block):
    return jnp.sum(block, axis=0, keepdims=True)


def layer_kernel(
    query_far,
    key_far,
    value_far,
    down_far,
    up_far,
    project_far,
    rows_far,
    query_bias_far,
    value_bias_far,
    picks_far,
    in_far,
    cot_far,
    out_ref,
    grad_ref,
    gout_half,
    gout_wide,
    vout_ref,
    query_ref,
    key_ref,
    value_ref,
    down_ref,
    up_ref,
    project_ref,
    row_refs,
    query_bias_ref,
    value_bias_ref,
    picks_ref,
    in_ref,
    cot_ref,
    pack_ref,
    vec_ref,
    mask_ref,
    half,
    wide,
    vec_z,
    vec_y,
    vec_all,
    masks,
    tokens,
    tokens_turned,
    cots,
    w_in,
    w_out,
    bias_q,
    bias_k,
    heads,
    keys_turned,
    mixed,
    lse,
    centre,
    first_low,
    first_turned,
    feed_low,
    branch_low,
    hat_first,
    fac_first,
    back_rows,
    active,
    slope,
    inner_buf,
    send_buf,
    recv_buf,
    mixed_back,
    key_sum,
    value_sum,
    heads_back,
    out_grad,
    diag_x,
    diag_y,
    near_x,
    near_y,
    near_z,
    deep_z,
    total,
    swap_out,
    vgrad,
    vsend,
    vrecv,
    send_sem,
    recv_sem,
    local_sem,
):
    dp, tensor = lax.axis_index("dp"), lax.axis_index("tensor")
    z, y = dp // 2, dp % 2
    a, b = tensor // 2, tensor % 2
    core_dev = (dp, tensor + 1 - 2 * b)
    x_dev = (dp, tensor + 2 - 4 * a)
    y_dev = (dp + 1 - 2 * y, tensor)

    def z_at(shift):
        return (z + shift) % 4

    def z_dev(shift):
        return (z_at(shift) * 2 + y, tensor)

    barrier = pltpu.get_barrier_semaphore()
    for dev in (core_dev, x_dev, y_dev, z_dev(1), z_dev(2), z_dev(3)):
        pl.semaphore_signal(barrier, inc=1, device_id=dev, device_id_type=MESH)
    loads = [
        (query_far, query_ref),
        (key_far, key_ref),
        (value_far, value_ref),
        (in_far, in_ref),
        (project_far, project_ref),
        (picks_far, picks_ref),
        (query_bias_far, query_bias_ref),
        (value_bias_far, value_bias_ref),
        *zip(rows_far, row_refs),
        (up_far, up_ref),
        (down_far, down_ref),
        (cot_far, cot_ref),
    ]
    loads = [
        pltpu.make_async_copy(src, goal, local_sem.at[index])
        for index, (src, goal) in enumerate(loads)
    ]
    for load in loads:
        load.start()

    def store_far(index, src, goal):
        return pltpu.make_async_copy(src, goal, local_sem.at[index])

    for load in loads:
        load.wait()

    def copy(index, src, dst, dev):
        return pltpu.make_async_remote_copy(
            src_ref=src,
            dst_ref=dst,
            send_sem=send_sem.at[index],
            recv_sem=recv_sem.at[index],
            device_id=dev,
            device_id_type=MESH,
        )

    def send(index, src, dst, dev):
        copy(index, src, dst, dev).start()

    def arrived(index, region):
        copy(index, region, region, core_dev).wait_recv()

    def left(index, region):
        copy(index, region, region, core_dev).wait_send()

    def store(pack):
        return (half, wide)[pack // 2], pack % 2

    def chip_rows(chip, start=0, size=96):
        first = pl.multiple_of(chip * 96, 16) + start
        return pl.ds(pl.multiple_of(first, 16), size)

    def piece(side, pack, chip, start=0, size=96):
        ref, slot = store(pack)
        return ref.at[side, slot, chip_rows(chip, start, size), :]

    def back_store(pack):
        if pack == 2:
            return wide, 0, slice(0, 768)
        if pack > 2:
            return half, pack - 3, slice(0, 384)
        return wide, 1, slice(384 * pack, 384 * pack + 384)

    def back_piece(side, pack, chip, start=0, size=96):
        ref, slot, cols = back_store(pack)
        return ref.at[side, slot, chip_rows(chip, start, size), cols]

    def part_of(refs, pack):
        return refs[1].at[0] if pack == 2 else refs[0].at[(0, 1, None, 2, 3)[pack]]

    def gather_id(pack, kind, j):
        return pack * 28 + 4 * kind + j

    def scatter_id(pack, kind, i):
        return 112 + pack * 24 + 4 * kind + i

    M_IN, M_COT, M_MASK, M_VZ, M_VY, M_VX = 232, 233, 234, 235, 238, 239
    M_TOK, M_OUT, M_GRAD, M_VG = 240, 242, 243, 244
    M_ROWS, M_PART = 250, 256
    Z_OWN, X_NEAR, Y_NEAR, X_CORNER, Y_CORNER, Z_X, Z_Y = range(7)

    def corner_id(pack, j):
        return gather_id(pack, (Z_OWN, Z_X, Z_Y)[j - 1], 0)

    D_X, D_Y, N_X, N_Y, L_Z, Q_Z = range(6)

    def gather_start(pack):
        own = (pack_ref.at[0], pack_ref.at[1], up_ref, down_ref)[pack]
        for j in (1, 3, 2):
            send(gather_id(pack, Z_OWN, j), own, piece(a, pack, dp), z_dev(j))
        send(gather_id(pack, X_NEAR, 0), own, piece(a, pack, dp), x_dev)
        send(gather_id(pack, Y_NEAR, 0), own, piece(a, pack, dp), y_dev)
        ref, slot = store(pack)
        ref[a, slot, chip_rows(dp), :] = own[...]

    def gather_spread(pack, j):
        chip = z_at(-j) * 2 + y
        arrived(gather_id(pack, Z_OWN, j), piece(a, pack, chip))
        spot = piece(a, pack, chip, LEAN, 96 - LEAN)
        send(gather_id(pack, X_NEAR, j), spot, spot, x_dev)
        send(gather_id(pack, Y_NEAR, j), spot, spot, y_dev)

    def gather_over_y(pack, j):
        first = 0 if j == 0 else LEAN
        chip = z_at(-j) * 2 + 1 - y
        arrived(gather_id(pack, Y_NEAR, j), piece(a, pack, chip, first, 96 - first))
        spot = piece(a, pack, chip, first, TURN - first)
        send(gather_id(pack, X_CORNER, j), spot, spot, x_dev)
        if j == 0:
            for step in (1, 3, 2):
                spot = piece(a, pack, chip, 0, LEAN)
                send(gather_id(pack, Z_Y, step), spot, spot, z_dev(step))

    def gather_over_x(pack, j):
        first = 0 if j == 0 else LEAN
        chip = z_at(-j) * 2 + y
        arrived(gather_id(pack, X_NEAR, j), piece(1 - a, pack, chip, first, 96 - first))
        spot = piece(1 - a, pack, chip, TURN, 96 - TURN)
        send(gather_id(pack, Y_CORNER, j), spot, spot, y_dev)
        if j == 0:
            for step in (1, 3, 2):
                spot = piece(1 - a, pack, chip, 0, LEAN)
                send(gather_id(pack, Z_X, step), spot, spot, z_dev(step))

    def gather_deep(pack, _):
        chip = z * 2 + 1 - y
        arrived(gather_id(pack, X_CORNER, 0), piece(1 - a, pack, chip, 0, TURN))
        spot = piece(1 - a, pack, chip, 0, LEAN)
        for step in (1, 3, 2):
            send(corner_id(pack, step), spot, spot, z_dev(step))

    def gather_end(pack):
        for j in range(4):
            over_y, over_x = z_at(-j) * 2 + 1 - y, z_at(-j) * 2 + y
            arrived(gather_id(pack, Y_CORNER, j), piece(1 - a, pack, over_y, TURN, 96 - TURN))
            if j > 0:
                arrived(gather_id(pack, X_CORNER, j), piece(1 - a, pack, over_y, LEAN, TURN - LEAN))
                arrived(gather_id(pack, Z_Y, j), piece(a, pack, over_y, 0, LEAN))
                arrived(gather_id(pack, Z_X, j), piece(1 - a, pack, over_x, 0, LEAN))
                arrived(corner_id(pack, j), piece(1 - a, pack, over_y, 0, LEAN))

    def gather_left(pack):
        def rows(size):
            return piece(a, pack, dp, 0, size)

        for j in range(4):
            first = 0 if j == 0 else LEAN
            left(gather_id(pack, X_NEAR, j), rows(96 - first))
            left(gather_id(pack, Y_NEAR, j), rows(96 - first))
            left(gather_id(pack, X_CORNER, j), rows(TURN - first))
            left(gather_id(pack, Y_CORNER, j), rows(96 - TURN))
            if j > 0:
                left(gather_id(pack, Z_OWN, j), rows(96))
                left(gather_id(pack, Z_Y, j), rows(LEAN))
                left(gather_id(pack, Z_X, j), rows(LEAN))
                left(corner_id(pack, j), rows(LEAN))

    def add_to(side, pack, chip, start, *blocks):
        ref, slot, cols = back_store(pack)
        rows = chip_rows(chip, start, blocks[0].shape[0])
        summed = ref[side, slot, rows, cols].astype(F32)
        for block in blocks:
            summed = summed + block.astype(F32)
        ref[side, slot, rows, cols] = summed.astype(BF16)

    def scatter_corner(pack, i):
        first = 0 if i == 0 else LEAN
        chip = z_at(i) * 2 + 1 - y
        over_x = part_of(diag_x, pack).at[i, pl.ds(0, BEND - first), :]
        send(scatter_id(pack, D_X, i), back_piece(1 - a, pack, chip, first, BEND - first), over_x, x_dev)
        over_y = part_of(diag_y, pack).at[i]
        send(scatter_id(pack, D_Y, i), back_piece(1 - a, pack, chip, BEND, 96 - BEND), over_y, y_dev)

    def scatter_first(pack):
        for i in (2, 1, 3):
            scatter_corner(pack, i)

    def scatter_start(pack):
        for i in (2, 1, 3):
            for side in range(2):
                for line in range(2):
                    spot = back_piece(side, pack, z_at(i) * 2 + line, 0, LEAN)
                    slot = part_of(deep_z, pack).at[i - 1, 2 * side + line]
                    send(scatter_id(pack, Q_Z, i), spot, slot, z_dev(i))

    def scatter_deep(pack, _):
        parts = part_of(deep_z, pack)
        for i in range(1, 4):
            arrived(scatter_id(pack, Q_Z, i), parts.at[i - 1])
        for side in range(2):
            for line in range(2):
                terms = [parts[i, 2 * side + line] for i in range(3)]
                add_to(side, pack, z * 2 + line, 0, *terms)
        scatter_corner(pack, 0)

    def scatter_near_y(pack, i):
        first = 0 if i == 0 else LEAN
        chip = z_at(i) * 2 + 1 - y
        over_x = part_of(diag_x, pack).at[i, pl.ds(0, BEND - first), :]
        arrived(scatter_id(pack, D_X, i), over_x)
        add_to(a, pack, chip, first, over_x[...])
        spot = back_piece(a, pack, chip, first, 96 - first)
        goal = part_of(near_y, pack).at[i, pl.ds(0, 96 - first), :]
        send(scatter_id(pack, N_Y, i), spot, goal, y_dev)

    def scatter_near_x(pack, i):
        first = 0 if i == 0 else LEAN
        chip = z_at(i) * 2 + y
        over_y = part_of(diag_y, pack).at[i]
        arrived(scatter_id(pack, D_Y, i), over_y)
        add_to(1 - a, pack, chip, BEND, over_y[...])
        spot = back_piece(1 - a, pack, chip, first, 96 - first)
        goal = part_of(near_x, pack).at[i, pl.ds(0, 96 - first), :]
        send(scatter_id(pack, N_X, i), spot, goal, x_dev)

    def scatter_line(pack, i):
        first = 0 if i == 0 else LEAN
        size = 96 - first
        from_x = part_of(near_x, pack).at[i, pl.ds(0, size), :]
        from_y = part_of(near_y, pack).at[i, pl.ds(0, size), :]
        arrived(scatter_id(pack, N_X, i), from_x)
        arrived(scatter_id(pack, N_Y, i), from_y)
        chip = z_at(i) * 2 + y
        ref, slot, cols = back_store(pack)
        rows = chip_rows(chip, first, size)
        own = ref[a, slot, rows, cols].astype(F32) + from_x[...].astype(F32) + from_y[...].astype(F32)
        if i == 0:
            part_of(total, pack)[...] = own
        else:
            ref[a, slot, rows, cols] = own.astype(BF16)
            spot = back_piece(a, pack, chip, first, size)
            send(scatter_id(pack, L_Z, i), spot, part_of(near_z, pack).at[i - 1], z_dev(i))

    def scatter_end(pack):
        parts, sums = part_of(near_z, pack), part_of(total, pack)
        for i in range(1, 4):
            arrived(scatter_id(pack, L_Z, i), parts.at[i - 1])
        goal = part_of((gout_half, gout_wide), pack)
        goal[0:LEAN, :] = sums[0:LEAN, :]
        own = sums[LEAN:96, :]
        for i in range(3):
            own = own + parts[i].astype(F32)
        goal[LEAN:96, :] = own

    def scatter_left(pack):
        def rows(size):
            return back_piece(a, pack, dp, 0, size)

        for i in range(4):
            first = 0 if i == 0 else LEAN
            left(scatter_id(pack, D_X, i), rows(BEND - first))
            left(scatter_id(pack, D_Y, i), rows(96 - BEND))
            left(scatter_id(pack, N_X, i), rows(96 - first))
            left(scatter_id(pack, N_Y, i), rows(96 - first))
            if i > 0:
                left(scatter_id(pack, L_Z, i), rows(96 - LEAN))
                left(scatter_id(pack, Q_Z, i), rows(4 * LEAN))

    def send_cot(pack, _):
        send(M_COT, cot_ref.at[1 - a], cots.at[a], x_dev)

    moves = (
        lambda pack, _: gather_start(pack),
        gather_spread,
        gather_over_y,
        gather_over_x,
        gather_deep,
        scatter_deep,
        scatter_near_y,
        scatter_near_x,
        scatter_line,
        send_cot,
    )

    def run(label):
        for kind, pack, place in PLAN.get(label, ()):
            moves[kind](pack, place)

    def run_at(step, prefix, count):
        for index in range(count):
            if PLAN.get(prefix + str(index)):
                pl.when(step == index)(lambda: run(prefix + str(index)))

    def turned(ref):
        block = ref[...].astype(F32)
        gap = jnp.zeros((block.shape[0], 128 - block.shape[1]), F32)
        return jnp.concatenate((block, gap), 1).T[: block.shape[1], :].astype(BF16)

    def placed(rows, width):
        gap = jnp.zeros((rows.shape[0], width - rows.shape[1]), F32)
        return pltpu.roll(jnp.concatenate((rows, gap), 1), dp * rows.shape[1], 1)

    project = turned(project_ref)
    pack_ref[0] = jnp.concatenate((query_ref[:, :128], key_ref[:, :128], value_ref[:, :128]), 1)
    pack_ref[1] = jnp.concatenate(
        (
            query_ref[:, 128:],
            key_ref[:, 128:],
            value_ref[:, 128:],
            project[:, 128:],
            project[:, :128],
        ),
        1,
    )
    rows = jnp.concatenate([ref[...].reshape(1, 96).astype(F32) for ref in row_refs], 0)
    query_row = placed(query_bias_ref[...].reshape(1, 24).astype(F32), 256)
    value_row = placed(value_bias_ref[...].reshape(1, 24).astype(F32), 256)
    gap = jnp.zeros((1, 128), F32)
    in_row = jnp.concatenate(
        (query_row[:, :128], gap, value_row[:, :128], query_row[:, 128:], value_row[:, 128:], gap), 1
    )
    vec_ref[...] = jnp.concatenate((placed(rows, 768), in_row, jnp.zeros((8, 768), F32)), 0).astype(
        BF16
    )
    column = lax.broadcasted_iota(jnp.int32, (16, 128), 1)
    row = lax.broadcasted_iota(jnp.int32, (16, 128), 0)
    fixed = (
        ((column - row <= 1) & (row - column <= 1))
        | (column == 0)
        | (column == 15)
        | (row == 0)
        | (row == 15)
    )
    for head in range(3):
        allowed = fixed
        for pick in range(picks_ref.shape[1]):
            picks = picks_ref[head, pick : pick + 1, :]
            picks = jnp.concatenate((picks, jnp.full((1, 112), -1, jnp.int32)), 1)
            allowed = allowed | (picks == row)
        mask_ref[16 * head : 16 * head + 16, :] = jnp.where(allowed, 1.0, 0.0).astype(BF16)
    pl.semaphore_wait(barrier, 6)
    send(M_MASK, mask_ref, masks.at[a], x_dev)
    send(M_IN, in_ref.at[1 - a], tokens.at[tensor], x_dev)
    for j in range(1, 4):
        send(M_VZ + j - 1, vec_ref, vec_z.at[j - 1], z_dev(j))
    gather_start(0)
    tokens[tensor] = in_ref[a]
    masks[a] = mask_ref[...]
    cots[a] = cot_ref[a]
    send(M_TOK, tokens.at[tensor], tokens.at[tensor], core_dev)
    vec_own = vec_ref[...].astype(F32)
    for j in range(1, 4):
        arrived(M_VZ + j - 1, vec_z.at[j - 1])
        vec_own = vec_own + vec_z[j - 1].astype(F32)
    vec_y[0] = vec_own.astype(BF16)
    send(M_VY, vec_y.at[0], vec_y.at[1], y_dev)
    arrived(M_MASK, masks.at[1 - a])
    spread = (
        lax.broadcasted_iota(jnp.int32, (128, 16 * BLOCK), 1) // BLOCK
        == lax.broadcasted_iota(jnp.int32, (128, 16 * BLOCK), 0)
    )
    spread = jnp.where(spread, 1.0, 0.0).astype(BF16)
    for side in range(2):
        bias = (dims(masks[side], spread, 1, 0) - 1.0) * 1e9
        for head in range(3):
            pair, place = (side, head) if head < 2 else (2, side)
            bias_k[pair, place] = bias[16 * head : 16 * head + 16]
            rows = masks[side, 16 * head : 16 * head + 16, :]
            turned_bias = (dims(rows, spread[:16], 0, 0) - 1.0) * 1e9
            for part in range(4):
                bias_q[pair, place, part] = turned_bias[4 * part : 4 * part + 4]
    run("pre")
    arrived(M_VY, vec_y.at[1])
    vec_all[a] = (vec_own + vec_y[1].astype(F32)).astype(BF16)
    send(M_VX, vec_all.at[a], vec_all.at[a], x_dev)
    other = (tensor + 2) % 4
    arrived(M_IN, tokens.at[other])
    send(M_TOK + 1, tokens.at[other], tokens.at[other], core_dev)
    run("tok")

    def vector(row):
        return vec_all[0, row : row + 1, :].astype(F32)

    def turn_rows(goal, ref, quarter):
        cols = pl.ds(pl.multiple_of(quarter * TILE, TILE), TILE)
        goal[:, cols] = ref[quarter].astype(F32).T.astype(BF16)

    arrived(M_TOK, tokens.at[0])
    arrived(M_TOK + 1, tokens.at[0])

    @pl.loop(0, 4)
    def _(quarter):
        turn_rows(tokens_turned, tokens, quarter)

    def project_heads(pair, bias):
        @pl.loop(0, 4)
        def _(quarter):
            rows = pl.ds(pl.multiple_of(quarter * TILE, TILE), TILE)
            block = dims(tokens[quarter], w_in[pair], 1, 0) + bias
            for kind in range(3):
                tile = block[:, 128 * kind : 128 * kind + 128]
                heads[3 * kind + pair, rows, :] = tile.astype(BF16)
                if kind == 1:
                    keys_turned[pair, :, rows] = tile.T.astype(BF16)

    run("p0")
    gather_end(0)
    arrived(M_VX, vec_all.at[1 - a])
    for side in range(2):
        w_in[side] = half[side, 0]
        project_heads(side, vec_all[side, 7:8, 0:384].astype(F32))
        run("q" + str(side))

    def third_heads():
        run("p1")
        gather_end(1)

        @pl.loop(0, 3)
        def _(part):
            rows = pl.ds(pl.multiple_of(part * TILE, TILE), TILE)
            third, out = pairs_of(half[0, 1, rows, :], half[1, 1, rows, :])
            w_in[2, rows, :] = third
            w_out[rows, :] = out

        vecs = [vec_all[side, :, 384:768].astype(F32) for side in range(2)]
        project_heads(2, pairs_of(vecs[0], vecs[1])[0][7:8])

    low = low_lanes((TILE, 128))
    none = jnp.zeros((TILE, 128), BF16)
    top = lax.broadcasted_iota(jnp.int32, (128, TILE), 0) < HEAD_DIM

    def of_head(block, head):
        return jnp.where(low, block, none) if head == 0 else jnp.where(low, none, block)

    @pl.loop(0, 12)
    def _(step):
        pl.when(step == 8)(third_heads)
        pair, part = step // 4, step % 4
        cols = pl.ds(pl.multiple_of(part * TILE, TILE), TILE)
        query_block = heads[pair, cols, :]
        terms, sums, mosts = [], [], []
        for head in range(2):
            scores = dims(of_head(query_block, head), heads[3 + pair], 1, 1).reshape(4, BLOCK, 1024)
            bias = bias_q[pair, head, part].reshape(4, 1, 1024)
            scores = (scores * (SCORE_SCALE * LOG2E) + bias).reshape(TILE, 1024)
            most = jnp.max(scores, axis=1, keepdims=True)
            term = jnp.exp2(scores - most)
            sums.append(jnp.sum(term, axis=1, keepdims=True))
            terms.append(term.astype(BF16))
            mosts.append(most)
        both = dims(jnp.concatenate(terms, 0), heads[6 + pair], 1, 0)
        mixed[pair, cols, :] = jnp.where(low, both[:TILE] / sums[0], both[TILE:] / sums[1]).astype(BF16)
        totals = [most + jnp.log2(total) for most, total in zip(mosts, sums)]
        turned_totals = jnp.where(low, totals[0], totals[1]).T
        lse[pair, 0, :, cols] = turned_totals[0:1]
        lse[pair, 1, :, cols] = turned_totals[HEAD_DIM : HEAD_DIM + 1]
        run_at(step, "f", 12)

    def beside(ref, indices, quarter):
        rows = pl.ds(pl.multiple_of(quarter * TILE, TILE), TILE)
        return jnp.concatenate([ref[index, rows, :] for index in indices], 1)

    def give(number, slot, block):
        send_buf[number % 2, slot] = block.astype(BF16)
        index = M_PART + 2 * number + slot
        send(index, send_buf.at[number % 2, slot], recv_buf.at[number % 2, slot], core_dev)

    def take(number, slot):
        arrived(M_PART + 2 * number + slot, recv_buf.at[number % 2, slot])
        return recv_buf[number % 2, slot].astype(F32)

    def given(number):
        for slot in range(2):
            left(M_PART + 2 * number + slot, send_buf.at[number % 2, slot])

    def share(kind, slot, ref):
        spot = ref.at[2 * slot + b]
        send(M_ROWS + 2 * kind + slot, spot, spot, core_dev)

    def shared(kind, slot, ref):
        arrived(M_ROWS + 2 * kind + slot, ref.at[2 * slot + 1 - b])

    def branch_part(quarter):
        return dims(beside(mixed, range(3), quarter), w_out[...], 1, 1)

    @pl.loop(0, 2)
    def _(slot):
        give(0, slot, branch_part(2 * slot + 1 - b))

    run("b0")

    @pl.loop(0, 2)
    def _(slot):
        quarter = 2 * slot + b
        own = branch_part(quarter)
        hidden = tokens[quarter].astype(F32) + own + take(0, slot) + vector(0)
        normed, factor = norm_of(hidden)
        hat_first[slot] = normed
        fac_first[slot] = factor
        first_low[quarter] = (normed * vector(1) + vector(2)).astype(BF16)
        share(0, slot, first_low)

    run("b1")
    for slot in range(2):
        turn_rows(first_turned, first_low, 2 * slot + b)
    run("b2")
    gather_end(2)

    def feed_up(quarter):
        @pl.loop(0, 2)
        def _(side):
            inner_buf[...] = (
                dims(first_low[quarter], wide[side, 0], 1, 0)
                + vec_all[side, 6:7, :].astype(F32)
            )

            @pl.loop(0, TILE // 32)
            def _(chunk):
                rows = pl.ds(pl.multiple_of(chunk * 32, 32), 32)
                inner = inner_buf[rows, :]
                normal = 0.5 * (1.0 + lax.erf(inner * 0.7071067811865476))
                density = jnp.exp2(inner * inner * (-0.5 * LOG2E)) * 0.3989422804014327
                active[side, quarter, rows, :] = (inner * normal).astype(BF16)
                slope[side, quarter, rows, :] = (normal + inner * density).astype(BF16)

    def feed_down(quarter):
        return dims(active[0, quarter], wide[0, 1], 1, 1) + dims(active[1, quarter], wide[1, 1], 1, 1)

    feed_up(b)
    run("u0")
    feed_up(2 + b)
    run("u1")
    for slot in range(2):
        shared(0, slot, first_low)
        feed_up(2 * slot + 1 - b)
        run("u" + str(2 + slot))
    gather_end(3)

    @pl.loop(0, 2, unroll=True)
    def _(slot):
        give(1, slot, feed_down(2 * slot + 1 - b))

    arrived(M_COT, cots.at[1 - a])
    vgrad[...] = jnp.zeros_like(vgrad)

    @pl.loop(0, 2, unroll=True)
    def _(slot):
        quarter = 2 * slot + b
        own = feed_down(quarter)
        second_in = hat_first[slot] * vector(1) + vector(2) + own + take(1, slot) + vector(3)
        normed, factor = norm_of(second_in)
        swap_out[slot] = (normed * vector(4) + vector(5)).astype(BF16)
        upstream = cots[slot].astype(F32)
        back = norm_pull(upstream, normed, factor, vector(4))
        back_rows[slot] = back
        feed_low[quarter] = back.astype(BF16)
        share(1, slot, feed_low)
        vgrad[0:1, :] += row_sum(upstream * normed)
        vgrad[1:2, :] += row_sum(upstream)
        vgrad[2:3, :] += row_sum(back)

    store_far(20, swap_out.at[a], out_ref.at[a]).start()
    send(M_OUT, swap_out.at[1 - a], out_ref.at[a], x_dev)
    for pack in range(4):
        gather_left(pack)

    def feed_back(quarter):
        for side in range(2):
            block = dims(feed_low[quarter], wide[side, 1], 1, 0) * slope[side, quarter].astype(F32)
            inner_low = block.astype(BF16)
            slope[side, quarter] = inner_low
            vgrad[6 + side : 7 + side, :] += row_sum(inner_low.astype(F32))

    def rest_back(quarter):
        return dims(slope[0, quarter], wide[0, 0], 1, 1) + dims(slope[1, quarter], wide[1, 0], 1, 1)

    def tall(ref, cols):
        return ref[:, :, cols].reshape(4 * TILE, TILE)

    sides = (1 - a, a)

    def down_grad(side, part):
        @pl.loop(0, 3)
        def _(piece_rows):
            rows = pl.ds(pl.multiple_of(piece_rows * TILE, TILE), TILE)
            right = active[side, :, :, 384 * part : 384 * part + 384].reshape(4 * TILE, 384)
            half[side, part, rows, :] = dims(tall(feed_low, rows), right, 0, 0).astype(BF16)


    @pl.loop(0, 2)
    def _(slot):
        feed_back(2 * slot + b)

    for slot in range(2):
        shared(1, slot, feed_low)
    for part in range(2):
        down_grad(sides[0], part)
        scatter_first(3 + part)
        down_grad(sides[1], part)
        scatter_start(3 + part)

    @pl.loop(0, 2)
    def _(slot):
        feed_back(2 * slot + 1 - b)

    given(0)

    @pl.loop(0, 2)
    def _(slot):
        give(2, slot, rest_back(2 * slot + 1 - b))

    for slot in range(2):
        turn_rows(first_turned, first_low, 2 * slot + 1 - b)
    run("r0")

    @pl.loop(0, 2)
    def _(slot):
        quarter = 2 * slot + b
        own = rest_back(quarter)
        upstream = back_rows[slot] + own + take(2, slot)
        normed = hat_first[slot]
        back = norm_pull(upstream, normed, fac_first[slot], vector(1))
        back_rows[slot] = back
        branch_low[quarter] = back.astype(BF16)
        share(2, slot, branch_low)
        vgrad[3:4, :] += row_sum(upstream * normed)
        vgrad[4:5, :] += row_sum(upstream)
        vgrad[5:6, :] += row_sum(back)

    run("r1")
    for side in sides:
        @pl.loop(0, 3)
        def _(part):
            rows = pl.ds(pl.multiple_of(part * TILE, TILE), TILE)
            right = slope[side].reshape(4 * TILE, 768)
            wide[side, 0, rows, :] = dims(first_turned[rows, :], right, 1, 0).astype(BF16)
        if side is sides[0]:
            scatter_first(2)
    scatter_start(2)
    run("r2")

    for slot in range(2):
        shared(2, slot, branch_low)

    @pl.loop(0, 4)
    def _(quarter):
        rows = pl.ds(pl.multiple_of(quarter * TILE, TILE), TILE)
        block = dims(branch_low[quarter], w_out[...], 1, 0).astype(BF16)
        for pair in range(3):
            mixed_back[pair, rows, :] = block[:, 128 * pair : 128 * pair + 128]

    run("r3")

    @pl.loop(0, 3)
    def _(part):
        rows = pl.ds(pl.multiple_of(part * TILE, TILE), TILE)
        right = jnp.concatenate([mixed[pair] for pair in range(3)], 1)
        out_grad[rows, :] = dims(tall(branch_low, rows), right, 0, 0).astype(BF16)
    run("r4")

    def heads_grad(pair, rows):
        right = jnp.concatenate([heads_back[3 * kind + pair] for kind in range(3)], 1)
        return dims(tokens_turned[rows, :], right, 1, 0)

    def first_heads_grad(side):
        @pl.loop(0, 3)
        def _(part):
            rows = pl.ds(pl.multiple_of(part * TILE, TILE), TILE)
            wide[side, 1, rows, 0:384] = heads_grad(side, rows).astype(BF16)

    @pl.loop(0, 12)
    def _(step):
        pair, part = step // 4, step % 4

        @pl.when(part == 0)
        def _():
            pick = (
                lax.broadcasted_iota(jnp.int32, (8, 128), 1) // HEAD_DIM
                == lax.broadcasted_iota(jnp.int32, (8, 128), 0)
            )
            pick = jnp.where(pick, 1.0, 0.0).astype(BF16)
            product = mixed[pair].astype(F32) * mixed_back[pair].astype(F32)
            high = product.astype(BF16)
            rest = (product - high.astype(F32)).astype(BF16)
            centre[...] = dims(pick, high, 1, 1) + dims(pick, rest, 1, 1)
            key_sum[...] = jnp.zeros_like(key_sum)
            value_sum[...] = jnp.zeros_like(value_sum)

        cols = pl.ds(pl.multiple_of(part * TILE, TILE), TILE)
        query_block, back_block = heads[pair, cols, :], mixed_back[pair, cols, :]
        value_block = heads[6 + pair]
        weights, score_backs, queries, backs, query_back = [], [], [], [], []
        for head in range(2):
            query_head, back_head = of_head(query_block, head), of_head(back_block, head)
            bias = bias_k[pair, head, :, cols] - lse[pair, head, :, cols]
            scores = dims(heads[3 + pair], query_head, 1, 1).reshape(16, BLOCK, TILE)
            scores = scores * (SCORE_SCALE * LOG2E) + bias.reshape(16, 1, TILE)
            weight = jnp.exp2(scores.reshape(1024, TILE))
            weight_back = dims(value_block, back_head, 1, 1)
            score_back = (weight * (weight_back - centre[head : head + 1, cols])).astype(BF16)
            weights.append(weight.astype(BF16))
            score_backs.append(score_back)
            queries.append(query_head)
            backs.append(back_head)
            query_back.append(dims(keys_turned[pair], score_back, 1, 0))
        value_sum[...] += dims(jnp.concatenate(weights, 1), jnp.concatenate(backs, 0), 1, 0)
        key_sum[...] += dims(jnp.concatenate(score_backs, 1), jnp.concatenate(queries, 0), 1, 0)
        query_grad = jnp.where(top, query_back[0], query_back[1]).T * SCORE_SCALE
        heads_back[pair, cols, :] = query_grad.astype(BF16)

        @pl.when(part == 3)
        def _():
            heads_back[3 + pair] = (key_sum[...] * SCORE_SCALE).astype(BF16)
            heads_back[6 + pair] = value_sum[...].astype(BF16)

        @pl.when(step == 7)
        def _():
            for side in range(2):
                first_heads_grad(side)
            scatter_first(0)
            scatter_start(0)

        run_at(step, "k", 12)

    @pl.loop(0, 3)
    def _(part):
        rows = pl.ds(pl.multiple_of(part * TILE, TILE), TILE)
        first, second = packs_of(heads_grad(2, rows), out_grad[rows, :].astype(F32))
        wide[0, 1, rows, 384:768] = first.astype(BF16)
        wide[1, 1, rows, 384:768] = second.astype(BF16)

    scatter_first(1)
    scatter_start(1)
    run("t0")
    for pair in range(3):
        vgrad[8:9, 128 * pair : 128 * pair + 128] = row_sum(heads_back[pair].astype(F32))
        vgrad[8:9, 384 + 128 * pair : 512 + 128 * pair] = row_sum(heads_back[6 + pair].astype(F32))
    send(M_VG, vgrad, vrecv.at[0], core_dev)

    def input_part(quarter):
        return sum(
            dims(beside(heads_back, (pair, 3 + pair, 6 + pair), quarter), w_in[pair], 1, 1)
            for pair in range(3)
        )

    given(1)

    @pl.loop(0, 2)
    def _(slot):
        give(3, slot, input_part(2 * slot + 1 - b))

    run("t1")
    arrived(M_VG, vrecv.at[0])
    mine = lax.broadcasted_iota(jnp.int32, (16, 768), 0) < 6
    vsend[0] = vgrad[...] + jnp.where(mine, vrecv[0], 0.0)
    send(M_VG + 1, vsend.at[0], vrecv.at[1], x_dev)

    @pl.loop(0, 2)
    def _(slot):
        own = input_part(2 * slot + b)
        back_rows[slot] = back_rows[slot] + own + take(3, slot)

    cots[0] = back_rows[1 - a].astype(BF16)
    send(M_GRAD, cots.at[0], cots.at[1], x_dev)
    store_far(21, back_rows.at[a], grad_ref.at[a]).start()
    arrived(M_VG + 1, vrecv.at[1])
    vsend[1] = vsend[0] + vrecv[1]
    send(M_VG + 2, vsend.at[1], vrecv.at[2], y_dev)
    run("t2")
    arrived(M_VG + 2, vrecv.at[2])
    vsend[2] = vsend[1] + vrecv[2]
    for j in range(1, 4):
        send(M_VG + 2 + j, vsend.at[2], vrecv.at[2 + j], z_dev(j))
    for pack in (3, 4, 2, 0):
        scatter_end(pack)
    run("t3")
    every = vsend[2]
    for j in range(1, 4):
        arrived(M_VG + 2 + j, vrecv.at[2 + j])
        every = every + vrecv[2 + j]
    vout_ref[...] = pltpu.roll(every, (8 - dp) % 8 * 96, 1)
    heads_row = every[8:9, :]
    for kind in range(2):
        row = heads_row[:, 384 * kind : 384 * kind + 384]
        low_row = low_lanes((1, 128))
        third = jnp.where(a == 0, row[:, 256:384], half_turn(row[:, 256:384]))
        both = jnp.concatenate(
            (jnp.where(a == 0, row[:, :128], row[:, 128:256]), jnp.where(low_row, third, 0.0)), 1
        )
        vout_ref[8 + kind : 9 + kind, 0:256] = pltpu.roll(both, (256 - dp * 24) % 256, 1)
    vout_ref[6:7, :] = jnp.where(a == 0, vout_ref[6:7, :], vout_ref[7:8, :])
    arrived(M_GRAD, cots.at[1])
    hat_first[0] = cots[1].astype(F32)
    store_far(22, hat_first.at[0], grad_ref.at[1 - a]).start()
    arrived(M_OUT, out_ref.at[1 - a])
    scatter_end(1)

    store_far(20, swap_out.at[a], out_ref.at[a]).wait()
    store_far(21, back_rows.at[a], grad_ref.at[a]).wait()
    store_far(22, hat_first.at[0], grad_ref.at[1 - a]).wait()

    for pack in range(5):
        scatter_left(pack)
    given(2)
    given(3)
    left(M_MASK, mask_ref)
    left(M_IN, in_ref.at[0])
    left(M_COT, cot_ref.at[0])
    left(M_OUT, swap_out.at[0])
    left(M_GRAD, cots.at[0])
    for j in range(3):
        left(M_VZ + j, vec_ref)
    left(M_VY, vec_y.at[0])
    left(M_VX, vec_all.at[0])
    for slot in range(2):
        left(M_TOK + slot, tokens.at[0])
        for kind in range(3):
            left(M_ROWS + 2 * kind + slot, first_low.at[0])
    for index in range(6):
        left(M_VG + index, vsend.at[0])


def finish_kernel(
    gout_half,
    gout_wide,
    vout_ref,
    from_output,
    from_grad,
    query_ref,
    key_ref,
    value_ref,
    project_ref,
    up_ref,
    down_ref,
    query_bias_ref,
    value_bias_ref,
    second_gain_ref,
    second_shift_ref,
    down_bias_ref,
    first_gain_ref,
    first_shift_ref,
    out_bias_ref,
    up_bias_ref,
    to_output,
    to_grad,
):
    row_refs = (
        second_gain_ref,
        second_shift_ref,
        down_bias_ref,
        first_gain_ref,
        first_shift_ref,
        out_bias_ref,
        up_bias_ref,
    )
    to_output[...] = from_output[...]
    to_grad[...] = from_grad[...]
    first, last = gout_half[0], gout_half[1]
    query_ref[...] = jnp.concatenate((first[:, 0:128], last[:, 0:64]), 1)
    key_ref[...] = jnp.concatenate((first[:, 128:256], last[:, 64:128]), 1)
    value_ref[...] = jnp.concatenate((first[:, 256:384], last[:, 128:192]), 1)
    gap = jnp.zeros((32, 256), F32)
    project = jnp.concatenate((last[:, 256:384], last[:, 128:256]), 1)
    project = jnp.concatenate((project, gap), 0).T
    project_ref[0:128, :] = project[0:128, :96]
    project_ref[128:192, :] = project[192:256, :96]
    up_ref[...] = gout_wide[0]
    down_ref[...] = jnp.concatenate((gout_half[2], gout_half[3]), 1)
    query_bias_ref[...] = vout_ref[8, 0:24]
    value_bias_ref[...] = vout_ref[9, 0:24]
    for row, ref in enumerate(row_refs):
        ref[...] = vout_ref[row, 0:96]


def layer_call(weights, rows, biases, random_blocks, tokens, cotangent):
    vmem = pltpu.VMEM
    anywhere = pl.BlockSpec(memory_space=pltpu.VMEM)
    far = pl.BlockSpec(memory_space=pl.ANY)
    shape = jax.ShapeDtypeStruct
    def both(*dims_, kind=BF16):
        return (vmem((4,) + dims_ + (384,), kind), vmem((1,) + dims_ + (768,), kind))

    like = lambda array: vmem(array.shape, array.dtype)
    scratch = [
        *(like(array) for array in weights),
        tuple(like(array) for array in rows),
        *(like(array) for array in (*biases, random_blocks, tokens, cotangent)),
        vmem((2, 96, 384), BF16),
        vmem((16, 768), BF16),
        vmem((48, 128), BF16),
        vmem((2, 2, 768, 384), BF16),
        vmem((2, 2, 768, 768), BF16),
        vmem((3, 16, 768), BF16),
        vmem((2, 16, 768), BF16),
        vmem((2, 16, 768), BF16),
        vmem((2, 48, 128), BF16),
        vmem((4, TILE, 768), BF16),
        vmem((768, 4 * TILE), BF16),
        vmem((2, TILE, 768), BF16),
        vmem((3, 768, 384), BF16),
        vmem((768, 384), BF16),
        vmem((3, 2, 4, 4, 1024), F32),
        vmem((3, 2, 16, 1024), F32),
        vmem((9, 1024, 128), BF16),
        vmem((3, 128, 1024), BF16),
        vmem((3, 1024, 128), BF16),
        vmem((3, 2, 1, 1024), F32),
        vmem((8, 1024), F32),
        vmem((4, TILE, 768), BF16),
        vmem((768, 4 * TILE), BF16),
        vmem((4, TILE, 768), BF16),
        vmem((4, TILE, 768), BF16),
        vmem((2, TILE, 768), F32),
        vmem((2, TILE, 1), F32),
        vmem((2, TILE, 768), F32),
        vmem((2, 4, TILE, 768), BF16),
        vmem((2, 4, TILE, 768), BF16),
        vmem((TILE, 768), F32),
        vmem((2, 2, TILE, 768), BF16),
        vmem((2, 2, TILE, 768), BF16),
        vmem((3, 1024, 128), BF16),
        vmem((1024, 128), F32),
        vmem((1024, 128), F32),
        vmem((9, 1024, 128), BF16),
        vmem((768, 384), BF16),
        both(4, 48),
        both(4, 48),
        both(4, 96),
        both(4, 96),
        both(3, 96 - LEAN),
        both(3, 4, LEAN),
        both(96, kind=F32),
        vmem((2, TILE, 768), BF16),
        vmem((16, 768), F32),
        vmem((3, 16, 768), F32),
        vmem((6, 16, 768), F32),
        pltpu.SemaphoreType.DMA((MESSAGES,)),
        pltpu.SemaphoreType.DMA((MESSAGES,)),
        pltpu.SemaphoreType.DMA((24,)),
    ]
    return pl.pallas_call(
        layer_kernel,
        out_shape=(
            shape(tokens.shape, BF16),
            shape(tokens.shape, F32),
            shape((4, 96, 384), F32),
            shape((1, 96, 768), F32),
            shape((16, 768), F32),
        ),
        in_specs=[far] * 6 + [(far,) * 7] + [far] * 5,
        out_specs=(far,) * 2 + (anywhere,) * 3,
        scratch_shapes=scratch,
        compiler_params=pltpu.CompilerParams(
            collective_id=0, has_side_effects=True, vmem_limit_bytes=63 << 20
        ),
    )(*weights, rows, *biases, random_blocks, tokens, cotangent)


def local_fast(
    inputs,
    random_blocks,
    query_weight,
    query_bias,
    key_weight,
    value_weight,
    value_bias,
    out_weight,
    out_bias,
    first_gain,
    first_shift,
    up_weight,
    up_bias,
    down_weight,
    down_bias,
    second_gain,
    second_shift,
    cotangent,
):
    output, input_grad, half_grads, wide_grads, sums = layer_call(
        (query_weight, key_weight, value_weight, down_weight.T, up_weight, out_weight),
        (out_bias, first_gain, first_shift, down_bias, second_gain, second_shift, up_bias),
        (query_bias, value_bias),
        random_blocks.transpose(0, 2, 1),
        inputs,
        cotangent,
    )
    like = lambda array: jax.ShapeDtypeStruct(array.shape, F32)
    whole = pl.BlockSpec(memory_space=pltpu.VMEM)
    outs = (query_weight, key_weight, value_weight, out_weight, up_weight, up_weight)
    outs += (query_bias, value_bias)
    outs += (second_gain, second_shift, down_bias, first_gain, first_shift, out_bias, up_bias)
    done = pl.pallas_call(
        finish_kernel,
        out_shape=tuple(like(array) for array in outs)
        + tuple(jax.ShapeDtypeStruct(array.shape, array.dtype) for array in (output, input_grad)),
        in_specs=[whole] * 5,
        out_specs=(whole,) * (len(outs) + 2),
    )(half_grads, wide_grads, sums, output, input_grad)
    query_grad, key_grad, value_grad, out_grad, up_grad, down_grad = done[:6]
    query_bias_grad, value_bias_grad = done[6:8]
    second_gain_grad, second_shift_grad, down_bias_grad = done[8:11]
    first_gain_grad, first_shift_grad, out_bias_grad, up_bias_grad = done[11:15]
    output, input_grad = done[15:]
    return (
        output,
        input_grad,
        query_grad,
        query_bias_grad,
        key_grad,
        value_grad,
        value_bias_grad,
        out_grad,
        out_bias_grad,
        first_gain_grad,
        first_shift_grad,
        up_grad,
        up_bias_grad,
        down_grad.T,
        down_bias_grad,
        second_gain_grad,
        second_shift_grad,
    )


def solution(mesh):
    sizes = mesh.shape
    fast = sizes["dp"] == 8 and sizes["tensor"] == 4
    return jax.shard_map(
        local_fast if fast else local,
        mesh=mesh,
        in_specs=(
            P("dp", "tensor", None),
            P("tensor", None, None),
            P("dp", "tensor"),
            P(("tensor", "dp")),
            P("dp", "tensor"),
            P("dp", "tensor"),
            P(("tensor", "dp")),
            P("tensor", "dp"),
            P("dp"),
            P("dp"),
            P("dp"),
            P("dp", "tensor"),
            P(("tensor", "dp")),
            P("tensor", "dp"),
            P("dp"),
            P("dp"),
            P("dp"),
            P("dp", "tensor", None),
        ),
        out_specs=(
            P("dp", "tensor", None),
            P("dp", "tensor", None),
            P("dp", "tensor"),
            P(("tensor", "dp")),
            P("dp", "tensor"),
            P("dp", "tensor"),
            P(("tensor", "dp")),
            P("tensor", "dp"),
            P("dp"),
            P("dp"),
            P("dp"),
            P("dp", "tensor"),
            P(("tensor", "dp")),
            P("tensor", "dp"),
            P("dp"),
            P("dp"),
            P("dp"),
        ),
        check_vma=False,
    )
```
